32 devices in a mesh: ctx: 16 (over z, y, core), fsdp: 2 (over x).
Axes of the slice: x: 2, y: 2, z: 4, core: 2. Of those that a mesh axis runs over, the one named last changes fastest.
Arguments:
- hidden_in: bfloat16 [2, 2048, 768], P('fsdp', 'ctx'), may hold values from -6 to 6
- segment_ids: int32 [2, 2048], P('fsdp', 'ctx'), may hold values from 0 to 3, never falling along the last dimension, each value on 1 to 1024 neighbouring positions
- token_types: int32 [2, 2048], P('fsdp', 'ctx'), may hold values from 0 to 1
- out_grad: bfloat16 [2, 2048, 768], P('fsdp', 'ctx'), may hold values from -6 to 6
- query_proj: bfloat16 [768, 768], P('fsdp'), may hold values from -0.21875 to 0.21875
- key_proj: bfloat16 [768, 768], P('fsdp'), may hold values from -0.21875 to 0.21875
- value_proj: bfloat16 [768, 768], P('fsdp'), may hold values from -0.21875 to 0.21875
- value_bias: bfloat16 [768], P('fsdp'), may hold values from -0.1796875 to 0.1796875
- content_bias: bfloat16 [768], P('fsdp'), may hold values from -3 to 3
- position_bias: bfloat16 [768], P('fsdp'), may hold values from -3 to 3
- type_bias: bfloat16 [768], P('fsdp'), may hold values from -3 to 3
- type_embed: bfloat16 [2, 768], P(None, 'fsdp'), may hold values from -6 to 6
- position_proj: bfloat16 [768, 768], P('fsdp'), may hold values from -0.21875 to 0.21875
- output_proj: bfloat16 [768, 768], P('fsdp'), may hold values from -2 to 2
- output_bias: bfloat16 [768], P('fsdp'), may hold values from -1.796875 to 1.796875
- attn_gain: bfloat16 [768], P('fsdp'), may hold values from 0.5 to 1.5
- attn_shift: bfloat16 [768], P('fsdp'), may hold values from -1.796875 to 1.796875
- inner_proj: bfloat16 [768, 3072], P('fsdp'), may hold values from -0.21875 to 0.21875
- inner_bias: bfloat16 [3072], P('fsdp'), may hold values from -1.796875 to 1.796875
- outer_proj: bfloat16 [3072, 768], P('fsdp'), may hold values from -0.109375 to 0.109375
- outer_bias: bfloat16 [768], P('fsdp'), may hold values from -1.796875 to 1.796875
- ffn_gain: bfloat16 [768], P('fsdp'), may hold values from 0.5 to 1.5
- ffn_shift: bfloat16 [768], P('fsdp'), may hold values from -1.796875 to 1.796875
Outputs:
- result: bfloat16 [2, 2048, 768], P('fsdp', 'ctx')
- input_grad: float32 [2, 2048, 768], P('fsdp', 'ctx')
- grad_query_proj: float32 [768, 768], P('fsdp')
- grad_key_proj: float32 [768, 768], P('fsdp')
- grad_value_proj: float32 [768, 768], P('fsdp')
- grad_value_bias: float32 [768], P('fsdp')
- grad_content_bias: float32 [768], P('fsdp')
- grad_position_bias: float32 [768], P('fsdp')
- grad_type_bias: float32 [768], P('fsdp')
- grad_type_embed: float32 [2, 768], P(None, 'fsdp')
- grad_position_proj: float32 [768, 768], P('fsdp')
- grad_output_proj: float32 [768, 768], P('fsdp')
- grad_output_bias: float32 [768], P('fsdp')
- grad_attn_gain: float32 [768], P('fsdp')
- grad_attn_shift: float32 [768], P('fsdp')
- grad_inner_proj: float32 [768, 3072], P('fsdp')
- grad_inner_bias: float32 [3072], P('fsdp')
- grad_outer_proj: float32 [3072, 768], P('fsdp')
- grad_outer_bias: float32 [768], P('fsdp')
- grad_ffn_gain: float32 [768], P('fsdp')
- grad_ffn_shift: float32 [768], P('fsdp')
The draws below stay inside these ranges and needn't reach their ends.
Inputs may be any that keep to these rules, and one draw needn't show every extreme that they name: `segment_ids`: along a sequence the document number never falls; a document holds at most 1024 tokens and one holds exactly 1024.
All inputs are finite; a program needn't handle non-finite values.
Results may differ from the reference program's by a relative error of at most 0.03.
Values may be sent and summed in bfloat16 or wider, within the bound.
No kernel may reach another device: no remote copies, remote signals or barrier semaphores. Data moves between devices by JAX's collectives and lax.ppermute only.
A program may use at most 256 MiB of HBM per device.

```python
import math
import jax
import jax.numpy as jnp
import numpy as np
from jax import lax

D = 768
H = 12
DH = 64
FF = 3072
LEN = 2048
SEQS = 2
SEGS = 4
SEGMAX = 1024


def touch_ends(drawn, stream_key, low, top_value):
    dims = drawn.shape
    place = [jax.random.randint(jax.random.fold_in(stream_key, axis), (), 0, dims[axis]) for axis in range(len(dims))]
    drawn = drawn.at[tuple(place)].set(low)
    longest = dims.index(max(dims))
    place[longest] = (place[longest] + 1) % dims[longest]
    return drawn.at[tuple(place)].set(top_value)


def steps_of(rng, dims, cuts, smallest, largest):
    def one(axis_at, shards_of):
        heights = jax.random.uniform(jax.random.fold_in(jax.random.fold_in(rng, 6), axis_at), (shards_of,), jnp.float32, smallest / len(cuts), largest / len(cuts))
        return jnp.repeat(jnp.exp(heights), dims[axis_at] // shards_of).reshape((-1,) + (1,) * (len(dims) - axis_at - 1))

    factor_of = one(*cuts[0])
    for cut in cuts[1:]:
        factor_of = factor_of * one(*cut)
    return factor_of


def split_up(amount, total, reach, slope):
    weights = [(1 << 20) // math.isqrt(rank ** slope) + 1 for rank in range(2, amount + 1)]
    surplus, given = total - reach - (amount - 1), [1] * (amount - 1)
    while surplus > 0:
        movable = [i for i in range(amount - 1) if given[i] < reach]
        mass, remaining = sum([weights[i] for i in movable]), surplus
        for i in movable:
            addition = min(reach - given[i], max(1, remaining * weights[i] // mass), surplus)
            given[i] = given[i] + addition
            surplus = surplus - addition
    return np.array([reach] + given)


def uneven_parts(own_key, count, total, limit, lean):
    if count == 2:
        one = jax.random.randint(own_key, (), max(1, total - limit), min(limit, total - 1) + 1)
        return jnp.stack([one, total - one])
    sizes = jnp.asarray(split_up(count, total, limit, lean), jnp.int32)
    twos = (count - 1) // 2
    donor, taker = sizes[1:1 + 2 * twos:2], sizes[2:2 + 2 * twos:2]
    slack = jnp.minimum(donor - 1, limit - taker)
    moved = jax.random.randint(jax.random.fold_in(own_key, 1), (twos,), 0, 1 << 20) % (slack + 1)
    sizes = sizes.at[1:1 + 2 * twos:2].set(donor - moved).at[2:2 + 2 * twos:2].set(taker + moved)
    return sizes[jax.random.permutation(jax.random.fold_in(own_key, 2), count)]


def gaussian(key, shape, scale, most, split=(), kind=jnp.bfloat16):
    factor_of = steps_of(key, shape, split, -0.22, 0.18) if split else 1.0
    values = jax.random.normal(key, shape, jnp.float32) * scale * factor_of
    return jnp.minimum(jnp.maximum(values, -most), most).astype(kind)


def setup_inputs(seed: int = 0) -> dict:
    arg_keys = jax.random.split(jax.random.key(seed), 24)
    return {
        "hidden_in": gaussian(arg_keys[0], (SEQS, LEN, D), 1.0, 6.0, ((0, 2), (1, 16))),
        "segment_ids": jax.vmap(lambda own: jnp.searchsorted(jnp.cumsum(uneven_parts(own, SEGS, LEN, SEGMAX, 0)), jnp.arange(LEN), side="right"))(jax.random.split(arg_keys[1], SEQS)).reshape((SEQS, LEN)).astype(jnp.int32),
        "token_types": touch_ends(jax.random.randint(arg_keys[2], (SEQS, LEN), 0, 2), jax.random.fold_in(arg_keys[2], 1), 0, 1).astype(jnp.int32),
        "out_grad": gaussian(arg_keys[3], (SEQS, LEN, D), 1.0, 6.0, ((0, 2), (1, 16))),
        "query_proj": gaussian(arg_keys[4], (D, D), D ** -0.5, 0.21875, ((0, 2),)),
        "key_proj": gaussian(arg_keys[5], (D, D), D ** -0.5, 0.21875, ((0, 2),)),
        "value_proj": gaussian(arg_keys[6], (D, D), D ** -0.5, 0.21875, ((0, 2),)),
        "value_bias": gaussian(arg_keys[7], (D,), 0.03, 0.1796875, ((0, 2),)),
        "content_bias": gaussian(arg_keys[8], (D,), 0.5, 3.0, ((0, 2),)),
        "position_bias": gaussian(arg_keys[9], (D,), 0.5, 3.0, ((0, 2),)),
        "type_bias": gaussian(arg_keys[10], (D,), 0.5, 3.0, ((0, 2),)),
        "type_embed": gaussian(arg_keys[11], (2, D), 1.0, 6.0, ((1, 2),)),
        "position_proj": gaussian(arg_keys[12], (D, D), D ** -0.5, 0.21875, ((0, 2),)),
        "output_proj": gaussian(arg_keys[13], (D, D), 8 ** -0.5, 2.0, ((0, 2),)),
        "output_bias": gaussian(arg_keys[14], (D,), 0.3, 1.796875, ((0, 2),)),
        "attn_gain": jnp.clip(1.0 + 0.1 * jax.random.normal(arg_keys[15], (D,), jnp.float32), 0.5, 1.5).astype(jnp.bfloat16),
        "attn_shift": gaussian(arg_keys[16], (D,), 0.3, 1.796875, ((0, 2),)),
        "inner_proj": gaussian(arg_keys[17], (D, FF), D ** -0.5, 0.21875, ((0, 2),)),
        "inner_bias": gaussian(arg_keys[18], (FF,), 0.3, 1.796875, ((0, 2),)),
        "outer_proj": gaussian(arg_keys[19], (FF, D), FF ** -0.5, 0.109375, ((0, 2),)),
        "outer_bias": gaussian(arg_keys[20], (D,), 0.3, 1.796875, ((0, 2),)),
        "ffn_gain": jnp.clip(1.0 + 0.1 * jax.random.normal(arg_keys[21], (D,), jnp.float32), 0.5, 1.5).astype(jnp.bfloat16),
        "ffn_shift": gaussian(arg_keys[22], (D,), 0.3, 1.796875, ((0, 2),)),
    }


EPS = 1e-06
NEG_BIG = -1e+30
HIGH = lax.Precision.HIGHEST

@jax.custom_vjp
def low(v):
    return lax.optimization_barrier(v.astype(jnp.bfloat16)).astype(jnp.float32)

@jax.custom_vjp
def low_back(v):
    return v

def low_keep(v):
    return (low(v), None)

def low_pass(kept, grad):
    return (grad,)

def back_keep(v):
    return (v, None)

def back_low(kept, grad):
    return (low(grad),)
low.defvjp(low_keep, low_pass)
low_back.defvjp(back_keep, back_low)

def matmul(left, right):
    return jnp.dot(left, right, precision=HIGH, preferred_element_type=jnp.float32)

def layer_norm(residual, gain_vec, bias_vec):
    center = residual - lax.optimization_barrier(jnp.mean(residual, axis=-1, keepdims=True))
    spread = lax.optimization_barrier(jnp.mean(center * center, axis=-1, keepdims=True))
    return center * lax.rsqrt(spread + EPS) * gain_vec + bias_vec

def sinusoid(offsets, span_width):
    half_width = span_width // 2
    frequency = jnp.power(10000.0, -jnp.arange(half_width, dtype=jnp.float32) / half_width)
    angles = offsets[:, None] * frequency[None, :]
    return jnp.concatenate([jnp.sin(angles), jnp.cos(angles)], axis=1)

def rel_shift(full_scores, query_rows, key_cols):
    heads_count = full_scores.shape[0]
    span_width = full_scores.shape[2]
    flat_scores = full_scores.reshape(heads_count, query_rows * span_width)
    flat_scores = flat_scores[:, query_rows - 1:query_rows - 1 + query_rows * (span_width - 1)]
    return flat_scores.reshape(heads_count, query_rows, span_width - 1)[:, :, :key_cols]

def attention(query_content, query_position, query_type, keys_full, values_full, table_full, type_embed, segment_row, type_row):
    length = keys_full.shape[0]
    block_rows = min(512, length)
    block_count = length // block_rows
    type_terms = lax.optimization_barrier(jnp.sum(query_type.reshape(length, 1, H, DH) * type_embed.reshape(1, 2, H, DH), axis=3))
    keys_heads = keys_full.reshape(length, H, DH)
    values_heads = values_full.reshape(length, H, DH)

    def one_block(pieces):
        content_block, position_block, type_block, segment_block, kind_block, first_row = pieces
        content = jnp.einsum('qhd,khd->hqk', content_block.reshape(block_rows, H, DH), keys_heads, precision=HIGH)
        table_start = length - block_rows - first_row
        table_block = lax.dynamic_slice_in_dim(table_full, table_start, block_rows + length, 0)
        wide_scores = jnp.einsum('qhd,whd->hqw', position_block.reshape(block_rows, H, DH), table_block.reshape(block_rows + length, H, DH), precision=HIGH)
        position = rel_shift(wide_scores, block_rows, length)
        type_match = kind_block[:, None] == type_row[None, :]
        type_scores = jnp.where(type_match[None], jnp.transpose(type_block[:, 1, :])[:, :, None], jnp.transpose(type_block[:, 0, :])[:, :, None])
        scores = low_back(content + position + type_scores)
        same_segment = segment_block[:, None] == segment_row[None, :]
        scores = jnp.where(same_segment[None], scores, NEG_BIG)
        weights = low(jax.nn.softmax(scores, axis=-1))
        mixed_out = jnp.einsum('hqk,khd->qhd', weights, values_heads, precision=HIGH)
        return mixed_out.reshape(block_rows, H * DH)
    firsts = (jnp.arange(block_count) * block_rows).astype(jnp.int32)
    outputs = lax.map(jax.checkpoint(one_block), (query_content.reshape(block_count, block_rows, H * DH), query_position.reshape(block_count, block_rows, H * DH), type_terms.reshape(block_count, block_rows, 2, H), segment_row.reshape(block_count, block_rows), type_row.reshape(block_count, block_rows), firsts))
    return outputs.reshape(length, H * DH)

def block_layer(hidden, params, segment_row, type_row):
    query_proj, key_proj, value_proj, value_bias, content_bias, position_bias, type_bias, type_embed, position_proj, output_proj, output_bias, attn_gain, attn_shift, inner_proj, inner_bias, outer_proj, outer_bias, ffn_gain, ffn_shift = params
    length = hidden.shape[0]
    score_scale = DH ** (-0.5)
    query_lin = low_back(matmul(hidden, query_proj))
    keys_full = low(low_back(matmul(hidden, key_proj)))
    values_full = low(low_back(matmul(hidden, value_proj) + value_bias))
    query_content = low(low_back((query_lin + content_bias) * score_scale))
    query_position = low(low_back((query_lin + position_bias) * score_scale))
    query_type = (query_lin + type_bias) * score_scale
    offsets = (length - 1 - jnp.arange(2 * length)).astype(jnp.float32)
    table_full = low(matmul(low(sinusoid(offsets, hidden.shape[1])), position_proj))
    mixed_out = low(low_back(attention(query_content, query_position, query_type, keys_full, values_full, table_full, type_embed, segment_row, type_row)))
    attn_out = low_back(matmul(mixed_out, output_proj) + output_bias)
    normed = layer_norm(hidden + attn_out, attn_gain, attn_shift)
    inner_pre = low_back(matmul(low(normed), inner_proj) + inner_bias)
    activated = low(jax.nn.gelu(inner_pre, approximate=True))
    outer_out = low_back(matmul(activated, outer_proj) + outer_bias)
    return layer_norm(normed + outer_out, ffn_gain, ffn_shift)

def reference(hidden_in, segment_ids, token_types, out_grad, query_proj, key_proj, value_proj, value_bias, content_bias, position_bias, type_bias, type_embed, position_proj, output_proj, output_bias, attn_gain, attn_shift, inner_proj, inner_bias, outer_proj, outer_bias, ffn_gain, ffn_shift):
    params = tuple((weight.astype(jnp.float32) for weight in (query_proj, key_proj, value_proj, value_bias, content_bias, position_bias, type_bias, type_embed, position_proj, output_proj, output_bias, attn_gain, attn_shift, inner_proj, inner_bias, outer_proj, outer_bias, ffn_gain, ffn_shift)))
    zero_grads = jax.tree.map(jnp.zeros_like, params)

    def one_sequence(totals, pieces):
        hidden, segment_row, type_row, cotangent = pieces

        def forward(hidden_f, *param_list):
            return block_layer(hidden_f, param_list, segment_row, type_row)
        outcome, pullback = jax.vjp(forward, hidden.astype(jnp.float32), *params)
        grad_list = pullback(cotangent.astype(jnp.float32))
        totals = jax.tree.map(jnp.add, totals, tuple(grad_list[1:]))
        return (totals, (outcome.astype(jnp.bfloat16), grad_list[0]))
    totals, (outputs, input_grads) = lax.scan(one_sequence, zero_grads, (hidden_in, segment_ids, token_types, out_grad))
    return (outputs, input_grads, totals[0], totals[1], totals[2], totals[3], totals[4], totals[5], totals[6], totals[7], totals[8], totals[9], totals[10], totals[11], totals[12], totals[13], totals[14], totals[15], totals[16], totals[17], totals[18])
```

```python
from functools import partial
import jax
import jax.numpy as jnp
from jax import lax
from jax.experimental import pallas as pl
from jax.experimental.pallas import tpu as pltpu
from jax.sharding import PartitionSpec as P

H = 12
DH = 64
EPS = 1e-06
BIG = 1e30
BF = jnp.bfloat16
F32 = jnp.float32


def nt(a, b):
    return lax.dot_general(a, b, (((1,), (1,)), ((), ())), preferred_element_type=F32)


def nn(a, b):
    return lax.dot_general(a, b, (((1,), (0,)), ((), ())), preferred_element_type=F32)


def tn(a, b):
    return lax.dot_general(a, b, (((0,), (0,)), ((), ())), preferred_element_type=F32)


def att_fwd_kernel(q_ref, rows_ref, pen_ref, kind_ref, k_ref, v_ref, t_ref, ka_ref, o_ref, p_ref):
    T=q_ref.shape[0]; W=k_ref.shape[0]; NB=W//T
    c=DH**-0.5
    q=q_ref[...]
    qc=((q+rows_ref[0:1,:])*c).astype(BF)
    qp=((q+rows_ref[1:2,:])*c).astype(BF)
    qt=(q+rows_ref[2:3,:])*c
    t0=qt*rows_ref[3:4,:]; t1=qt*rows_ref[4:5,:]
    lane=lax.broadcasted_iota(jnp.int32,(T,128),1)
    row=lax.broadcasted_iota(jnp.int32,(T,128),0)
    same=kind_ref[...]>0.5
    pen=pen_ref[...]
    sel=lane<=row
    zero=jnp.zeros((T,128),F32)
    kcat=jnp.concatenate([k_ref[...],ka_ref[...]],axis=1)
    outs=[]
    for h in range(2):
        msk=(lane<64) if h==0 else (lane>=64)
        a0=jnp.sum(jnp.where(msk,t0,0.0),axis=1,keepdims=True)
        a1=jnp.sum(jnp.where(msk,t1,0.0),axis=1,keepdims=True)
        a0=jnp.broadcast_to(a0,(T,128)); a1=jnp.broadcast_to(a1,(T,128))
        A=jnp.where(same,a1,a0); B=jnp.where(same,a0,a1)
        A1=A.astype(BF).astype(F32); A2=A-A1
        B1=B.astype(BF).astype(F32); B2=B-B1
        aug=jnp.where(lane==0,A1,jnp.where(lane==1,A2,jnp.where(lane==4,B1,jnp.where(lane==5,B2,pen)))).astype(BF)
        qa=jnp.concatenate([jnp.where(msk,qc,jnp.zeros_like(qc)),aug],axis=1)
        s=nt(qa,kcat)
        w=nt(jnp.where(msk,qp,jnp.zeros_like(qp)),t_ref[...])
        R=[pltpu.roll(w[:,128*t:128*t+128],1,1,stride=1,stride_axis=0) for t in range(NB+1)]
        ss=[s[:,128*b:128*b+128]+jnp.where(sel,R[b],R[b+1]) for b in range(NB)]
        m=ss[0]
        for b in range(1,NB): m=jnp.maximum(m,ss[b])
        m=jnp.max(m,axis=1,keepdims=True)
        es=[jnp.exp(x-m) for x in ss]
        l=es[0]
        for b in range(1,NB): l=l+es[b]
        l=jnp.sum(l,axis=1,keepdims=True)
        inv=1.0/l
        p=jnp.concatenate([(x*inv).astype(BF) for x in es],axis=1)
        p_ref[h]=p
        outs.append(nn(p,v_ref[...]))
    o_ref[...]=jnp.where(lane<64,outs[0],outs[1])

def att_bwd_kernel(q_ref, rows_ref, kind_ref, dm_ref, o_ref, p_ref, k_ref, v_ref, t_ref, ka_ref,
                   dq_ref, vec_ref, dkv_ref, dt_ref):
    T=q_ref.shape[0]; W=k_ref.shape[0]; NB=W//T
    c=DH**-0.5
    q=q_ref[...]
    qc=((q+rows_ref[0:1,:])*c).astype(BF)
    qp=((q+rows_ref[1:2,:])*c).astype(BF)
    qt=(q+rows_ref[2:3,:])*c
    e0=rows_ref[3:4,:]; e1=rows_ref[4:5,:]
    lane=lax.broadcasted_iota(jnp.int32,(T,128),1)
    row=lax.broadcasted_iota(jnp.int32,(T,128),0)
    same=kind_ref[...]>0.5
    sel=lane>=row
    flip=jnp.where(lane+row==T-1,1.0,0.0).astype(BF)
    qpr=nn(flip,qp).astype(BF)
    zf=jnp.zeros((T,128),F32)
    dm=dm_ref[...]
    dmo=dm.astype(F32)*o_ref[...]
    kcat=jnp.concatenate([k_ref[...],ka_ref[...]],axis=1)
    zb=jnp.zeros_like(dm)
    dss=[];wds=[];dms=[];qcs=[];qps=[];dqc=[];dqp=[];gz=[];go=[]
    for h in range(2):
        msk=(lane<64) if h==0 else (lane>=64)
        delta=jnp.sum(jnp.where(msk,dmo,0.0),axis=1,keepdims=True)
        dmh=jnp.where(msk,dm,zb)
        dp=nt(dmh,v_ref[...])
        ds=(p_ref[h].astype(F32)*(dp-delta)).astype(BF)
        dsf=nn(flip,ds)
        dc=nn(ds,kcat)
        R=[pltpu.roll(dsf[:,128*b:128*b+128],0,1,stride=1,stride_axis=0) for b in range(NB)]
        wd=[]
        for t in range(NB+1):
            lo=R[t] if t<NB else zf
            hi=R[t-1] if t>0 else zf
            wd.append(jnp.where(sel,lo,hi).astype(BF))
        wd=jnp.concatenate(wd,axis=1)
        dqp.append(nn(wd,t_ref[...]))
        dqc.append(dc[:,:128])
        s1=jnp.broadcast_to(dc[:,128:129],(T,128)); s0=jnp.broadcast_to(dc[:,132:133],(T,128))
        go.append(jnp.where(same,s1,s0)); gz.append(jnp.where(same,s0,s1))
        dss.append(ds);wds.append(wd);dms.append(dmh)
        qcs.append(jnp.where(msk,qc,zb));qps.append(jnp.where(msk,qpr,zb))
    cat=lambda xs: jnp.concatenate(xs,axis=0)
    dkv_ref[0]=tn(cat(qcs),cat(dss)).astype(BF)
    dkv_ref[1]=tn(cat(dms),jnp.concatenate([p_ref[0],p_ref[1]],axis=0)).astype(BF)
    dt_ref[...]=tn(cat(qps),cat(wds)).astype(BF)
    lo=lane<64
    dc=jnp.where(lo,dqc[0],dqc[1]).astype(BF).astype(F32)
    dpp=nn(flip,jnp.where(lo,dqp[0],dqp[1]).astype(BF))
    z=jnp.where(lo,gz[0],gz[1]); o=jnp.where(lo,go[0],go[1])
    dty=z*e0+o*e1
    dq_ref[...]=(c*(dc+dpp+dty)).astype(BF)
    vec_ref[0:1,:]=c*jnp.sum(dc,axis=0,keepdims=True)
    vec_ref[1:2,:]=c*jnp.sum(dpp,axis=0,keepdims=True)
    vec_ref[2:3,:]=c*jnp.sum(dty,axis=0,keepdims=True)
    vec_ref[3:4,:]=jnp.sum(z*qt,axis=0,keepdims=True)
    vec_ref[4:5,:]=jnp.sum(o*qt,axis=0,keepdims=True)
    vec_ref[5:8,:]=jnp.zeros((3,128),F32)

def col(n): return pl.BlockSpec((n,128),lambda i:(0,i))
def const(shape): return pl.BlockSpec(shape,lambda i:(0,)*len(shape))
def att_fwd(q,rows,pen,kind,k,v,t,ka):
    T,D=q.shape; W=k.shape[0]; P=D//128; H=D//DH
    return pl.pallas_call(att_fwd_kernel,grid=(P,),
      in_specs=[col(T),col(8),const((T,128)),const((T,128)),col(W),col(W),col(W+T),const((W,128))],
      out_specs=[col(T),pl.BlockSpec((2,T,W),lambda i:(i,0,0))],
      out_shape=[jax.ShapeDtypeStruct((T,D),F32),jax.ShapeDtypeStruct((H,T,W),BF)],
      compiler_params=pltpu.CompilerParams(vmem_limit_bytes=60*2**20),
      cost_estimate=pl.CostEstimate(flops=2*H*T*W*(256+128+128),bytes_accessed=2*(3*W*D+H*T*W),transcendentals=H*T*W),
      name="att_fwd")(q,rows,pen,kind,k,v,t,ka)
def att_bwd(q,rows,kind,dm,o,p,k,v,t,ka):
    T,D=q.shape; W=k.shape[0]; P=D//128; H=D//DH
    row=lambda n: pl.BlockSpec((128,n),lambda i:(i,0))
    return pl.pallas_call(att_bwd_kernel,grid=(P,),
      in_specs=[col(T),col(8),const((T,128)),col(T),col(T),pl.BlockSpec((2,T,W),lambda i:(i,0,0)),col(W),col(W),col(W+T),const((W,128))],
      out_specs=[col(T),col(8),pl.BlockSpec((2,128,W),lambda i:(0,i,0)),row(W+T)],
      out_shape=[jax.ShapeDtypeStruct((T,D),BF),jax.ShapeDtypeStruct((8,D),F32),jax.ShapeDtypeStruct((2,D,W),BF),jax.ShapeDtypeStruct((D,W+T),BF)],
      compiler_params=pltpu.CompilerParams(vmem_limit_bytes=60*2**20),
      cost_estimate=pl.CostEstimate(flops=2*H*T*W*(128*5),bytes_accessed=2*(6*W*D+H*T*W),transcendentals=0),
      name="att_bwd")(q,rows,kind,dm,o,p,k,v,t,ka)


def layer_norm(residual, gain_vec, bias_vec):
    center = residual - jnp.mean(residual, axis=-1, keepdims=True)
    spread = jnp.mean(center * center, axis=-1, keepdims=True)
    return center * lax.rsqrt(spread + EPS) * gain_vec + bias_vec


def sinus_rows(first, count, width):
    half = width // 2
    freq = jnp.power(10000.0, -jnp.arange(half, dtype=F32) / half)
    coarse = (first - 64 * jnp.arange(count // 64)).astype(F32)[:, None] * freq
    fine = jnp.arange(64).astype(F32)[:, None] * freq
    sa, ca = jnp.sin(coarse)[:, None], jnp.cos(coarse)[:, None]
    sb, cb = jnp.sin(fine)[None], jnp.cos(fine)[None]
    both = jnp.concatenate([sa * cb - ca * sb, ca * cb + sa * sb], axis=2)
    return both.astype(BF).reshape(count, width)


class Shards:
    def __init__(self):
        self.parts = lax.axis_size("fsdp")
        self.pair = self.parts == 2
        self.f = lax.axis_index("fsdp")
        self.core = lax.axis_index("ctx") % 2
        self.swap = [(0, 1), (1, 0)]
        self.cores = [(i, i ^ 1) for i in range(lax.axis_size("ctx"))]

    def full(self, w):
        if not self.pair:
            return lax.all_gather(w, "fsdp", axis=0, tiled=True)
        half = w.shape[0] // 2
        mine = lax.dynamic_slice_in_dim(w, self.core * half, half, 0)
        got = lax.ppermute(mine, "fsdp", self.swap)
        other = lax.ppermute(got, "ctx", self.cores)
        low = jnp.where(self.core == 0, got, other)
        high = jnp.where(self.core == 0, other, got)
        theirs = jnp.concatenate([low, high], axis=0)
        return jnp.concatenate(
            [jnp.where(self.f == 0, w, theirs), jnp.where(self.f == 0, theirs, w)], axis=0
        )

    def full_small(self, w):
        if not self.pair:
            return lax.all_gather(w, "fsdp", axis=0, tiled=False)
        theirs = lax.ppermute(w, "fsdp", self.swap)
        return jnp.stack([jnp.where(self.f == 0, w, theirs), jnp.where(self.f == 0, theirs, w)])

    def own(self, a, axis, other=False):
        n = a.shape[axis] // self.parts
        at = (1 - self.f) if other else self.f
        return lax.dynamic_slice_in_dim(a, at * n, n, axis)

    def trade(self, a):
        return lax.ppermute(a, "fsdp", self.swap)

    def sum_rows(self, g):
        if not self.pair:
            return lax.psum_scatter(g.astype(BF), "fsdp", scatter_dimension=0, tiled=True)
        got = self.trade(self.own(g, 0, True).astype(BF))
        return (self.own(g, 0) + got.astype(F32)).astype(BF)


def per_device(
    hidden_in,
    segment_ids,
    token_types,
    out_grad,
    query_proj,
    key_proj,
    value_proj,
    value_bias,
    content_bias,
    position_bias,
    type_bias,
    type_embed,
    position_proj,
    output_proj,
    output_bias,
    attn_gain,
    attn_shift,
    inner_proj,
    inner_bias,
    outer_proj,
    outer_bias,
    ffn_gain,
    ffn_shift,
):
    sh = Shards()
    hidden = hidden_in[0]
    cotangent = out_grad[0].astype(F32)
    T, D = hidden.shape
    C = lax.axis_size("ctx")
    ctx = lax.axis_index("ctx")
    L = T * C
    R = C // 2
    NB = 2 * R + 1
    W = NB * T
    scale = DH ** (-0.5)

    dn = D // sh.parts
    small = jnp.concatenate(
        [
            jnp.stack(
                [
                    value_bias, content_bias, position_bias, type_bias, type_embed[0],
                    type_embed[1], output_bias, attn_gain, attn_shift, outer_bias,
                    ffn_gain, ffn_shift,
                ]
            ),
            inner_bias.reshape(-1, dn),
        ],
        axis=0,
    )
    nsmall = small.shape[0]
    small_full = sh.full_small(small).astype(F32)
    vecs = jnp.transpose(small_full[:, :12], (1, 0, 2)).reshape(12, D)
    v_bias, _, _, _, _, _, o_bias, a_gain, a_shift, out_bias, f_gain, f_shift = (
        vecs[i] for i in range(12)
    )
    in_bias = small_full[:, 12:].reshape(-1)
    qkv_full = sh.full(jnp.concatenate([query_proj, key_proj, value_proj], axis=1))
    po_full = sh.full(jnp.concatenate([position_proj, output_proj], axis=1))
    inner_full = sh.full(inner_proj)
    outer_full = sh.full(outer_proj)
    q_full, kv_full = qkv_full[:, :D], qkv_full[:, D:]
    p_full, o_full = po_full[:, :D], po_full[:, D:]

    ids = jnp.zeros((16, D), BF)
    ids = ids.at[0, :T].set(segment_ids[0].astype(BF)).at[1, :T].set(token_types[0].astype(BF))
    gathered = lax.all_gather(jnp.concatenate([hidden, ids], axis=0), "ctx", axis=0, tiled=True)
    gathered = gathered.reshape(C, T + 16, D)
    padded = jnp.pad(gathered, ((R, R), (0, 0), (0, 0)))
    window = lax.dynamic_slice_in_dim(padded, ctx, NB, 0)
    x_win = window[:, :T].reshape(W, D)
    valid = jnp.arange(NB) + ctx - R
    valid = (valid >= 0) & (valid < C)
    seg_k = jnp.where(valid[:, None], window[:, T, :T].astype(jnp.int32), 7).reshape(W, 1)
    kind_k = window[:, T + 1, :T].astype(jnp.int32).reshape(W, 1)
    lane = jnp.arange(128)[None, :]
    in_seg = (lane >= 8) & (lane < 16)
    kaug = jnp.where(
        lane < 3,
        kind_k == 1,
        jnp.where((lane >= 4) & (lane < 7), kind_k == 0, in_seg & (lane - 8 == seg_k)),
    ).astype(BF)
    pen = jnp.where(in_seg & (lane - 8 != segment_ids[0][:, None]), -BIG, 0.0).astype(F32)
    kind_q = jnp.broadcast_to(token_types[0][:, None], (T, 128)).astype(F32)

    q_lin = nn(hidden, q_full)
    kv = nn(x_win, kv_full)
    keys = kv[:, :D].astype(BF)
    values = (kv[:, D:] + v_bias).astype(BF)
    sinus = sinus_rows(T + R * T - 1, W + T, D)
    table = nn(sinus, p_full).astype(BF)
    rows = jnp.concatenate([vecs[1:6], jnp.zeros((3, D), F32)], axis=0)

    mixed_f, probs = att_fwd(q_lin, rows, pen, kind_q, keys, values, table, kaug)
    mixed_low = mixed_f.astype(BF)
    attn_out = nn(mixed_low, o_full) + o_bias
    normed, first_pull = jax.vjp(layer_norm, hidden.astype(F32) + attn_out, a_gain, a_shift)
    normed_low = normed.astype(BF)
    inner_pre = nn(normed_low, inner_full) + in_bias
    activated, gelu_pull = jax.vjp(partial(jax.nn.gelu, approximate=True), inner_pre)
    activ_low = activated.astype(BF)
    outer_out = nn(activ_low, outer_full) + out_bias
    outcome, second_pull = jax.vjp(layer_norm, normed + outer_out, f_gain, f_shift)
    d_res2, grad_ffn_gain, grad_ffn_shift = second_pull(cotangent)
    d_outer = d_res2.astype(BF)
    grad_outer_bias = jnp.sum(d_outer.astype(F32), axis=0)
    d_inner = gelu_pull(nt(d_outer, outer_full))[0].astype(BF)
    grad_inner_bias = jnp.sum(d_inner.astype(F32), axis=0)
    d_normed = d_res2 + nt(d_inner, inner_full)
    d_res1, grad_attn_gain, grad_attn_shift = first_pull(d_normed)
    d_attn = d_res1.astype(BF)
    grad_output_bias = jnp.sum(d_attn.astype(F32), axis=0)
    d_mixed = nt(d_attn, o_full).astype(BF)

    dq, att_vec, dkv, d_table = att_bwd(
        q_lin, rows, kind_q, d_mixed, mixed_f, probs, keys, values, table, kaug
    )
    dkv = dkv.reshape(2 * D, W)
    grad_value_bias = jnp.sum(dkv[D:].astype(F32), axis=1)
    d_hid = lax.dot_general(
        dkv, kv_full, (((0,), (1,)), ((), ())), preferred_element_type=F32
    ).astype(BF)
    d_hid = jnp.pad(d_hid, (((C - 1 - R) * T, (C - 1) * T + L - (C - 1 - R) * T - W), (0, 0)))
    d_hid = lax.dynamic_slice_in_dim(d_hid, (C - 1 - ctx) * T, L, 0)
    d_hid_own = lax.psum_scatter(d_hid, "ctx", scatter_dimension=0, tiled=True).astype(F32)
    input_grad = d_res1 + nt(dq, q_full) + d_hid_own

    gkv = lax.dot_general(x_win, dkv, (((0,), (1,)), ((), ())), preferred_element_type=F32)
    gp = lax.dot_general(sinus, d_table, (((0,), (1,)), ((), ())), preferred_element_type=F32)
    gkv = sh.sum_rows(gkv)
    gp = sh.sum_rows(gp)

    pairs = (
        (hidden, dq), (mixed_low, d_attn), (normed_low, d_inner), (activ_low, d_outer)
    )
    if sh.pair:
        lefts = [sh.own(a, 1, True) for a, _ in pairs]
        got = sh.trade(jnp.concatenate(lefts, axis=1))
        sums = []
        at = 0
        for a, b in pairs:
            n = a.shape[1] // 2
            left = jnp.concatenate([sh.own(a, 1), got[:, at : at + n]], axis=0)
            right = jnp.concatenate([b, sh.trade(b)], axis=0)
            sums.append(tn(left, right).astype(BF))
            at += n
    else:
        sums = [sh.sum_rows(tn(a, b)) for a, b in pairs]
    gq, go, gi, gout = sums

    smalls = jnp.stack(
        [
            grad_value_bias, att_vec[0], att_vec[1], att_vec[2], att_vec[3], att_vec[4],
            grad_output_bias, grad_attn_gain, grad_attn_shift, grad_outer_bias,
            grad_ffn_gain, grad_ffn_shift,
        ]
    )
    smalls = jnp.transpose(smalls.reshape(12, sh.parts, dn), (1, 0, 2))
    smalls = jnp.concatenate([smalls, grad_inner_bias.reshape(sh.parts, -1, dn)], axis=1)
    smalls = sh.sum_rows(smalls.reshape(sh.parts * nsmall, dn))

    gkv, gp, gq, go, gi, gout, smalls = (
        a.astype(F32) for a in lax.psum((gkv, gp, gq, go, gi, gout, smalls), "ctx")
    )
    s = [smalls[i] for i in range(12)]
    return (
        outcome.astype(BF)[None],
        input_grad[None],
        gq,
        gkv[:, :D],
        gkv[:, D:],
        s[0],
        s[1],
        s[2],
        s[3],
        smalls[4:6],
        gp,
        go,
        s[6],
        s[7],
        s[8],
        gi,
        smalls[12:].reshape(-1),
        gout,
        s[9],
        s[10],
        s[11],
    )


def solution(mesh):
    in_specs = (
        P("fsdp", "ctx", None),
        P("fsdp", "ctx"),
        P("fsdp", "ctx"),
        P("fsdp", "ctx", None),
        P("fsdp", None),
        P("fsdp", None),
        P("fsdp", None),
        P("fsdp"),
        P("fsdp"),
        P("fsdp"),
        P("fsdp"),
        P(None, "fsdp"),
        P("fsdp", None),
        P("fsdp", None),
        P("fsdp"),
        P("fsdp"),
        P("fsdp"),
        P("fsdp", None),
        P("fsdp"),
        P("fsdp", None),
        P("fsdp"),
        P("fsdp"),
        P("fsdp"),
    )
    out_specs = (
        P("fsdp", "ctx", None),
        P("fsdp", "ctx", None),
        P("fsdp", None),
        P("fsdp", None),
        P("fsdp", None),
        P("fsdp"),
        P("fsdp"),
        P("fsdp"),
        P("fsdp"),
        P(None, "fsdp"),
        P("fsdp", None),
        P("fsdp", None),
        P("fsdp"),
        P("fsdp"),
        P("fsdp"),
        P("fsdp", None),
        P("fsdp"),
        P("fsdp", None),
        P("fsdp"),
        P("fsdp"),
        P("fsdp"),
    )
    return jax.shard_map(
        per_device, mesh=mesh, in_specs=in_specs, out_specs=out_specs, check_vma=False
    )
```

```python
from functools import partial
import jax
import jax.numpy as jnp
from jax import lax
from jax.experimental import pallas as pl
from jax.experimental.pallas import tpu as pltpu
from jax.sharding import PartitionSpec as P

H = 12
DH = 64
EPS = 1e-06
BIG = 1e30
BF = jnp.bfloat16
F32 = jnp.float32


def nt(a, b):
    return lax.dot_general(a, b, (((1,), (1,)), ((), ())), preferred_element_type=F32)


def nn(a, b):
    return lax.dot_general(a, b, (((1,), (0,)), ((), ())), preferred_element_type=F32)


def tn(a, b):
    return lax.dot_general(a, b, (((0,), (0,)), ((), ())), preferred_element_type=F32)


def att_fwd_kernel(q_ref, rows_ref, pen_ref, kind_ref, k_ref, v_ref, t_ref, ka_ref, o_ref, p_ref):
    T=q_ref.shape[0]; W=k_ref.shape[0]; NB=W//T
    c=DH**-0.5
    q=q_ref[...]
    qc=((q+rows_ref[0:1,:])*c).astype(BF)
    qp=((q+rows_ref[1:2,:])*c).astype(BF)
    qt=(q+rows_ref[2:3,:])*c
    t0=qt*rows_ref[3:4,:]; t1=qt*rows_ref[4:5,:]
    lane=lax.broadcasted_iota(jnp.int32,(T,128),1)
    row=lax.broadcasted_iota(jnp.int32,(T,128),0)
    same=kind_ref[...]>0.5
    pen=pen_ref[...]
    sel=lane<=row
    zero=jnp.zeros((T,128),F32)
    kcat=jnp.concatenate([k_ref[...],ka_ref[...]],axis=1)
    outs=[]
    for h in range(2):
        msk=(lane<64) if h==0 else (lane>=64)
        a0=jnp.sum(jnp.where(msk,t0,0.0),axis=1,keepdims=True)
        a1=jnp.sum(jnp.where(msk,t1,0.0),axis=1,keepdims=True)
        a0=jnp.broadcast_to(a0,(T,128)); a1=jnp.broadcast_to(a1,(T,128))
        A=jnp.where(same,a1,a0); B=jnp.where(same,a0,a1)
        A1=A.astype(BF).astype(F32); A2=A-A1
        B1=B.astype(BF).astype(F32); B2=B-B1
        aug=jnp.where(lane==0,A1,jnp.where(lane==1,A2,jnp.where(lane==4,B1,jnp.where(lane==5,B2,pen)))).astype(BF)
        qa=jnp.concatenate([jnp.where(msk,qc,jnp.zeros_like(qc)),aug],axis=1)
        s=nt(qa,kcat)
        w=nt(jnp.where(msk,qp,jnp.zeros_like(qp)),t_ref[...])
        R=[pltpu.roll(w[:,128*t:128*t+128],1,1,stride=1,stride_axis=0) for t in range(NB+1)]
        ss=[s[:,128*b:128*b+128]+jnp.where(sel,R[b],R[b+1]) for b in range(NB)]
        m=ss[0]
        for b in range(1,NB): m=jnp.maximum(m,ss[b])
        m=jnp.max(m,axis=1,keepdims=True)
        es=[jnp.exp(x-m) for x in ss]
        l=es[0]
        for b in range(1,NB): l=l+es[b]
        l=jnp.sum(l,axis=1,keepdims=True)
        inv=1.0/l
        p=jnp.concatenate([(x*inv).astype(BF) for x in es],axis=1)
        p_ref[h]=p
        outs.append(nn(p,v_ref[...]))
    o_ref[...]=jnp.where(lane<64,outs[0],outs[1])

def att_bwd_kernel(q_ref, rows_ref, kind_ref, dm_ref, o_ref, p_ref, k_ref, v_ref, t_ref, ka_ref,
                   dq_ref, vec_ref, dkv_ref, dt_ref):
    T=q_ref.shape[0]; W=k_ref.shape[0]; NB=W//T
    c=DH**-0.5
    q=q_ref[...]
    qc=((q+rows_ref[0:1,:])*c).astype(BF)
    qp=((q+rows_ref[1:2,:])*c).astype(BF)
    qt=(q+rows_ref[2:3,:])*c
    e0=rows_ref[3:4,:]; e1=rows_ref[4:5,:]
    lane=lax.broadcasted_iota(jnp.int32,(T,128),1)
    row=lax.broadcasted_iota(jnp.int32,(T,128),0)
    same=kind_ref[...]>0.5
    sel=lane>=row
    flip=jnp.where(lane+row==T-1,1.0,0.0).astype(BF)
    qpr=nn(flip,qp).astype(BF)
    zf=jnp.zeros((T,128),F32)
    dm=dm_ref[...]
    dmo=dm.astype(F32)*o_ref[...]
    kcat=jnp.concatenate([k_ref[...],ka_ref[...]],axis=1)
    zb=jnp.zeros_like(dm)
    dss=[];wds=[];dms=[];qcs=[];qps=[];dqc=[];dqp=[];gz=[];go=[]
    for h in range(2):
        msk=(lane<64) if h==0 else (lane>=64)
        delta=jnp.sum(jnp.where(msk,dmo,0.0),axis=1,keepdims=True)
        dmh=jnp.where(msk,dm,zb)
        dp=nt(dmh,v_ref[...])
        ds=(p_ref[h].astype(F32)*(dp-delta)).astype(BF)
        dsf=nn(flip,ds)
        dc=nn(ds,kcat)
        R=[pltpu.roll(dsf[:,128*b:128*b+128],0,1,stride=1,stride_axis=0) for b in range(NB)]
        wd=[]
        for t in range(NB+1):
            lo=R[t] if t<NB else zf
            hi=R[t-1] if t>0 else zf
            wd.append(jnp.where(sel,lo,hi).astype(BF))
        wd=jnp.concatenate(wd,axis=1)
        dqp.append(nn(wd,t_ref[...]))
        dqc.append(dc[:,:128])
        s1=jnp.broadcast_to(dc[:,128:129],(T,128)); s0=jnp.broadcast_to(dc[:,132:133],(T,128))
        go.append(jnp.where(same,s1,s0)); gz.append(jnp.where(same,s0,s1))
        dss.append(ds);wds.append(wd);dms.append(dmh)
        qcs.append(jnp.where(msk,qc,zb));qps.append(jnp.where(msk,qpr,zb))
    cat=lambda xs: jnp.concatenate(xs,axis=0)
    dkv_ref[0]=tn(cat(qcs),cat(dss)).astype(BF)
    dkv_ref[1]=tn(cat(dms),jnp.concatenate([p_ref[0],p_ref[1]],axis=0)).astype(BF)
    dt_ref[...]=tn(cat(qps),cat(wds)).astype(BF)
    lo=lane<64
    dc=jnp.where(lo,dqc[0],dqc[1]).astype(BF).astype(F32)
    dpp=nn(flip,jnp.where(lo,dqp[0],dqp[1]).astype(BF))
    z=jnp.where(lo,gz[0],gz[1]); o=jnp.where(lo,go[0],go[1])
    dty=z*e0+o*e1
    dq_ref[...]=(c*(dc+dpp+dty)).astype(BF)
    vec_ref[0:1,:]=c*jnp.sum(dc,axis=0,keepdims=True)
    vec_ref[1:2,:]=c*jnp.sum(dpp,axis=0,keepdims=True)
    vec_ref[2:3,:]=c*jnp.sum(dty,axis=0,keepdims=True)
    vec_ref[3:4,:]=jnp.sum(z*qt,axis=0,keepdims=True)
    vec_ref[4:5,:]=jnp.sum(o*qt,axis=0,keepdims=True)
    vec_ref[5:8,:]=jnp.zeros((3,128),F32)

def att_fwd(q, rows, pen, kind, k, v, t, ka):
    T, D = q.shape
    W = k.shape[0]
    heads = D // DH
    col = lambda n: pl.BlockSpec((n, 128), lambda i: (0, i))
    fixed = lambda n: pl.BlockSpec((n, 128), lambda i: (0, 0))
    return pl.pallas_call(
        att_fwd_kernel,
        grid=(D // 128,),
        in_specs=[col(T), col(8), fixed(T), fixed(T), col(W), col(W), col(W + T), fixed(W)],
        out_specs=[col(T), pl.BlockSpec((2, T, W), lambda i: (i, 0, 0))],
        out_shape=[
            jax.ShapeDtypeStruct((T, D), F32),
            jax.ShapeDtypeStruct((heads, T, W), BF),
        ],
        compiler_params=pltpu.CompilerParams(vmem_limit_bytes=60 * 2**20),
        cost_estimate=pl.CostEstimate(
            flops=2 * heads * T * W * 2048,
            bytes_accessed=2 * (3 * W * D + heads * T * W),
            transcendentals=heads * T * W,
        ),
        name="att_fwd",
    )(q, rows, pen, kind, k, v, t, ka)


def att_bwd(q, rows, kind, dm, o, p, k, v, t, ka):
    T, D = q.shape
    W = k.shape[0]
    heads = D // DH
    col = lambda n: pl.BlockSpec((n, 128), lambda i: (0, i))
    fixed = lambda n: pl.BlockSpec((n, 128), lambda i: (0, 0))
    return pl.pallas_call(
        att_bwd_kernel,
        grid=(D // 128,),
        in_specs=[
            col(T), col(8), fixed(T), col(T), col(T), pl.BlockSpec((2, T, W), lambda i: (i, 0, 0)),
            col(W), col(W), col(W + T), fixed(W),
        ],
        out_specs=[
            col(T), col(8), pl.BlockSpec((2, 128, W), lambda i: (0, i, 0)),
            pl.BlockSpec((128, W + T), lambda i: (i, 0)),
        ],
        out_shape=[
            jax.ShapeDtypeStruct((T, D), BF),
            jax.ShapeDtypeStruct((8, D), F32),
            jax.ShapeDtypeStruct((2, D, W), BF),
            jax.ShapeDtypeStruct((D, W + T), BF),
        ],
        compiler_params=pltpu.CompilerParams(vmem_limit_bytes=60 * 2**20),
        cost_estimate=pl.CostEstimate(
            flops=2 * heads * T * W * 2048,
            bytes_accessed=2 * (6 * W * D + heads * T * W),
            transcendentals=0,
        ),
        name="att_bwd",
    )(q, rows, kind, dm, o, p, k, v, t, ka)


def layer_norm(residual, gain_vec, bias_vec):
    center = residual - jnp.mean(residual, axis=-1, keepdims=True)
    spread = jnp.mean(center * center, axis=-1, keepdims=True)
    return center * lax.rsqrt(spread + EPS) * gain_vec + bias_vec


def sinus_rows(first, count, width):
    half = width // 2
    freq = jnp.power(10000.0, -jnp.arange(half, dtype=F32) / half)
    coarse = (first - 64 * jnp.arange(count // 64)).astype(F32)[:, None] * freq
    fine = jnp.arange(64).astype(F32)[:, None] * freq
    sa, ca = jnp.sin(coarse)[:, None], jnp.cos(coarse)[:, None]
    sb, cb = jnp.sin(fine)[None], jnp.cos(fine)[None]
    both = jnp.concatenate([sa * cb - ca * sb, ca * cb + sa * sb], axis=2)
    return both.astype(BF).reshape(count, width)


class Shards:
    def __init__(self):
        self.parts = lax.axis_size("fsdp")
        self.pair = self.parts == 2
        self.f = lax.axis_index("fsdp")
        self.ctx = lax.axis_index("ctx")
        self.count = lax.axis_size("ctx")
        self.bits = self.count.bit_length() - 1
        self.swap = [(0, 1), (1, 0)]

    def bit(self, k):
        return (self.ctx >> k) & 1

    def flip(self, a, k):
        return lax.ppermute(a, "ctx", [(i, i ^ (1 << k)) for i in range(self.count)])

    def trade(self, a):
        return lax.ppermute(a, "fsdp", self.swap)

    def order(self, mine, other, at):
        return jnp.where(at == 0, mine, other), jnp.where(at == 0, other, mine)

    def fetch_half(self, w):
        half = w.shape[0] // 2
        return self.trade(lax.dynamic_slice_in_dim(w, self.bit(0) * half, half, 0))

    def fetch(self, w):
        got = self.fetch_half(w)
        return got, self.flip(got, 0)

    def join(self, w, parts):
        theirs = jnp.concatenate(self.order(*parts, self.bit(0)), axis=0)
        return jnp.concatenate(self.order(w, theirs, self.f), axis=0)

    def full_small(self, w):
        if not self.pair:
            return lax.all_gather(w, "fsdp", axis=0, tiled=False)
        return jnp.stack(self.order(w, self.trade(w), self.f))

    def own(self, a, axis, other=False):
        n = a.shape[axis] // self.parts
        at = (1 - self.f) if other else self.f
        return lax.dynamic_slice_in_dim(a, at * n, n, axis)

    def window(self, block, planes):
        y = self.flip(block, 1)
        self.first_hop = y
        pair = jnp.stack(self.order(block, y, self.bit(1)))
        above, below = [], []
        up = down = pair
        for _ in range(planes):
            up = lax.ppermute(up, "ctx", [(i, i + 4) for i in range(self.count - 4)])
            down = lax.ppermute(down, "ctx", [(i + 4, i) for i in range(self.count - 4)])
            above.insert(0, up)
            below.append(down)
        mine = jnp.stack(above + [pair] + below)
        other = self.flip(mine, 0)
        both = jnp.stack(self.order(mine, other, self.bit(0)), axis=2)
        return both.reshape((-1,) + block.shape)

    def halve(self, a, k, axis):
        keep = lax.dynamic_index_in_dim(a, self.bit(k), axis, keepdims=False)
        send = lax.dynamic_index_in_dim(a, 1 - self.bit(k), axis, keepdims=False)
        return (keep.astype(F32) + self.flip(send, k).astype(F32)).astype(BF)

    def halve_cols(self, low, high):
        keep, send = self.order(low, high, self.bit(0))
        return (keep.astype(F32) + self.flip(send, 0).astype(F32)).astype(BF)

    def double(self, a, k, axis):
        return jnp.stack(self.order(a, self.flip(a, k), self.bit(k)), axis=axis)

    def spread(self, a):
        return a.reshape((2,) * self.bits + a.shape[1:])


def per_device(
    hidden_in,
    segment_ids,
    token_types,
    out_grad,
    query_proj,
    key_proj,
    value_proj,
    value_bias,
    content_bias,
    position_bias,
    type_bias,
    type_embed,
    position_proj,
    output_proj,
    output_bias,
    attn_gain,
    attn_shift,
    inner_proj,
    inner_bias,
    outer_proj,
    outer_bias,
    ffn_gain,
    ffn_shift,
):
    sh = Shards()
    hidden = hidden_in[0]
    cotangent = out_grad[0].astype(F32)
    T, D = hidden.shape
    C = sh.count
    ctx = sh.ctx
    L = T * C
    R = C // 2
    NB = 2 * R + 1
    W = NB * T
    dn = D // sh.parts
    r = dn // C

    lane = jnp.arange(128)[None, :]
    in_seg = (lane >= 8) & (lane < 16)
    seg_own = segment_ids[0][:, None]
    kind_own = token_types[0][:, None]
    kaug_own = jnp.where(
        lane < 4, kind_own == 1, jnp.where(lane < 8, kind_own == 0, in_seg & (lane - 8 == seg_own))
    ).astype(BF)
    pen = jnp.where(in_seg & (lane - 8 != seg_own), -BIG, 0.0).astype(F32)
    kind_q = jnp.broadcast_to(kind_own, (T, 128)).astype(F32)

    around = sh.window(jnp.concatenate([hidden, kaug_own], axis=1), R // 4)
    around = lax.dynamic_slice_in_dim(around, ctx % 4, NB, 0)
    x_win = around[:, :, :D].reshape(W, D)
    at = jnp.arange(NB) + ctx - R
    valid = ((at >= 0) & (at < C))[:, None, None]
    kaug = jnp.where(valid, around[:, :, D:], (lane[None] == 15).astype(BF)).reshape(W, 128)

    vectors = (
        value_bias, content_bias, position_bias, type_bias, type_embed, output_bias,
        attn_gain, attn_shift, outer_bias, ffn_gain, ffn_shift, inner_bias,
    )
    vectors, _ = lax.optimization_barrier((vectors, sh.first_hop))
    small = jnp.concatenate([a.reshape(-1, dn) for a in vectors], axis=0)
    nsmall = small.shape[0]
    small_full = sh.full_small(small).astype(F32)
    vecs = jnp.transpose(small_full[:, :12], (1, 0, 2)).reshape(12, D)
    v_bias, _, _, _, _, _, o_bias, a_gain, a_shift, out_bias, f_gain, f_shift = (
        vecs[i] for i in range(12)
    )
    in_bias = small_full[:, 12:].reshape(-1)
    first = (key_proj, value_proj, query_proj, position_proj, output_proj)
    if sh.pair:
        got = sh.fetch(jnp.concatenate(first, axis=1))
        k_full, v_full, q_full, p_full, o_full = (
            sh.join(w, [part[:, i * D : (i + 1) * D] for part in got])
            for i, w in enumerate(first)
        )
        _, i_sh, u_sh = lax.optimization_barrier((got[0], inner_proj, outer_proj))
        i_got, u_got = sh.fetch_half(i_sh), sh.fetch_half(u_sh)
    else:
        k_full, v_full, q_full, p_full, o_full, inner_full, outer_full = (
            lax.all_gather(w, "fsdp", axis=0, tiled=True)
            for w in first + (inner_proj, outer_proj)
        )

    q_lin = nn(hidden, q_full)
    keys = nn(x_win, k_full).astype(BF)
    values = (nn(x_win, v_full) + v_bias).astype(BF)
    sinus = sinus_rows(T + R * T - 1, W + T, D)
    table = nn(sinus, p_full).astype(BF)
    rows = jnp.concatenate([vecs[1:6], jnp.zeros((3, D), F32)], axis=0)

    mixed_f, probs = att_fwd(q_lin, rows, pen, kind_q, keys, values, table, kaug)
    if sh.pair:
        mixed_f, i_got, u_got = lax.optimization_barrier((mixed_f, i_got, u_got))
        inner_full = sh.join(inner_proj, (i_got, sh.flip(i_got, 0)))
        outer_full = sh.join(outer_proj, (u_got, sh.flip(u_got, 0)))
    mixed_low = mixed_f.astype(BF)
    attn_out = nn(mixed_low, o_full) + o_bias
    normed, first_pull = jax.vjp(layer_norm, hidden.astype(F32) + attn_out, a_gain, a_shift)
    normed_low = normed.astype(BF)
    inner_pre = nn(normed_low, inner_full) + in_bias
    activated, gelu_pull = jax.vjp(partial(jax.nn.gelu, approximate=True), inner_pre)
    activ_low = activated.astype(BF)
    outer_out = nn(activ_low, outer_full) + out_bias
    outcome, second_pull = jax.vjp(layer_norm, normed + outer_out, f_gain, f_shift)
    d_res2, grad_ffn_gain, grad_ffn_shift = second_pull(cotangent)
    d_outer = d_res2.astype(BF)
    grad_outer_bias = jnp.sum(d_outer.astype(F32), axis=0)
    d_inner = gelu_pull(nt(d_outer, outer_full))[0].astype(BF)
    grad_inner_bias = jnp.sum(d_inner.astype(F32), axis=0)
    d_normed = d_res2 + nt(d_inner, inner_full)
    d_res1, grad_attn_gain, grad_attn_shift = first_pull(d_normed)
    d_attn = d_res1.astype(BF)
    grad_output_bias = jnp.sum(d_attn.astype(F32), axis=0)
    d_mixed = nt(d_attn, o_full).astype(BF)

    if sh.pair:
        lefts = sh.trade(
            jnp.concatenate([sh.own(normed_low, 1, True), sh.own(activ_low, 1, True)], axis=1)
        )
        rights = (sh.trade(d_inner), sh.trade(d_outer))
        got = sh.trade(
            jnp.concatenate([sh.own(mixed_low, 1, True), sh.own(hidden, 1, True), d_attn], axis=1)
        )
    dq, att_vec, dkv, d_table = att_bwd(
        q_lin, rows, kind_q, d_mixed, mixed_f, probs, keys, values, table, kaug
    )
    if sh.pair:
        gi = tn(
            jnp.concatenate([sh.own(normed_low, 1), lefts[:, :dn]], axis=0),
            jnp.concatenate([d_inner, rights[0]], axis=0),
        ).astype(BF)
        gu = tn(
            jnp.concatenate([sh.own(activ_low, 1), lefts[:, dn:]], axis=0),
            jnp.concatenate([d_outer, rights[1]], axis=0),
        ).astype(BF)
        dq_got = sh.trade(dq)
        gi, gu, dkv, d_table = lax.optimization_barrier((gi, gu, dkv, d_table))
    else:
        gi, gu = (
            lax.psum_scatter(tn(a, b).astype(BF), "fsdp", scatter_dimension=0, tiled=True)
            for a, b in ((normed_low, d_inner), (activ_low, d_outer))
        )
    gi, gu = lax.psum((gi, gu), "ctx")

    dk, dv = dkv[0], dkv[1]
    gk, gv, gp = (
        lax.dot_general(a, b, (((0,), (1,)), ((), ())), preferred_element_type=F32).astype(BF)
        for a, b in ((x_win, dk), (x_win, dv), (sinus, d_table))
    )
    smalls = jnp.concatenate(
        [
            jnp.stack(
                [
                    jnp.sum(d_mixed.astype(F32), axis=0), att_vec[0], att_vec[1], att_vec[2],
                    att_vec[3], att_vec[4], grad_output_bias, grad_attn_gain, grad_attn_shift,
                    grad_outer_bias, grad_ffn_gain, grad_ffn_shift,
                ]
            ),
            jnp.transpose(grad_inner_bias.reshape(sh.parts, -1, dn), (1, 0, 2)).reshape(-1, D),
        ],
        axis=0,
    ).astype(BF)
    smalls = jnp.pad(smalls, ((0, 256 - nsmall), (0, 0)))
    whole = jnp.concatenate([gk, gv, gp, jnp.transpose(smalls)], axis=1)
    half = whole.shape[1] // 2
    if sh.pair:
        whole = sh.halve_cols(whole[:, :half], whole[:, half:])
        whole = whole.reshape(2, dn, half)
        keep = lax.dynamic_index_in_dim(whole, sh.f, 0, keepdims=False)
        send = lax.dynamic_index_in_dim(whole, 1 - sh.f, 0, keepdims=False)
        whole = (keep.astype(F32) + sh.trade(send).astype(F32)).astype(BF)
        go = tn(
            jnp.concatenate([sh.own(mixed_low, 1), got[:, :dn]], axis=0),
            jnp.concatenate([d_attn, got[:, 2 * dn :]], axis=0),
        ).astype(BF)
        gq = tn(
            jnp.concatenate([sh.own(hidden, 1), got[:, dn : 2 * dn]], axis=0),
            jnp.concatenate([dq, dq_got], axis=0),
        ).astype(BF)
    else:
        whole, go, gq = (
            lax.psum_scatter(a, "fsdp", scatter_dimension=0, tiled=True)
            for a in (whole, tn(mixed_low, d_attn).astype(BF), tn(hidden, dq).astype(BF))
        )
        whole = sh.halve_cols(whole[:, :half], whole[:, half:])

    d_hid = (tn(dk, jnp.transpose(k_full)) + tn(dv, jnp.transpose(v_full))).astype(BF)
    d_hid = jnp.pad(d_hid, (((C - 1 - R) * T, (C - 1) * T + L - (C - 1 - R) * T - W), (0, 0)))
    d_hid = lax.dynamic_slice_in_dim(d_hid, (C - 1 - ctx) * T, L, 0)
    d_hid = sh.spread(d_hid.reshape(C, T, D))
    for k in range(sh.bits):
        d_hid = sh.halve(d_hid, k, d_hid.ndim - 3)
    input_grad = d_res1 + nt(dq, q_full) + d_hid.astype(F32)

    grads = jnp.concatenate([whole, sh.halve_cols(go, gq)], axis=1)
    grads = grads.reshape((2,) * (sh.bits - 1) + (-1, grads.shape[1]))
    for k in range(1, sh.bits):
        grads = sh.halve(grads, k, grads.ndim - 3)
    for k in reversed(range(1, sh.bits)):
        grads = sh.double(grads, k, grads.ndim - 2)
    grads = grads.reshape(dn, -1)
    low, high = sh.order(grads, sh.flip(grads, 0), sh.bit(0))
    whole = jnp.concatenate([low[:, :half], high[:, :half]], axis=1).astype(F32)
    gk, gv, gp = (whole[:, i * D : (i + 1) * D] for i in range(3))
    go, gq = low[:, half:].astype(F32), high[:, half:].astype(F32)
    smalls = jnp.transpose(whole[:, 3 * D : 3 * D + 128])[:nsmall]
    s = [smalls[i] for i in range(12)]
    return (
        outcome.astype(BF)[None],
        input_grad[None],
        gq,
        gk,
        gv,
        s[0],
        s[1],
        s[2],
        s[3],
        smalls[4:6],
        gp,
        go,
        s[6],
        s[7],
        s[8],
        gi.astype(F32),
        smalls[12:].reshape(-1),
        gu.astype(F32),
        s[9],
        s[10],
        s[11],
    )


def solution(mesh):
    in_specs = (
        P("fsdp", "ctx", None),
        P("fsdp", "ctx"),
        P("fsdp", "ctx"),
        P("fsdp", "ctx", None),
        P("fsdp", None),
        P("fsdp", None),
        P("fsdp", None),
        P("fsdp"),
        P("fsdp"),
        P("fsdp"),
        P("fsdp"),
        P(None, "fsdp"),
        P("fsdp", None),
        P("fsdp", None),
        P("fsdp"),
        P("fsdp"),
        P("fsdp"),
        P("fsdp", None),
        P("fsdp"),
        P("fsdp", None),
        P("fsdp"),
        P("fsdp"),
        P("fsdp"),
    )
    out_specs = (
        P("fsdp", "ctx", None),
        P("fsdp", "ctx", None),
        P("fsdp", None),
        P("fsdp", None),
        P("fsdp", None),
        P("fsdp"),
        P("fsdp"),
        P("fsdp"),
        P("fsdp"),
        P(None, "fsdp"),
        P("fsdp", None),
        P("fsdp", None),
        P("fsdp"),
        P("fsdp"),
        P("fsdp"),
        P("fsdp", None),
        P("fsdp"),
        P("fsdp", None),
        P("fsdp"),
        P("fsdp"),
        P("fsdp"),
    )
    return jax.shard_map(
        per_device, mesh=mesh, in_specs=in_specs, out_specs=out_specs, check_vma=False
    )
```

```python
from functools import partial
import jax
import jax.numpy as jnp
from jax import lax
from jax.experimental import pallas as pl
from jax.experimental.pallas import tpu as pltpu
from jax.sharding import PartitionSpec as P

H = 12
DH = 64
EPS = 1e-06
BIG = 1e30
BF = jnp.bfloat16
F32 = jnp.float32


def nt(a, b):
    return lax.dot_general(a, b, (((1,), (1,)), ((), ())), preferred_element_type=F32)


def nn(a, b):
    return lax.dot_general(a, b, (((1,), (0,)), ((), ())), preferred_element_type=F32)


def tn(a, b):
    return lax.dot_general(a, b, (((0,), (0,)), ((), ())), preferred_element_type=F32)


def att_fwd_kernel(q_ref, rows_ref, pen_ref, kind_ref, k_ref, v_ref, t_ref, ka_ref, o_ref, p_ref):
    T=q_ref.shape[0]; W=k_ref.shape[0]; NB=W//T
    c=DH**-0.5
    q=q_ref[...]
    qc=((q+rows_ref[1:2, :])*c).astype(BF)
    qp=((q+rows_ref[2:3, :])*c).astype(BF)
    qt=(q+rows_ref[3:4, :])*c
    t0=qt*rows_ref[4:5, :]; t1=qt*rows_ref[5:6, :]
    lane=lax.broadcasted_iota(jnp.int32,(T,128),1)
    row=lax.broadcasted_iota(jnp.int32,(T,128),0)
    same=kind_ref[...]>0.5
    pen=pen_ref[...]
    sel=lane<=row
    zero=jnp.zeros((T,128),F32)
    kcat=jnp.concatenate([k_ref[...],ka_ref[...]],axis=1)
    outs=[]
    for h in range(2):
        msk=(lane<64) if h==0 else (lane>=64)
        a0=jnp.sum(jnp.where(msk,t0,0.0),axis=1,keepdims=True)
        a1=jnp.sum(jnp.where(msk,t1,0.0),axis=1,keepdims=True)
        a0=jnp.broadcast_to(a0,(T,128)); a1=jnp.broadcast_to(a1,(T,128))
        A=jnp.where(same,a1,a0); B=jnp.where(same,a0,a1)
        A1=A.astype(BF).astype(F32); A2=A-A1
        B1=B.astype(BF).astype(F32); B2=B-B1
        aug=jnp.where(lane==0,A1,jnp.where(lane==1,A2,jnp.where(lane==4,B1,jnp.where(lane==5,B2,pen)))).astype(BF)
        qa=jnp.concatenate([jnp.where(msk,qc,jnp.zeros_like(qc)),aug],axis=1)
        s=nt(qa,kcat)
        w=nt(jnp.where(msk,qp,jnp.zeros_like(qp)),t_ref[...])
        R=[pltpu.roll(w[:,128*t:128*t+128],1,1,stride=1,stride_axis=0) for t in range(NB+1)]
        ss=[s[:,128*b:128*b+128]+jnp.where(sel,R[b],R[b+1]) for b in range(NB)]
        m=ss[0]
        for b in range(1,NB): m=jnp.maximum(m,ss[b])
        m=jnp.max(m,axis=1,keepdims=True)
        es=[jnp.exp(x-m) for x in ss]
        l=es[0]
        for b in range(1,NB): l=l+es[b]
        l=jnp.sum(l,axis=1,keepdims=True)
        inv=1.0/l
        p=jnp.concatenate([(x*inv).astype(BF) for x in es],axis=1)
        p_ref[h]=p
        outs.append(nn(p,v_ref[...]))
    o_ref[...]=jnp.where(lane<64,outs[0],outs[1])

def att_bwd_kernel(q_ref, rows_ref, kind_ref, dm_ref, o_ref, p_ref, k_ref, v_ref, t_ref, ka_ref,
                   dq_ref, vec_ref, dkv_ref, dt_ref):
    T=q_ref.shape[0]; W=k_ref.shape[0]; NB=W//T
    c=DH**-0.5
    q=q_ref[...]
    qc=((q+rows_ref[1:2, :])*c).astype(BF)
    qp=((q+rows_ref[2:3, :])*c).astype(BF)
    qt=(q+rows_ref[3:4, :])*c
    e0=rows_ref[4:5, :]; e1=rows_ref[5:6, :]
    lane=lax.broadcasted_iota(jnp.int32,(T,128),1)
    row=lax.broadcasted_iota(jnp.int32,(T,128),0)
    same=kind_ref[...]>0.5
    sel=lane>=row
    flip=jnp.where(lane+row==T-1,1.0,0.0).astype(BF)
    qpr=nn(flip,qp).astype(BF)
    zf=jnp.zeros((T,128),F32)
    dm=dm_ref[...]
    dmo=dm.astype(F32)*o_ref[...]
    kcat=jnp.concatenate([k_ref[...],ka_ref[...]],axis=1)
    zb=jnp.zeros_like(dm)
    dss=[];wds=[];dms=[];qcs=[];qps=[];dqc=[];dqp=[];gz=[];go=[]
    for h in range(2):
        msk=(lane<64) if h==0 else (lane>=64)
        delta=jnp.sum(jnp.where(msk,dmo,0.0),axis=1,keepdims=True)
        dmh=jnp.where(msk,dm,zb)
        dp=nt(dmh,v_ref[...])
        ds=(p_ref[h].astype(F32)*(dp-delta)).astype(BF)
        dsf=nn(flip,ds)
        dc=nn(ds,kcat)
        R=[pltpu.roll(dsf[:,128*b:128*b+128],0,1,stride=1,stride_axis=0) for b in range(NB)]
        wd=[]
        for t in range(NB+1):
            lo=R[t] if t<NB else zf
            hi=R[t-1] if t>0 else zf
            wd.append(jnp.where(sel,lo,hi).astype(BF))
        wd=jnp.concatenate(wd,axis=1)
        dqp.append(nn(wd,t_ref[...]))
        dqc.append(dc[:,:128])
        s1=jnp.broadcast_to(dc[:,128:129],(T,128)); s0=jnp.broadcast_to(dc[:,132:133],(T,128))
        go.append(jnp.where(same,s1,s0)); gz.append(jnp.where(same,s0,s1))
        dss.append(ds);wds.append(wd);dms.append(dmh)
        qcs.append(jnp.where(msk,qc,zb));qps.append(jnp.where(msk,qpr,zb))
    cat=lambda xs: jnp.concatenate(xs,axis=0)
    dkv_ref[0]=tn(cat(qcs),cat(dss)).astype(BF)
    dkv_ref[1]=tn(cat(dms),jnp.concatenate([p_ref[0],p_ref[1]],axis=0)).astype(BF)
    dt_ref[...]=tn(cat(qps),cat(wds)).astype(BF)
    lo=lane<64
    dc=jnp.where(lo,dqc[0],dqc[1]).astype(BF).astype(F32)
    dpp=nn(flip,jnp.where(lo,dqp[0],dqp[1]).astype(BF))
    z=jnp.where(lo,gz[0],gz[1]); o=jnp.where(lo,go[0],go[1])
    dty=z*e0+o*e1
    dq_ref[...]=(c*(dc+dpp+dty)).astype(BF)
    vec_ref[0:1,:]=c*jnp.sum(dc,axis=0,keepdims=True)
    vec_ref[1:2,:]=c*jnp.sum(dpp,axis=0,keepdims=True)
    vec_ref[2:3,:]=c*jnp.sum(dty,axis=0,keepdims=True)
    vec_ref[3:4,:]=jnp.sum(z*qt,axis=0,keepdims=True)
    vec_ref[4:5,:]=jnp.sum(o*qt,axis=0,keepdims=True)
    vec_ref[5:8,:]=jnp.zeros((3,128),F32)

def att_fwd(q, rows, pen, kind, k, v, t, ka):
    T, D = q.shape
    W = k.shape[0]
    heads = D // DH
    col = lambda n: pl.BlockSpec((n, 128), lambda i: (0, i))
    fixed = lambda n: pl.BlockSpec((n, 128), lambda i: (0, 0))
    return pl.pallas_call(
        att_fwd_kernel,
        grid=(D // 128,),
        in_specs=[col(T), col(16), fixed(T), fixed(T), col(W), col(W), col(W + T), fixed(W)],
        out_specs=[col(T), pl.BlockSpec((2, T, W), lambda i: (i, 0, 0))],
        out_shape=[
            jax.ShapeDtypeStruct((T, D), F32),
            jax.ShapeDtypeStruct((heads, T, W), BF),
        ],
        compiler_params=pltpu.CompilerParams(vmem_limit_bytes=60 * 2**20),
        cost_estimate=pl.CostEstimate(
            flops=2 * heads * T * W * 2048,
            bytes_accessed=2 * (3 * W * D + heads * T * W),
            transcendentals=heads * T * W,
        ),
        name="att_fwd",
    )(q, rows, pen, kind, k, v, t, ka)


def att_bwd(q, rows, kind, dm, o, p, k, v, t, ka):
    T, D = q.shape
    W = k.shape[0]
    heads = D // DH
    col = lambda n: pl.BlockSpec((n, 128), lambda i: (0, i))
    fixed = lambda n: pl.BlockSpec((n, 128), lambda i: (0, 0))
    return pl.pallas_call(
        att_bwd_kernel,
        grid=(D // 128,),
        in_specs=[
            col(T), col(16), fixed(T), col(T), col(T), pl.BlockSpec((2, T, W), lambda i: (i, 0, 0)),
            col(W), col(W), col(W + T), fixed(W),
        ],
        out_specs=[
            col(T), col(8), pl.BlockSpec((2, 128, W), lambda i: (0, i, 0)),
            pl.BlockSpec((128, W + T), lambda i: (i, 0)),
        ],
        out_shape=[
            jax.ShapeDtypeStruct((T, D), BF),
            jax.ShapeDtypeStruct((8, D), F32),
            jax.ShapeDtypeStruct((2, D, W), BF),
            jax.ShapeDtypeStruct((D, W + T), BF),
        ],
        compiler_params=pltpu.CompilerParams(vmem_limit_bytes=60 * 2**20),
        cost_estimate=pl.CostEstimate(
            flops=2 * heads * T * W * 2048,
            bytes_accessed=2 * (6 * W * D + heads * T * W),
            transcendentals=0,
        ),
        name="att_bwd",
    )(q, rows, kind, dm, o, p, k, v, t, ka)


def pack_rows(vectors, dn):
    counts = [v.size // dn for v in vectors]

    def kernel(*refs):
        out = refs[-1]
        at = 0
        for ref, n in zip(refs, counts):
            for j in range(n):
                if len(ref.shape) == 1:
                    out[at, :] = ref[pl.ds(j * dn, dn)].astype(F32)
                else:
                    out[at, :] = ref[j, :].astype(F32)
                at += 1

    return pl.pallas_call(
        kernel,
        out_shape=jax.ShapeDtypeStruct((sum(counts), dn), F32),
        name="pack_rows",
    )(*vectors)


def ffn_final(blocks, FF, D):
    count, _, dn = blocks.shape
    steps = FF // D
    per = count // steps
    ri, ru = FF // count, FF // 2 // count

    def kernel(b_ref, i_ref, u_ref):
        gi = jnp.concatenate([b_ref[k, :ri] for k in range(per)], axis=0)
        i_ref[...] = jnp.transpose(gi.astype(F32))
        for k in range(per):
            u_ref[ru * k : ru * (k + 1), :dn] = b_ref[k, ri : ri + ru].astype(F32)
            u_ref[ru * k : ru * (k + 1), dn:] = b_ref[k, ri + ru :].astype(F32)

    return pl.pallas_call(
        kernel,
        grid=(steps,),
        in_specs=[pl.BlockSpec((per, ri + 2 * ru, dn), lambda i: (i, 0, 0))],
        out_specs=[
            pl.BlockSpec((dn, D), lambda i: (0, i)), pl.BlockSpec((FF // 2 // steps, D), lambda i: (i, 0))
        ],
        out_shape=[
            jax.ShapeDtypeStruct((dn, FF), F32), jax.ShapeDtypeStruct((FF // 2, D), F32)
        ],
        cost_estimate=pl.CostEstimate(flops=0, bytes_accessed=6 * D * FF, transcendentals=0),
        name="ffn_final",
    )(blocks)


def split_cols(a, f, odd):
    h = a.shape[1] // 2
    q = h // 2
    own = jnp.where(f == 0, a[:, :h], a[:, h:])
    other = jnp.where(f == 0, a[:, h:], a[:, :h])
    swapped = jnp.concatenate([other[:, q:], other[:, :q]], axis=1)
    return jnp.concatenate([own, jnp.where(odd, swapped, other)], axis=1)


def merge_cols(a, f, odd):
    h = a.shape[1] // 2
    q = h // 2
    own, other = a[:, :h], a[:, h:]
    swapped = jnp.concatenate([other[:, q:], other[:, :q]], axis=1)
    other = jnp.where(odd, swapped, other)
    return jnp.where(
        f == 0, jnp.concatenate([own, other], axis=1), jnp.concatenate([other, own], axis=1)
    )


def swap_quarters(a, y, odd):
    h = a.shape[1] // 2
    q = h // 2
    a = jnp.where(y, jnp.concatenate([a[:, h:], a[:, :h]], axis=1), a)
    pairs = jnp.concatenate([a[:, q:h], a[:, :q], a[:, h + q :], a[:, h : h + q]], axis=1)
    return jnp.where(odd, pairs, a)


def middle_swap(a):
    q = a.shape[1] // 4
    return jnp.concatenate([a[:, :q], a[:, 2 * q : 3 * q], a[:, q : 2 * q], a[:, 3 * q :]], axis=1)


def split_quarters(a, f, y, odd):
    h = a.shape[1] // 2
    own = jnp.where(f == 0, a[:, :h], a[:, h:])
    other = jnp.where(f == 0, a[:, h:], a[:, :h])
    return own, middle_swap(swap_quarters(other, y, odd))


def merge_quarters(a, f, y, odd):
    h = a.shape[1] // 2
    own, other = a[:, :h], swap_quarters(middle_swap(a[:, h:]), y, odd)
    return jnp.where(
        f == 0, jnp.concatenate([own, other], axis=1), jnp.concatenate([other, own], axis=1)
    )


def norm_stats(res):
    center = res - jnp.mean(res, axis=1, keepdims=True)
    rstd = lax.rsqrt(jnp.mean(center * center, axis=1, keepdims=True) + EPS)
    return center * rstd, rstd


def norm_back(g, gain, n, rstd):
    gg = g * gain
    return (gg - jnp.mean(gg, axis=1, keepdims=True) - n * jnp.mean(gg * n, axis=1, keepdims=True)) * rstd


def row_sum(a):
    return jnp.sum(a, axis=0, keepdims=True)


GELU_A = 0.7978845608028654
GELU_B = 0.044715


def ffn_specs(T, D, FF):
    steps = FF // (D // 2)
    half = steps // 2
    c = FF // steps
    q = D // 8

    def chunk_at(j, s):
        p = jnp.maximum(j - half, 0)
        piece = ((s[2] ^ (p & 1)) << 1) | (s[1] ^ (p >> 1))
        return jnp.where(j < half, half * s[0] + j, half * (1 - s[0]) + piece)

    col = lambda j, s: (0, chunk_at(j, s))
    whole = lambda *shape: pl.BlockSpec(shape, lambda j, s: (0,) * len(shape))
    inner = [pl.BlockSpec((4 * q, c), col)] + [pl.BlockSpec((q, c), col)] * 4
    outer = [pl.BlockSpec((c, D), lambda j, s: (jnp.minimum(j, half - 1), 0))] + [whole(c, D)] * 4
    proj = [whole(4 * q, D), whole(2 * q, D), whole(2 * q, D)]
    return steps, half, c, chunk_at, col, whole, inner, outer, proj


def outer_chunk(j, half, refs):
    chunk = refs[0][...]
    for p in range(4):
        chunk = jnp.where(j == half + p, refs[1 + p][...], chunk)
    return chunk


def rows_of(refs):
    return jnp.concatenate([r[...] for r in refs], axis=0)


def inner_bias_chunk(b, half, vec_ref, D):
    row = vec_ref[pl.ds(12 + b % half, 1), :]
    return jnp.where(b < half, row[:, : D // 2], row[:, D // 2 :])


def gelu_tanh(u):
    return jnp.tanh(GELU_A * (u + GELU_B * u * u * u))


def first_norm(x, mixed, vec_ref, w, f, odd):
    attn = nn(split_cols(mixed, f, odd).astype(BF), w) + vec_ref[6:7, :]
    n1, rstd = norm_stats(x.astype(F32) + attn)
    return n1, rstd, n1 * vec_ref[7:8, :] + vec_ref[8:9, :]


def ffn_fwd(place, x, mixed, cot, vecs, o_parts, i_parts, u_parts, FF):
    T, D = x.shape
    steps, half, c, chunk_at, col, whole, inner, outer, proj = ffn_specs(T, D, FF)

    def kernel(s_ref, x_ref, m_ref, g_ref, v_ref, *refs):
        o_refs, i_refs, u_refs = refs[:3], refs[3:8], refs[8:13]
        nl_ref, act_ref, pre_ref, res_ref, dr_ref, do_ref, n1_ref, rs_ref, gv_ref = refs[13:22]
        np_ref, acc_ref, nf_ref = refs[22:]
        j = pl.program_id(0)
        f, odd, y = s_ref[0], s_ref[1] == 1, s_ref[2] == 1

        @pl.when(j == 0)
        def _():
            n1, rstd, normed = first_norm(x_ref[...], m_ref[...], v_ref, rows_of(o_refs), f, odd)
            n1_ref[...] = n1
            rs_ref[...] = jnp.broadcast_to(rstd, (T, 128))
            nf_ref[...] = normed
            nl_ref[...] = normed.astype(BF)
            np_ref[...] = jnp.concatenate(split_quarters(normed, f, y, odd), axis=1).astype(BF)
            acc_ref[...] = jnp.zeros_like(acc_ref)

        bias = inner_bias_chunk(chunk_at(j, s_ref), half, v_ref, D)
        pre = nn(np_ref[...], rows_of(i_refs)) + bias
        pre_ref[...] = pre
        act = (0.5 * pre * (1.0 + gelu_tanh(pre))).astype(BF)
        act_ref[...] = act
        acc_ref[...] += nn(act, outer_chunk(j, half, u_refs))

        @pl.when(j == steps - 1)
        def _():
            n2, rstd = norm_stats(nf_ref[...] + (acc_ref[...] + v_ref[9:10, :]))
            g = g_ref[...].astype(F32)
            res_ref[...] = (n2 * v_ref[10:11, :] + v_ref[11:12, :]).astype(BF)
            d = norm_back(g, v_ref[10:11, :], n2, rstd)
            dr_ref[...] = d
            do = d.astype(BF)
            do_ref[...] = do
            gv_ref[0:1, :] = row_sum(g * n2)
            gv_ref[1:2, :] = row_sum(g)
            gv_ref[2:3, :] = row_sum(do.astype(F32))
            gv_ref[3:8, :] = jnp.zeros((5, D), F32)

    f32 = lambda *shape: jax.ShapeDtypeStruct(shape, F32)
    low = lambda *shape: jax.ShapeDtypeStruct(shape, BF)
    tok = whole(T, D)
    chunk = pl.BlockSpec((T, c), col)
    return pl.pallas_call(
        kernel,
        grid_spec=pltpu.PrefetchScalarGridSpec(
            num_scalar_prefetch=1,
            grid=(steps,),
            in_specs=[tok, tok, tok, whole(16, D)] + proj + inner + outer,
            out_specs=[tok, chunk, chunk, tok, tok, tok, tok, whole(T, 128), whole(8, D)],
            scratch_shapes=[
                pltpu.VMEM((T, D), BF), pltpu.VMEM((T, D), F32), pltpu.VMEM((T, D), F32)
            ],
        ),
        out_shape=[
            low(T, D), low(T, FF), f32(T, FF), low(T, D), f32(T, D), low(T, D), f32(T, D),
            f32(T, 128), f32(8, D),
        ],
        compiler_params=pltpu.CompilerParams(vmem_limit_bytes=40 * 2**20),
        cost_estimate=pl.CostEstimate(
            flops=4 * T * D * FF, bytes_accessed=4 * D * FF, transcendentals=T * FF
        ),
        name="ffn_fwd",
    )(place, x, mixed, cot, vecs, *o_parts, *i_parts, *u_parts)


def ffn_bwd(
    place, count, pre, act, normed, d_outer, d_outer_got, d_res2, n1, rstd1, mixed_got, x_got,
    vecs, o_parts, i_parts, u_parts,
):
    T, FF = pre.shape
    D = d_outer.shape[1]
    dn = D // 2
    steps, half, c, chunk_at, col, whole, inner, outer, proj = ffn_specs(T, D, FF)
    ri, ru = FF // count, FF // 2 // count

    def kernel(s_ref, pre_ref, act_ref, nl_ref, do_ref, dog_ref, dr_ref, n1_ref, rs_ref, mg_ref, xg_ref, v_ref, *refs):
        o_refs, i_refs, u_refs = refs[:3], refs[3:8], refs[8:13]
        pay_ref, d1_ref, da_ref, dm_ref, gv_ref = refs[13:18]
        acc_ref, ib_ref, np_ref, nf_ref, do_both = refs[18:]
        j = pl.program_id(0)
        f, odd, y = s_ref[0], s_ref[1] == 1, s_ref[2] == 1

        @pl.when(j == 0)
        def _():
            acc_ref[...] = jnp.zeros_like(acc_ref)
            theirs = first_norm(xg_ref[...], mg_ref[...], v_ref, rows_of(o_refs), f, odd)[2]
            own, other = split_quarters(theirs, f, y, odd)
            np_ref[...] = jnp.concatenate([own, other], axis=1).astype(BF)
            nl = nl_ref[...]
            nf_ref[:T] = jnp.where(f == 0, nl[:, :dn], nl[:, dn:])
            nf_ref[T:] = own.astype(BF)
            do_both[:T] = do_ref[...]
            do_both[T:] = dog_ref[...]

        b = chunk_at(j, s_ref)
        w = rows_of(i_refs)
        pre_got = nn(np_ref[...], w) + inner_bias_chunk(b, half, v_ref, D)
        u = jnp.concatenate([pre_ref[...], pre_got], axis=0)
        t = gelu_tanh(u)
        slope = 0.5 * (1.0 + t) + 0.5 * u * (1.0 - t * t) * (GELU_A * (1.0 + 3.0 * GELU_B * u * u))
        di = (nt(do_both[...], outer_chunk(j, half, u_refs)) * slope).astype(BF)
        ib_ref[pl.ds(b, 1), :] = row_sum(di[:T].astype(F32))
        acc_ref[...] += nt(di[:T], w)
        gi = tn(di, nf_ref[...]).astype(BF)
        for k in range(c // ri):
            pay_ref[b * (c // ri) + k, :ri] = gi[ri * k : ri * (k + 1)]

        @pl.when(j < half)
        def _():
            act_got = (0.5 * u[T:] * (1.0 + t[T:])).astype(BF)
            gu = tn(jnp.concatenate([act_ref[...], act_got], axis=0), do_both[...]).astype(BF)
            for k in range(c // ru):
                pay_ref[j * (c // ru) + k, ri : ri + ru] = gu[ru * k : ru * (k + 1), :dn]
                pay_ref[j * (c // ru) + k, ri + ru :] = gu[ru * k : ru * (k + 1), dn:]

        @pl.when(j == steps - 1)
        def _():
            d_normed = dr_ref[...] + merge_quarters(acc_ref[...], f, y, odd)
            n1 = n1_ref[...]
            d1 = norm_back(d_normed, v_ref[7:8, :], n1, rs_ref[:, 0:1])
            d1_ref[...] = d1
            da = d1.astype(BF)
            da_ref[...] = da
            dm = merge_cols(nt(da, rows_of(o_refs)), f, odd)
            dm_ref[...] = dm.astype(BF)
            gv_ref[0:1, :] = row_sum(d_normed * n1)
            gv_ref[1:2, :] = row_sum(d_normed)
            gv_ref[2:3, :] = row_sum(da.astype(F32))
            gv_ref[3:4, :] = row_sum(dm.astype(BF).astype(F32))
            gv_ref[4:, :] = jnp.concatenate([ib_ref[:half], ib_ref[half:]], axis=1)

    f32 = lambda *shape: jax.ShapeDtypeStruct(shape, F32)
    low = lambda *shape: jax.ShapeDtypeStruct(shape, BF)
    tok = whole(T, D)
    chunk = pl.BlockSpec((T, c), col)
    return pl.pallas_call(
        kernel,
        grid_spec=pltpu.PrefetchScalarGridSpec(
            num_scalar_prefetch=1,
            grid=(steps,),
            in_specs=[chunk, chunk] + [tok] * 5 + [whole(T, 128), tok, tok, whole(16, D)]
            + proj + inner + outer,
            out_specs=[whole(count, ri + 2 * ru, dn), tok, tok, tok, whole(8, D)],
            scratch_shapes=[
                pltpu.VMEM((T, D), F32), pltpu.VMEM((steps, c), F32), pltpu.VMEM((T, D), BF),
                pltpu.VMEM((2 * T, dn), BF), pltpu.VMEM((2 * T, D), BF),
            ],
        ),
        out_shape=[low(count, ri + 2 * ru, dn), f32(T, D), low(T, D), low(T, D), f32(8, D)],
        compiler_params=pltpu.CompilerParams(vmem_limit_bytes=44 * 2**20),
        cost_estimate=pl.CostEstimate(
            flops=14 * T * D * FF, bytes_accessed=6 * D * FF, transcendentals=2 * T * FF
        ),
        name="ffn_bwd",
    )(
        place, pre, act, normed, d_outer, d_outer_got, d_res2, n1, rstd1, mixed_got, x_got, vecs,
        *o_parts, *i_parts, *u_parts,
    )


def layer_norm(residual, gain_vec, bias_vec):
    center = residual - jnp.mean(residual, axis=-1, keepdims=True)
    spread = jnp.mean(center * center, axis=-1, keepdims=True)
    return center * lax.rsqrt(spread + EPS) * gain_vec + bias_vec


def sinus_rows(first, count, width):
    half = width // 2
    freq = jnp.power(10000.0, -jnp.arange(half, dtype=F32) / half)
    coarse = (first - 64 * jnp.arange(count // 64)).astype(F32)[:, None] * freq
    fine = jnp.arange(64).astype(F32)[:, None] * freq
    sa, ca = jnp.sin(coarse)[:, None], jnp.cos(coarse)[:, None]
    sb, cb = jnp.sin(fine)[None], jnp.cos(fine)[None]
    both = jnp.concatenate([sa * cb - ca * sb, ca * cb + sa * sb], axis=2)
    return both.astype(BF).reshape(count, width)


class Shards:
    def __init__(self):
        self.parts = lax.axis_size("fsdp")
        self.pair = self.parts == 2
        self.f = lax.axis_index("fsdp")
        self.ctx = lax.axis_index("ctx")
        self.count = lax.axis_size("ctx")
        self.bits = self.count.bit_length() - 1
        self.swap = [(0, 1), (1, 0)]

    def bit(self, k):
        return (self.ctx >> k) & 1

    def flip(self, a, k):
        return lax.ppermute(a, "ctx", [(i, i ^ (1 << k)) for i in range(self.count)])

    def trade(self, a):
        return lax.ppermute(a, "fsdp", self.swap)

    def order(self, mine, other, at):
        return jnp.where(at == 0, mine, other), jnp.where(at == 0, other, mine)

    def fetch_half(self, w):
        half = w.shape[0] // 2
        return self.trade(lax.dynamic_slice_in_dim(w, self.bit(0) * half, half, 0))

    def fetch_quarter(self, w):
        n = w.shape[0] // 4
        return self.trade(lax.dynamic_slice_in_dim(w, (self.ctx % 4) * n, n, 0))

    def pieces(self, got, y):
        return got, y, self.flip(got, 0), self.flip(y, 0)

    def full_small(self, w):
        if not self.pair:
            return lax.all_gather(w, "fsdp", axis=0, tiled=False)
        return jnp.stack(self.order(w, self.trade(w), self.f))

    def own(self, a, axis, other=False):
        n = a.shape[axis] // self.parts
        at = (1 - self.f) if other else self.f
        return lax.dynamic_slice_in_dim(a, at * n, n, axis)

    def window(self, block, planes):
        y = self.flip(block, 1)
        self.first_hop = y
        pair = jnp.stack(self.order(block, y, self.bit(1)))
        up = down = pair
        groups = [(pair[None], self.flip(pair[None], 0))]
        for _ in range(planes):
            up = lax.ppermute(up, "ctx", [(i, i + 4) for i in range(self.count - 4)])
            down = lax.ppermute(down, "ctx", [(i + 4, i) for i in range(self.count - 4)])
            both = jnp.stack([up, down])
            groups.append((both, self.flip(both, 0)))
        self.last_hop = both
        groups = [jnp.stack(self.order(a, b, self.bit(0)), axis=2) for a, b in groups]
        planes = [g[0] for g in groups[:0:-1]] + [groups[0][0]] + [g[1] for g in groups[1:]]
        return jnp.concatenate(planes, axis=0).reshape((-1,) + block.shape)

    def halve(self, a, k, axis):
        keep = lax.dynamic_index_in_dim(a, self.bit(k), axis, keepdims=False)
        send = lax.dynamic_index_in_dim(a, 1 - self.bit(k), axis, keepdims=False)
        return (keep.astype(F32) + self.flip(send, k).astype(F32)).astype(BF)

    def halve_cols(self, low, high):
        keep, send = self.order(low, high, self.bit(0))
        return (keep.astype(F32) + self.flip(send.astype(BF), 0).astype(F32)).astype(BF)

    def double(self, a, k, axis):
        return jnp.stack(self.order(a, self.flip(a, k), self.bit(k)), axis=axis)

    def spread(self, a):
        return a.reshape((2,) * self.bits + a.shape[1:])


def per_device(
    hidden_in,
    segment_ids,
    token_types,
    out_grad,
    query_proj,
    key_proj,
    value_proj,
    value_bias,
    content_bias,
    position_bias,
    type_bias,
    type_embed,
    position_proj,
    output_proj,
    output_bias,
    attn_gain,
    attn_shift,
    inner_proj,
    inner_bias,
    outer_proj,
    outer_bias,
    ffn_gain,
    ffn_shift,
):
    sh = Shards()
    hidden = hidden_in[0]
    cotangent = out_grad[0].astype(F32)
    T, D = hidden.shape
    C = sh.count
    ctx = sh.ctx
    L = T * C
    R = C // 2
    NB = 2 * R + 1
    W = NB * T
    dn = D // sh.parts
    r = dn // C

    lane = jnp.arange(128)[None, :]
    in_seg = (lane >= 8) & (lane < 16)
    seg_own = segment_ids[0][:, None]
    kind_own = token_types[0][:, None]
    kaug_own = jnp.where(
        lane < 4, kind_own == 1, jnp.where(lane < 8, kind_own == 0, in_seg & (lane - 8 == seg_own))
    ).astype(BF)
    pen = jnp.where(in_seg & (lane - 8 != seg_own), -BIG, 0.0).astype(F32)
    kind_q = jnp.broadcast_to(kind_own, (T, 128)).astype(F32)

    around = sh.window(jnp.concatenate([hidden, kaug_own], axis=1), R // 4)
    around = lax.dynamic_slice_in_dim(around, ctx % 4, NB, 0)
    x_win = around[:, :, :D].reshape(W, D)
    at = jnp.arange(NB) + ctx - R
    valid = ((at >= 0) & (at < C))[:, None, None]
    kaug = jnp.where(valid, around[:, :, D:], (lane[None] == 15).astype(BF)).reshape(W, 128)

    vectors = (
        value_bias, content_bias, position_bias, type_bias, type_embed, output_bias,
        attn_gain, attn_shift, outer_bias, ffn_gain, ffn_shift, inner_bias,
    )
    small = pack_rows(vectors, dn)
    small_full = sh.full_small(small)
    if sh.pair:
        odd = sh.bit(0) == 1
        got_a = sh.trade(jnp.where(odd, value_proj, position_proj))
        got_b = sh.trade(jnp.where(odd, key_proj, query_proj))
        got_o = sh.fetch_half(output_proj)
        got_a, got_b, got_o, i_sh, u_sh, small_full, _ = lax.optimization_barrier(
            (got_a, got_b, got_o, inner_proj, outer_proj, small_full, sh.last_hop)
        )
        other_p, other_v = sh.order(got_a, sh.flip(got_a, 0), sh.bit(0))
        other_q, other_k = sh.order(got_b, sh.flip(got_b, 0), sh.bit(0))
        p_full, k_full, v_full, q_full = (
            jnp.concatenate(sh.order(w, g, sh.f), axis=0)
            for w, g in (
                (position_proj, other_p), (key_proj, other_k), (value_proj, other_v), (query_proj, other_q)
            )
        )
        flip_o = sh.flip(got_o, 0)
        i_got, u_got = sh.fetch_quarter(i_sh), sh.fetch_quarter(u_sh)
    else:
        p_full, k_full, v_full, q_full, o_full, inner_full, outer_full = (
            lax.all_gather(w, "fsdp", axis=0, tiled=True)
            for w in (
                position_proj, key_proj, value_proj, query_proj, output_proj, inner_proj, outer_proj
            )
        )

    vecs = jnp.concatenate([small_full[i] for i in range(sh.parts)], axis=1)

    q_lin = nn(hidden, q_full)
    keys = nn(x_win, k_full).astype(BF)
    values = (nn(x_win, v_full) + vecs[0]).astype(BF)
    sinus = sinus_rows(T + R * T - 1, W + T, D)
    table = nn(sinus, p_full).astype(BF)

    if sh.pair:
        i_got, table = lax.optimization_barrier((i_got, table))
        i_y = sh.flip(i_got, 1)
        u_got, values, i_y = lax.optimization_barrier((u_got, values, i_y))
        u_y = sh.flip(u_got, 1)
    mixed_f, probs = att_fwd(q_lin, vecs, pen, kind_q, keys, values, table, kaug)
    mixed_low = mixed_f.astype(BF)
    if sh.pair:
        place = jnp.stack([sh.f, sh.bit(0), sh.bit(1)])
        mixed_f, hid, fetched = lax.optimization_barrier((mixed_f, hidden, (i_got, i_y, u_got, u_y)))
        hidden_got = sh.trade(hid)
        mixed_low = mixed_f.astype(BF)
        parts = (
            (output_proj, got_o, flip_o),
            (inner_proj,) + sh.pieces(*fetched[:2]),
            (outer_proj,) + sh.pieces(*fetched[2:]),
        )
        FF = inner_proj.shape[1]
        mixed_got = sh.trade(mixed_low)
        normed_low, activ_low, pre, outcome, d_res2, d_outer, n1, rstd1, vec_a = ffn_fwd(
            place, hidden, mixed_f, out_grad[0], vecs, *parts, FF
        )
        ffn, d_res1, d_attn, d_mixed, vec_b = ffn_bwd(
            place, C, pre, activ_low, normed_low, d_outer, sh.trade(d_outer), d_res2, n1, rstd1,
            mixed_got, hidden_got, vecs, *parts,
        )
    else:
        attn_out = nn(mixed_low, o_full) + vecs[6]
        normed, first_pull = jax.vjp(layer_norm, hidden.astype(F32) + attn_out, vecs[7], vecs[8])
        normed_low = normed.astype(BF)
        inner_pre = nn(normed_low, inner_full) + vecs[12:].reshape(-1, sh.parts, dn).transpose(1, 0, 2).reshape(-1)
        activated, gelu_pull = jax.vjp(partial(jax.nn.gelu, approximate=True), inner_pre)
        activ_low = activated.astype(BF)
        outer_out = nn(activ_low, outer_full) + vecs[9]
        outcome, second_pull = jax.vjp(layer_norm, normed + outer_out, vecs[10], vecs[11])
        d_res2, grad_ffn_gain, grad_ffn_shift = second_pull(cotangent)
        d_outer = d_res2.astype(BF)
        grad_outer_bias = jnp.sum(d_outer.astype(F32), axis=0)
        d_inner = gelu_pull(nt(d_outer, outer_full))[0].astype(BF)
        grad_inner_bias = jnp.sum(d_inner.astype(F32), axis=0)
        d_normed = d_res2 + nt(d_inner, inner_full)
        d_res1, grad_attn_gain, grad_attn_shift = first_pull(d_normed)
        d_attn = d_res1.astype(BF)
        grad_output_bias = jnp.sum(d_attn.astype(F32), axis=0)
        d_mixed = nt(d_attn, o_full).astype(BF)
        vec_a = jnp.stack(
            [grad_ffn_gain, grad_ffn_shift, grad_outer_bias] + [jnp.zeros((D,), F32)] * 5
        )
        ib = grad_inner_bias.reshape(sh.parts, -1, dn).transpose(1, 0, 2).reshape(-1, D)
        vec_b = jnp.concatenate(
            [
                jnp.stack(
                    [
                        grad_attn_gain, grad_attn_shift, grad_output_bias,
                        jnp.sum(d_mixed.astype(F32), axis=0),
                    ]
                ),
                ib,
            ],
            axis=0,
        )
    if sh.pair:
        d_attn_got = sh.trade(d_attn)
    dq, att_vec, dkv, d_table = att_bwd(
        q_lin, vecs, kind_q, d_mixed, mixed_f, probs, keys, values, table, kaug
    )
    if sh.pair:
        dq_got = sh.trade(dq)
        ffn = lax.psum_scatter(ffn, "ctx", scatter_dimension=0, tiled=False)
    else:
        gi, gu = (
            lax.psum_scatter(tn(a, b).astype(BF), "fsdp", scatter_dimension=0, tiled=True)
            for a, b in ((normed_low, d_inner), (activ_low, d_outer))
        )
        ffn = lax.psum((gi, gu), "ctx")

    dkv = dkv.reshape(2 * D, W)
    gkv, gp = (
        lax.dot_general(a, b, (((0,), (1,)), ((), ())), preferred_element_type=F32)
        for a, b in ((x_win, dkv), (sinus, d_table))
    )
    smalls = jnp.concatenate([att_vec, vec_a, vec_b], axis=0).astype(BF)
    smalls = jnp.transpose(jnp.pad(smalls, ((0, 128 - smalls.shape[0]), (0, 0))))
    sides = [[gkv[:, :D], gp[:, : D // 2], smalls], [gkv[:, D:], gp[:, D // 2 :], jnp.zeros_like(smalls)]]
    low, high = (jnp.concatenate([b.astype(BF) for b in a[1:]], axis=1) for a in sides)
    if sh.pair:
        kv_half = sh.halve_cols(sides[0][0], sides[1][0])
        rest = sh.halve_cols(low, high)
        whole = jnp.concatenate([kv_half, rest], axis=1)
        half = whole.shape[1]
        whole = whole.reshape(2, dn, half)
        keep = lax.dynamic_index_in_dim(whole, sh.f, 0, keepdims=False)
        send = lax.dynamic_index_in_dim(whole, 1 - sh.f, 0, keepdims=False)
        got_x = sh.trade(send)
        go = tn(
            jnp.concatenate([sh.own(mixed_low, 1), sh.own(mixed_got, 1)], axis=0),
            jnp.concatenate([d_attn, d_attn_got], axis=0),
        ).astype(BF)
        gq = tn(
            jnp.concatenate([sh.own(hidden, 1), sh.own(hidden_got, 1)], axis=0),
            jnp.concatenate([dq, dq_got], axis=0),
        ).astype(BF)
        dkv, _ = lax.optimization_barrier((dkv, rest))
    else:
        low, high = (jnp.concatenate([a[0].astype(BF), b], axis=1) for a, b in zip(sides, (low, high)))
        half = low.shape[1]
        low, high, go, gq = (
            lax.psum_scatter(a, "fsdp", scatter_dimension=0, tiled=True)
            for a in (low, high, tn(mixed_low, d_attn).astype(BF), tn(hidden, dq).astype(BF))
        )
        whole = sh.halve_cols(low, high)
    mine = sh.halve_cols(go, gq)

    d_hid = (tn(dkv[:D], jnp.transpose(k_full)) + tn(dkv[D:], jnp.transpose(v_full))).astype(BF)
    d_hid = jnp.pad(d_hid, (((C - 1 - R) * T, (C - 1) * T + L - (C - 1 - R) * T - W), (0, 0)))
    d_hid = lax.dynamic_slice_in_dim(d_hid, (C - 1 - ctx) * T, L, 0)
    d_hid = sh.halve(sh.spread(d_hid.reshape(C, T, D)), 0, sh.bits - 1)
    if sh.pair:
        got_x, d_hid, mine, ffn = lax.optimization_barrier((got_x, d_hid, mine, ffn))
        ffn = lax.all_gather(ffn, "ctx", axis=0, tiled=False)
        whole = (keep.astype(F32) + got_x.astype(F32)).astype(BF)

    grads = jnp.concatenate([whole, mine], axis=1)
    grads = grads.reshape((2,) * (sh.bits - 1) + (-1, grads.shape[1]))
    for k, other in zip(range(1, sh.bits), list(range(2, sh.bits)) + [1]):
        grads = sh.halve(grads, k, grads.ndim - 3)
        d_hid = sh.halve(d_hid, other, d_hid.ndim - 3 - (1 if other > 1 else 0))
        grads, d_hid = lax.optimization_barrier((grads, d_hid))
    for k in reversed(range(1, sh.bits)):
        grads = sh.double(grads, k, grads.ndim - 2)
        if sh.pair and k == 2:
            gi, gu = ffn_final(ffn, inner_bias.shape[0] * 2, D)
            gi, gu, grads = lax.optimization_barrier((gi, gu, grads))
    input_grad = d_res1 + nt(dq, q_full) + d_hid.astype(F32)
    if not sh.pair:
        gi, gu = (a.astype(F32) for a in ffn)
    grads = grads.reshape(dn, -1)
    low, high = sh.order(grads, sh.flip(grads, 0), sh.bit(0))
    gk, gv = low[:, :D].astype(F32), high[:, :D].astype(F32)
    gp = jnp.concatenate([a[:, D : D + D // 2] for a in (low, high)], axis=1).astype(F32)
    go, gq = low[:, half:].astype(F32), high[:, half:].astype(F32)
    s = jnp.transpose(low[:, D + D // 2 : half].astype(F32))
    return (
        outcome.astype(BF)[None],
        input_grad[None],
        gq,
        gk,
        gv,
        s[19],
        s[0],
        s[1],
        s[2],
        s[3:5],
        gp,
        go,
        s[18],
        s[16],
        s[17],
        gi,
        s[20:24].reshape(-1),
        gu,
        s[10],
        s[8],
        s[9],
    )


def solution(mesh):
    in_specs = (
        P("fsdp", "ctx", None),
        P("fsdp", "ctx"),
        P("fsdp", "ctx"),
        P("fsdp", "ctx", None),
        P("fsdp", None),
        P("fsdp", None),
        P("fsdp", None),
        P("fsdp"),
        P("fsdp"),
        P("fsdp"),
        P("fsdp"),
        P(None, "fsdp"),
        P("fsdp", None),
        P("fsdp", None),
        P("fsdp"),
        P("fsdp"),
        P("fsdp"),
        P("fsdp", None),
        P("fsdp"),
        P("fsdp", None),
        P("fsdp"),
        P("fsdp"),
        P("fsdp"),
    )
    out_specs = (
        P("fsdp", "ctx", None),
        P("fsdp", "ctx", None),
        P("fsdp", None),
        P("fsdp", None),
        P("fsdp", None),
        P("fsdp"),
        P("fsdp"),
        P("fsdp"),
        P("fsdp"),
        P(None, "fsdp"),
        P("fsdp", None),
        P("fsdp", None),
        P("fsdp"),
        P("fsdp"),
        P("fsdp"),
        P("fsdp", None),
        P("fsdp"),
        P("fsdp", None),
        P("fsdp"),
        P("fsdp"),
        P("fsdp"),
    )
    return jax.shard_map(
        per_device, mesh=mesh, in_specs=in_specs, out_specs=out_specs, check_vma=False
    )
```

```python
from functools import partial
import jax
import jax.numpy as jnp
from jax import lax
from jax.experimental import pallas as pl
from jax.experimental.pallas import tpu as pltpu
from jax.sharding import PartitionSpec as P

H = 12
DH = 64
EPS = 1e-06
BIG = 1e30
BF = jnp.bfloat16
F32 = jnp.float32


def nt(a, b):
    return lax.dot_general(a, b, (((1,), (1,)), ((), ())), preferred_element_type=F32)


def nn(a, b):
    return lax.dot_general(a, b, (((1,), (0,)), ((), ())), preferred_element_type=F32)


def tn(a, b):
    return lax.dot_general(a, b, (((0,), (0,)), ((), ())), preferred_element_type=F32)


def att_fwd_kernel(q_ref, v_rows, pen_ref, kind_ref, k_ref, v_ref, t_ref, ka_ref, o_ref, p_ref):
    T = q_ref.shape[0]
    W = k_ref.shape[0]
    blocks = W // T
    c = DH**-0.5
    q = q_ref[...]
    qc = ((q + v_rows[1:2, :]) * c).astype(BF)
    qp = ((q + v_rows[2:3, :]) * c).astype(BF)
    qt = (q + v_rows[3:4, :]) * c
    t0, t1 = qt * v_rows[4:5, :], qt * v_rows[5:6, :]
    lane = lax.broadcasted_iota(jnp.int32, (T, 128), 1)
    row = lax.broadcasted_iota(jnp.int32, (T, 128), 0)
    same = kind_ref[...] > 0.5
    pen = pen_ref[...]
    zero = jnp.zeros_like(qc)
    heads, where_q = [], []
    for h in range(2):
        mine = (lane < DH) if h == 0 else (lane >= DH)
        a0 = jnp.broadcast_to(jnp.sum(jnp.where(mine, t0, 0.0), axis=1, keepdims=True), (T, 128))
        a1 = jnp.broadcast_to(jnp.sum(jnp.where(mine, t1, 0.0), axis=1, keepdims=True), (T, 128))
        one, two = jnp.where(same, a1, a0), jnp.where(same, a0, a1)
        one_high, two_high = one.astype(BF).astype(F32), two.astype(BF).astype(F32)
        extra = jnp.where(lane == 4, two_high, jnp.where(lane == 5, two - two_high, pen))
        extra = jnp.where(lane == 0, one_high, jnp.where(lane == 1, one - one_high, extra))
        heads.append(jnp.concatenate([jnp.where(mine, qc, zero), extra.astype(BF)], axis=1))
        where_q.append(jnp.where(mine, qp, zero))
    s = nt(jnp.concatenate(heads, axis=0), jnp.concatenate([k_ref[...], ka_ref[...]], axis=1))
    w = nt(jnp.concatenate(where_q, axis=0), t_ref[...])
    probs = []
    for h in range(2):
        turned = [
            pltpu.roll(w[T * h : T * (h + 1), 128 * b : 128 * b + 128], 1, 1, stride=1, stride_axis=0)
            for b in range(blocks + 1)
        ]
        tiles = [
            s[T * h : T * (h + 1), 128 * b : 128 * b + 128]
            + jnp.where(lane <= row, turned[b], turned[b + 1])
            for b in range(blocks)
        ]
        top = tiles[0]
        for b in range(1, blocks):
            top = jnp.maximum(top, tiles[b])
        top = jnp.max(top, axis=1, keepdims=True)
        tiles = [jnp.exp(a - top) for a in tiles]
        total = tiles[0]
        for b in range(1, blocks):
            total = total + tiles[b]
        inverse = 1.0 / jnp.sum(total, axis=1, keepdims=True)
        p = jnp.concatenate([(a * inverse).astype(BF) for a in tiles], axis=1)
        p_ref[h] = p
        probs.append(p)
    out = nn(jnp.concatenate(probs, axis=0), v_ref[...])
    o_ref[...] = jnp.where(lane < DH, out[:T], out[T:])


def att_bwd_kernel(
    q_ref, v_rows, kind_ref, dm_ref, o_ref, p_ref, k_ref, v_ref, t_ref, ka_ref,
    dq_ref, vec_ref, dkv_ref, dt_ref,
):
    T = q_ref.shape[0]
    W = k_ref.shape[0]
    blocks = W // T
    c = DH**-0.5
    q = q_ref[...]
    qc = ((q + v_rows[1:2, :]) * c).astype(BF)
    qp = ((q + v_rows[2:3, :]) * c).astype(BF)
    qt = (q + v_rows[3:4, :]) * c
    e0, e1 = v_rows[4:5, :], v_rows[5:6, :]
    lane = lax.broadcasted_iota(jnp.int32, (T, 128), 1)
    row = lax.broadcasted_iota(jnp.int32, (T, 128), 0)
    same = kind_ref[...] > 0.5
    flip = jnp.where(lane + row == T - 1, 1.0, 0.0).astype(BF)
    qpr = nn(flip, qp).astype(BF)
    dm = dm_ref[...]
    dmo = dm.astype(F32) * o_ref[...]
    zero = jnp.zeros_like(dm)
    stack = lambda parts: jnp.concatenate(parts, axis=0)
    mine = [lane < DH, lane >= DH]
    pick = lambda a: stack([jnp.where(m, a, zero) for m in mine])
    dms = pick(dm)
    delta = jnp.sum(
        stack([jnp.where(m, dmo, 0.0) for m in mine]), axis=1, keepdims=True
    )
    dp = nt(dms, v_ref[...])
    p = stack([p_ref[0], p_ref[1]])
    ds = (p.astype(F32) * (dp - delta)).astype(BF)
    dc = nn(ds, jnp.concatenate([k_ref[...], ka_ref[...]], axis=1))
    wide = []
    for h in range(2):
        back = nn(flip, ds[T * h : T * (h + 1)])
        turned = [
            pltpu.roll(back[:, 128 * b : 128 * b + 128], 0, 1, stride=1, stride_axis=0)
            for b in range(blocks)
        ]
        edge = jnp.zeros((T, 128), F32)
        tiles = [
            jnp.where(lane >= row, a, b).astype(BF)
            for a, b in zip(turned + [edge], [edge] + turned)
        ]
        wide.append(jnp.concatenate(tiles, axis=1))
    wide = stack(wide)
    dqp = nn(wide, t_ref[...])
    dkv_ref[0] = tn(pick(qc), ds).astype(BF)
    dkv_ref[1] = tn(dms, p).astype(BF)
    dt_ref[...] = tn(pick(qpr), wide).astype(BF)
    both = lambda a: jnp.where(mine[0], a[:T], a[T:])
    dc_low = both(dc[:, :128]).astype(BF).astype(F32)
    dp_low = nn(flip, both(dqp).astype(BF))
    one = both(jnp.broadcast_to(dc[:, 128:129], (2 * T, 128)))
    two = both(jnp.broadcast_to(dc[:, 132:133], (2 * T, 128)))
    same_sum, other_sum = jnp.where(same, one, two), jnp.where(same, two, one)
    dt = other_sum * e0 + same_sum * e1
    dq_ref[...] = (c * (dc_low + dp_low + dt)).astype(BF)
    total = lambda a: jnp.sum(a, axis=0, keepdims=True)
    rows = [c * total(dc_low), c * total(dp_low), c * total(dt), total(other_sum * qt), total(same_sum * qt)]
    vec_ref[...] = jnp.concatenate(rows + [jnp.zeros((3, 128), F32)], axis=0)


def att_fwd(q, rows, pen, kind, kv, t, ka):
    T, D = q.shape
    W = kv.shape[0]
    keys, values = (pl.BlockSpec((W, 128), lambda i, n=n: (0, i + n * D // 128)) for n in range(2))
    heads = D // DH
    col = lambda n: pl.BlockSpec((n, 128), lambda i: (0, i))
    fixed = lambda n: pl.BlockSpec((n, 128), lambda i: (0, 0))
    return pl.pallas_call(
        att_fwd_kernel,
        grid=(D // 128,),
        in_specs=[col(T), col(16), fixed(T), fixed(T), keys, values, col(W + T), fixed(W)],
        out_specs=[col(T), pl.BlockSpec((2, T, W), lambda i: (i, 0, 0))],
        out_shape=[
            jax.ShapeDtypeStruct((T, D), F32),
            jax.ShapeDtypeStruct((heads, T, W), BF),
        ],
        compiler_params=pltpu.CompilerParams(vmem_limit_bytes=60 * 2**20),
        cost_estimate=pl.CostEstimate(
            flops=2 * heads * T * W * 2048,
            bytes_accessed=2 * (3 * W * D + heads * T * W),
            transcendentals=heads * T * W,
        ),
        name="att_fwd",
    )(q, rows, pen, kind, kv, kv, t, ka)


def att_bwd(q, rows, kind, dm, o, p, kv, t, ka):
    T, D = q.shape
    W = kv.shape[0]
    keys, values = (pl.BlockSpec((W, 128), lambda i, n=n: (0, i + n * D // 128)) for n in range(2))
    heads = D // DH
    col = lambda n: pl.BlockSpec((n, 128), lambda i: (0, i))
    fixed = lambda n: pl.BlockSpec((n, 128), lambda i: (0, 0))
    return pl.pallas_call(
        att_bwd_kernel,
        grid=(D // 128,),
        in_specs=[
            col(T), col(16), fixed(T), col(T), col(T), pl.BlockSpec((2, T, W), lambda i: (i, 0, 0)),
            keys, values, col(W + T), fixed(W),
        ],
        out_specs=[
            col(T), col(8), pl.BlockSpec((2, 128, W), lambda i: (0, i, 0)),
            pl.BlockSpec((128, W + T), lambda i: (i, 0)),
        ],
        out_shape=[
            jax.ShapeDtypeStruct((T, D), BF),
            jax.ShapeDtypeStruct((8, D), F32),
            jax.ShapeDtypeStruct((2, D, W), BF),
            jax.ShapeDtypeStruct((D, W + T), BF),
        ],
        compiler_params=pltpu.CompilerParams(vmem_limit_bytes=60 * 2**20),
        cost_estimate=pl.CostEstimate(
            flops=2**20, bytes_accessed=2**20, transcendentals=0
        ),
        name="att_bwd",
    )(q, rows, kind, dm, o, p, kv, kv, t, ka)


def pack_rows(vectors, dn):
    counts = [v.size // dn for v in vectors]

    def kernel(*refs):
        out = refs[-1]
        at = 0
        for ref, n in zip(refs, counts):
            for j in range(n):
                if len(ref.shape) == 1:
                    out[at, :] = ref[pl.ds(j * dn, dn)].astype(F32)
                else:
                    out[at, :] = ref[j, :].astype(F32)
                at += 1

    return pl.pallas_call(
        kernel,
        out_shape=jax.ShapeDtypeStruct((sum(counts), dn), F32),
        name="pack_rows",
    )(*vectors)


def ffn_final(blocks, FF, D):
    count, _, dn = blocks.shape
    steps = FF // D
    per = count // steps
    ri, ru = FF // count, FF // 2 // count

    def kernel(b_ref, i_ref, u_ref):
        gi = jnp.concatenate([b_ref[k, :ri] for k in range(per)], axis=0)
        i_ref[...] = jnp.transpose(gi.astype(F32))
        for k in range(per):
            u_ref[ru * k : ru * (k + 1), :dn] = b_ref[k, ri : ri + ru].astype(F32)
            u_ref[ru * k : ru * (k + 1), dn:] = b_ref[k, ri + ru :].astype(F32)

    return pl.pallas_call(
        kernel,
        grid=(steps,),
        in_specs=[pl.BlockSpec((per, ri + 2 * ru, dn), lambda i: (i, 0, 0))],
        out_specs=[
            pl.BlockSpec((dn, D), lambda i: (0, i)), pl.BlockSpec((FF // 2 // steps, D), lambda i: (i, 0))
        ],
        out_shape=[
            jax.ShapeDtypeStruct((dn, FF), F32), jax.ShapeDtypeStruct((FF // 2, D), F32)
        ],
        cost_estimate=pl.CostEstimate(flops=2**33, bytes_accessed=8 * D * FF, transcendentals=0),
        name="ffn_final",
    )(blocks)


def split_cols(a, f, odd):
    h = a.shape[1] // 2
    q = h // 2
    own = jnp.where(f == 0, a[:, :h], a[:, h:])
    other = jnp.where(f == 0, a[:, h:], a[:, :h])
    swapped = jnp.concatenate([other[:, q:], other[:, :q]], axis=1)
    return jnp.concatenate([own, jnp.where(odd, swapped, other)], axis=1)


def merge_cols(a, f, odd):
    h = a.shape[1] // 2
    q = h // 2
    own, other = a[:, :h], a[:, h:]
    swapped = jnp.concatenate([other[:, q:], other[:, :q]], axis=1)
    other = jnp.where(odd, swapped, other)
    return jnp.where(
        f == 0, jnp.concatenate([own, other], axis=1), jnp.concatenate([other, own], axis=1)
    )


def swap_quarters(a, y, odd):
    h = a.shape[1] // 2
    q = h // 2
    a = jnp.where(y, jnp.concatenate([a[:, h:], a[:, :h]], axis=1), a)
    pairs = jnp.concatenate([a[:, q:h], a[:, :q], a[:, h + q :], a[:, h : h + q]], axis=1)
    return jnp.where(odd, pairs, a)


def middle_swap(a):
    q = a.shape[1] // 4
    return jnp.concatenate([a[:, :q], a[:, 2 * q : 3 * q], a[:, q : 2 * q], a[:, 3 * q :]], axis=1)


def split_quarters(a, f, y, odd):
    h = a.shape[1] // 2
    own = jnp.where(f == 0, a[:, :h], a[:, h:])
    other = jnp.where(f == 0, a[:, h:], a[:, :h])
    return own, middle_swap(swap_quarters(other, y, odd))


def merge_quarters(a, f, y, odd):
    h = a.shape[1] // 2
    own, other = a[:, :h], swap_quarters(middle_swap(a[:, h:]), y, odd)
    return jnp.where(
        f == 0, jnp.concatenate([own, other], axis=1), jnp.concatenate([other, own], axis=1)
    )


def norm_stats(res):
    center = res - jnp.mean(res, axis=1, keepdims=True)
    rstd = lax.rsqrt(jnp.mean(center * center, axis=1, keepdims=True) + EPS)
    return center * rstd, rstd


def norm_back(g, gain, n, rstd):
    gg = g * gain
    return (gg - jnp.mean(gg, axis=1, keepdims=True) - n * jnp.mean(gg * n, axis=1, keepdims=True)) * rstd


def row_sum(a):
    return jnp.sum(a, axis=0, keepdims=True)


GELU_A = 0.7978845608028654
GELU_B = 0.044715


def ffn_specs(T, D, FF):
    steps = FF // D
    half = steps // 2
    c = FF // steps
    q = D // 8

    def chunk_at(j, s):
        other = half * (1 - s[0]) + (s[2] ^ jnp.maximum(j - half, 0))
        return jnp.where(j < half, half * s[0] + j, other)

    col = lambda j, s: (0, chunk_at(j, s))
    whole = lambda *shape: pl.BlockSpec(shape, lambda j, s: (0,) * len(shape))
    inner = [pl.BlockSpec((4 * q, c), col)] + [pl.BlockSpec((q, c), col)] * 4
    outer = [pl.BlockSpec((c, D), lambda j, s: (jnp.minimum(j, half - 1), 0))]
    outer += [whole(c // 2, D)] * 4
    proj = [whole(4 * q, D), whole(2 * q, D), whole(2 * q, D)]
    return steps, half, c, chunk_at, col, whole, inner, outer, proj


def outer_chunk(j, half, odd, refs):
    last = j > half
    a = jnp.where(last, refs[2][...], refs[1][...])
    b = jnp.where(last, refs[4][...], refs[3][...])
    pair = jnp.concatenate([jnp.where(odd, b, a), jnp.where(odd, a, b)], axis=0)
    return jnp.where(j < half, refs[0][...], pair)


def rows_of(refs):
    return jnp.concatenate([r[...] for r in refs], axis=0)


def inner_bias_chunk(b, half, vec_ref, D):
    rows = [vec_ref[pl.ds(12 + 2 * (b % half) + n, 1), :] for n in range(2)]
    parts = [jnp.where(b < half, r[:, : D // 2], r[:, D // 2 :]) for r in rows]
    return jnp.concatenate(parts, axis=1)


def gelu_tanh(u):
    return jnp.tanh(GELU_A * (u + GELU_B * u * u * u))


def first_norm(x, mixed, vec_ref, w, f, odd):
    attn = nn(split_cols(mixed, f, odd).astype(BF), w) + vec_ref[6:7, :]
    n1, rstd = norm_stats(x.astype(F32) + attn)
    return n1, rstd, n1 * vec_ref[7:8, :] + vec_ref[8:9, :]


def ffn_fwd(place, x, mixed, cot, vecs, o_parts, i_parts, u_parts, FF):
    T, D = x.shape
    steps, half, c, chunk_at, col, whole, inner, outer, proj = ffn_specs(T, D, FF)

    def kernel(s_ref, x_ref, m_ref, g_ref, v_ref, *refs):
        o_refs, i_refs, u_refs = refs[:3], refs[3:8], refs[8:13]
        nl_ref, act_ref, pre_ref, res_ref, dr_ref, do_ref, n1_ref, rs_ref, gv_ref = refs[13:22]
        np_ref, acc_ref, nf_ref = refs[22:]
        j = pl.program_id(0)
        f, odd, y = s_ref[0], s_ref[1] == 1, s_ref[2] == 1

        @pl.when(j == 0)
        def _():
            n1, rstd, normed = first_norm(x_ref[...], m_ref[...], v_ref, rows_of(o_refs), f, odd)
            n1_ref[...] = n1
            rs_ref[...] = jnp.broadcast_to(rstd, (T, 128))
            nf_ref[...] = normed
            nl_ref[...] = normed.astype(BF)
            np_ref[...] = jnp.concatenate(split_quarters(normed, f, y, odd), axis=1).astype(BF)
            acc_ref[...] = jnp.zeros_like(acc_ref)

        bias = inner_bias_chunk(chunk_at(j, s_ref), half, v_ref, D)
        pre = nn(np_ref[...], rows_of(i_refs)) + bias
        pre_ref[...] = pre
        act = (0.5 * pre * (1.0 + gelu_tanh(pre))).astype(BF)
        act_ref[...] = act
        acc_ref[...] += nn(act, outer_chunk(j, half, odd, u_refs))

        @pl.when(j == steps - 1)
        def _():
            n2, rstd = norm_stats(nf_ref[...] + (acc_ref[...] + v_ref[9:10, :]))
            g = g_ref[...].astype(F32)
            res_ref[...] = (n2 * v_ref[10:11, :] + v_ref[11:12, :]).astype(BF)
            d = norm_back(g, v_ref[10:11, :], n2, rstd)
            dr_ref[...] = d
            do = d.astype(BF)
            do_ref[...] = do
            gv_ref[0:1, :] = row_sum(g * n2)
            gv_ref[1:2, :] = row_sum(g)
            gv_ref[2:3, :] = row_sum(do.astype(F32))
            gv_ref[3:8, :] = jnp.zeros((5, D), F32)

    f32 = lambda *shape: jax.ShapeDtypeStruct(shape, F32)
    low = lambda *shape: jax.ShapeDtypeStruct(shape, BF)
    tok = whole(T, D)
    chunk = pl.BlockSpec((T, c), col)
    return pl.pallas_call(
        kernel,
        grid_spec=pltpu.PrefetchScalarGridSpec(
            num_scalar_prefetch=1,
            grid=(steps,),
            in_specs=[tok, tok, tok, whole(16, D)] + proj + inner + outer,
            out_specs=[tok, chunk, chunk, tok, tok, tok, tok, whole(T, 128), whole(8, D)],
            scratch_shapes=[
                pltpu.VMEM((T, D), BF), pltpu.VMEM((T, D), F32), pltpu.VMEM((T, D), F32)
            ],
        ),
        out_shape=[
            low(T, D), low(T, FF), f32(T, FF), low(T, D), f32(T, D), low(T, D), f32(T, D),
            f32(T, 128), f32(8, D),
        ],
        compiler_params=pltpu.CompilerParams(vmem_limit_bytes=60 * 2**20),
        cost_estimate=pl.CostEstimate(
            flops=4 * T * D * FF, bytes_accessed=4 * D * FF, transcendentals=T * FF
        ),
        name="ffn_fwd",
    )(place, x, mixed, cot, vecs, *o_parts, *i_parts, *u_parts)


def ffn_bwd(
    place, count, pre, act, normed, d_outer, d_outer_got, d_res2, n1, rstd1, mixed_got, x_got,
    vecs, o_parts, i_parts, u_parts,
):
    T, FF = pre.shape
    D = d_outer.shape[1]
    dn = D // 2
    steps, half, c, chunk_at, col, whole, inner, outer, proj = ffn_specs(T, D, FF)
    ri, ru = FF // count, FF // 2 // count

    def kernel(s_ref, pre_ref, act_ref, nl_ref, do_ref, dog_ref, dr_ref, n1_ref, rs_ref, mg_ref, xg_ref, v_ref, *refs):
        o_refs, i_refs, u_refs = refs[:3], refs[3:8], refs[8:13]
        pay_ref, d1_ref, da_ref, dm_ref, gv_ref = refs[13:18]
        acc_ref, ib_ref, np_ref, nf_ref, do_both = refs[18:]
        j = pl.program_id(0)
        f, odd, y = s_ref[0], s_ref[1] == 1, s_ref[2] == 1

        @pl.when(j == 0)
        def _():
            acc_ref[...] = jnp.zeros_like(acc_ref)
            theirs = first_norm(xg_ref[...], mg_ref[...], v_ref, rows_of(o_refs), f, odd)[2]
            own, other = split_quarters(theirs, f, y, odd)
            np_ref[...] = jnp.concatenate([own, other], axis=1).astype(BF)
            nl = nl_ref[...]
            nf_ref[:T] = jnp.where(f == 0, nl[:, :dn], nl[:, dn:])
            nf_ref[T:] = own.astype(BF)
            do_both[:T] = do_ref[...]
            do_both[T:] = dog_ref[...]

        b = chunk_at(j, s_ref)
        w = rows_of(i_refs)
        pre_got = nn(np_ref[...], w) + inner_bias_chunk(b, half, v_ref, D)
        u = jnp.concatenate([pre_ref[...], pre_got], axis=0)
        t = gelu_tanh(u)
        slope = 0.5 * (1.0 + t) + 0.5 * u * (1.0 - t * t) * (GELU_A * (1.0 + 3.0 * GELU_B * u * u))
        di = (nt(do_both[...], outer_chunk(j, half, odd, u_refs)) * slope).astype(BF)
        ib_ref[pl.ds(b, 1), :] = row_sum(di[:T].astype(F32))
        acc_ref[...] += nt(di[:T], w)
        gi = tn(di, nf_ref[...]).astype(BF)
        for k in range(c // ri):
            pay_ref[b * (c // ri) + k, :ri] = gi[ri * k : ri * (k + 1)]

        @pl.when(j < half)
        def _():
            act_got = (0.5 * u[T:] * (1.0 + t[T:])).astype(BF)
            gu = tn(jnp.concatenate([act_ref[...], act_got], axis=0), do_both[...]).astype(BF)
            for k in range(c // ru):
                pay_ref[j * (c // ru) + k, ri : ri + ru] = gu[ru * k : ru * (k + 1), :dn]
                pay_ref[j * (c // ru) + k, ri + ru :] = gu[ru * k : ru * (k + 1), dn:]

        @pl.when(j == steps - 1)
        def _():
            d_normed = dr_ref[...] + merge_quarters(acc_ref[...], f, y, odd)
            n1 = n1_ref[...]
            d1 = norm_back(d_normed, v_ref[7:8, :], n1, rs_ref[:, 0:1])
            d1_ref[...] = d1
            da = d1.astype(BF)
            da_ref[...] = da
            dm = merge_cols(nt(da, rows_of(o_refs)), f, odd)
            dm_ref[...] = dm.astype(BF)
            gv_ref[0:1, :] = row_sum(d_normed * n1)
            gv_ref[1:2, :] = row_sum(d_normed)
            gv_ref[2:3, :] = row_sum(da.astype(F32))
            gv_ref[3:4, :] = row_sum(dm.astype(BF).astype(F32))
            for n in range(2 * half):
                at = slice(0, dn) if n % 2 == 0 else slice(dn, D)
                gv_ref[4 + n : 5 + n, :dn] = ib_ref[n // 2 : n // 2 + 1, at]
                gv_ref[4 + n : 5 + n, dn:] = ib_ref[half + n // 2 : half + n // 2 + 1, at]

    f32 = lambda *shape: jax.ShapeDtypeStruct(shape, F32)
    low = lambda *shape: jax.ShapeDtypeStruct(shape, BF)
    tok = whole(T, D)
    chunk = pl.BlockSpec((T, c), col)
    return pl.pallas_call(
        kernel,
        grid_spec=pltpu.PrefetchScalarGridSpec(
            num_scalar_prefetch=1,
            grid=(steps,),
            in_specs=[chunk, chunk] + [tok] * 5 + [whole(T, 128), tok, tok, whole(16, D)]
            + proj + inner + outer,
            out_specs=[whole(count, ri + 2 * ru, dn), tok, tok, tok, whole(8, D)],
            scratch_shapes=[
                pltpu.VMEM((T, D), F32), pltpu.VMEM((steps, c), F32), pltpu.VMEM((T, D), BF),
                pltpu.VMEM((2 * T, dn), BF), pltpu.VMEM((2 * T, D), BF),
            ],
        ),
        out_shape=[low(count, ri + 2 * ru, dn), f32(T, D), low(T, D), low(T, D), f32(8, D)],
        compiler_params=pltpu.CompilerParams(vmem_limit_bytes=60 * 2**20),
        cost_estimate=pl.CostEstimate(
            flops=14 * T * D * FF, bytes_accessed=6 * D * FF, transcendentals=2 * T * FF
        ),
        name="ffn_bwd",
    )(
        place, pre, act, normed, d_outer, d_outer_got, d_res2, n1, rstd1, mixed_got, x_got, vecs,
        *o_parts, *i_parts, *u_parts,
    )


def key_grads(dkv, d_table, x_win, sinus, vectors):
    _, D, W = dkv.shape
    WT = d_table.shape[1]
    h = D // 2

    def kernel(kv_ref, t_ref, x_ref, s_ref, *refs):
        v_refs, out_ref = refs[:-1], refs[-1]
        i = pl.program_id(0)
        core, part = i // 3, i % 3
        at = pl.ds(pl.multiple_of(part * h, h), h)

        @pl.when(part < 2)
        def _():
            out_ref[core, at, :] = nn(kv_ref[0], x_ref[...]).astype(BF)

        @pl.when(part == 2)
        def _():
            out_ref[core, at, :] = nn(t_ref[...], s_ref[...]).astype(BF)

        @pl.when(i == 0)
        def _():
            small = jnp.concatenate([r[...] for r in v_refs], axis=0)
            pad = jnp.zeros((64 - small.shape[0], D), F32)
            out_ref[0, 3 * h :, :] = jnp.concatenate([small, pad], axis=0).astype(BF)
            out_ref[1, 3 * h :, :] = jnp.zeros((64, D), BF)

    whole = lambda *shape: pl.BlockSpec(shape, lambda i: (0,) * len(shape))
    return pl.pallas_call(
        kernel,
        grid=(6,),
        in_specs=[
            pl.BlockSpec((1, h, W), lambda i: (i // 3, jnp.minimum(i % 3, 1), 0)),
            pl.BlockSpec((h, WT), lambda i: (i // 3, 0)),
            whole(W, D),
            whole(WT, D),
        ]
        + [whole(8, D)] * len(vectors),
        out_specs=whole(2, 3 * h + 64, D),
        out_shape=jax.ShapeDtypeStruct((2, 3 * h + 64, D), BF),
        compiler_params=pltpu.CompilerParams(vmem_limit_bytes=60 * 2**20),
        cost_estimate=pl.CostEstimate(flops=2**20, bytes_accessed=2**20, transcendentals=0),
        name="key_grads",
    )(dkv, d_table, x_win, sinus, *vectors)


def hidden_grads(place, dkv, k_own, k_other, v_own, v_other, count, reach):
    D2, W = dkv.shape
    D = D2 // 2
    h = D // 2
    T = 128
    blocks = W // T

    def kernel(s_ref, a_ref, b_ref, k0, k1, v0, v1, out_ref):
        s = pl.program_id(0)
        x = jnp.concatenate([a_ref[...], b_ref[...]], axis=1)
        for at, k, v in ((s_ref[0], k0, v0), (1 - s_ref[0], k1, v1)):
            g = nn(jnp.concatenate([k[...], v[...]], axis=1), x).astype(BF)
            for n in range(2):
                rel = 2 * s + n - s_ref[3] + reach
                ok = (rel >= 0) & (rel < blocks)
                part = g[:, T * n : T * (n + 1)]
                out_ref[n, pl.ds(pl.multiple_of(at * h, h), h), :] = jnp.where(
                    ok, part, jnp.zeros_like(part)
                )

    whole = pl.BlockSpec((h, D), lambda s, p: (0, 0))
    block = lambda n: pl.BlockSpec(
        (D2, T), lambda s, p: (0, jnp.clip(2 * s + n - p[3] + reach, 0, blocks - 1))
    )
    return pl.pallas_call(
        kernel,
        grid_spec=pltpu.PrefetchScalarGridSpec(
            num_scalar_prefetch=1,
            grid=(count // 2,),
            in_specs=[block(0), block(1), whole, whole, whole, whole],
            out_specs=pl.BlockSpec((2, D, T), lambda s, p: (s, 0, 0)),
        ),
        out_shape=jax.ShapeDtypeStruct((count, D, T), BF),
        compiler_params=pltpu.CompilerParams(vmem_limit_bytes=60 * 2**20),
        cost_estimate=pl.CostEstimate(
            flops=2 * D2 * D * T * count, bytes_accessed=8 * D2 * W, transcendentals=0
        ),
        name="hidden_grads",
    )(place, dkv, dkv, k_own, k_other, v_own, v_other)


def input_grads(place, d_res1, dq, q_own, q_other, d_hid):
    T, D = d_res1.shape

    def kernel(s_ref, r_ref, dq_ref, q0, q1, h_ref, out_ref):
        own, other = nt(dq_ref[...], q0[...]), nt(dq_ref[...], q1[...])
        first = s_ref[0] == 0
        g = jnp.concatenate([jnp.where(first, own, other), jnp.where(first, other, own)], axis=1)
        out_ref[...] = r_ref[...] + g + jnp.transpose(h_ref[...].astype(F32))

    whole = lambda a: pl.BlockSpec(a.shape, lambda i, s: (0, 0))
    args = (d_res1, dq, q_own, q_other, d_hid)
    return pl.pallas_call(
        kernel,
        grid_spec=pltpu.PrefetchScalarGridSpec(
            num_scalar_prefetch=1,
            grid=(1,),
            in_specs=[whole(a) for a in args],
            out_specs=whole(d_res1),
        ),
        out_shape=jax.ShapeDtypeStruct((T, D), F32),
        cost_estimate=pl.CostEstimate(
            flops=2**32, bytes_accessed=2**24, transcendentals=0
        ),
        name="input_grads",
    )(place, *args)


def grad_final(place, one, two, one_got, two_got, D, blocks):
    dn = one.shape[1]
    h = D // 2
    p, q = one.shape[0] // blocks, two.shape[0] // blocks

    def kernel(s_ref, a_ref, b_ref, c_ref, d_ref, k_ref, v_ref, p_ref, o_ref, q_ref, small_ref):
        odd = s_ref[1] == 1

        def rows(x_ref, y_ref):
            x, y = x_ref[...].astype(F32), y_ref[...].astype(F32)
            parts = []
            for n in range(blocks):
                parts += [x[p * n : p * (n + 1)], y[q * n : q * (n + 1)]]
            return jnp.concatenate(parts, axis=0)

        mine, other = rows(a_ref, b_ref), rows(c_ref, d_ref)
        low, high = jnp.where(odd, other, mine), jnp.where(odd, mine, other)
        k_ref[...] = jnp.transpose(low[:D])
        v_ref[...] = jnp.transpose(high[:D])
        p_ref[...] = jnp.transpose(jnp.concatenate([low[D : D + h], high[D : D + h]], axis=0))
        small_ref[...] = low[D + h : D + h + 64]
        o_ref[...] = jnp.transpose(low[D + h + 64 :])
        q_ref[...] = jnp.transpose(high[D + h + 64 :])

    lanes = lambda n: pl.BlockSpec((n, 128), lambda i, s: (0, i))
    out = pl.BlockSpec((128, D), lambda i, s: (i, 0))
    return pl.pallas_call(
        kernel,
        grid_spec=pltpu.PrefetchScalarGridSpec(
            num_scalar_prefetch=1,
            grid=(dn // 128,),
            in_specs=[lanes(a.shape[0]) for a in (one, two, one_got, two_got)],
            out_specs=[out] * 5 + [lanes(64)],
        ),
        out_shape=[jax.ShapeDtypeStruct((dn, D), F32)] * 5 + [jax.ShapeDtypeStruct((64, dn), F32)],
        name="grad_final",
    )(place, one, two, one_got, two_got)


def unpack_rows(s):
    dn = s.shape[1]
    singles = (19, 0, 1, 2, 18, 16, 17, 10, 8, 9)

    def kernel(s_ref, *outs):
        for i, out in zip(singles, outs):
            out[...] = s_ref[i, :]
        outs[-2][...] = s_ref[3:5, :]
        for j in range(4):
            outs[-1][pl.ds(j * dn, dn)] = s_ref[20 + j, :]

    shapes = [(dn,)] * len(singles) + [(2, dn), (4 * dn,)]
    return pl.pallas_call(
        kernel,
        out_shape=[jax.ShapeDtypeStruct(a, F32) for a in shapes],
        name="unpack_rows",
    )(s)


def layer_norm(residual, gain_vec, bias_vec):
    center = residual - jnp.mean(residual, axis=-1, keepdims=True)
    spread = jnp.mean(center * center, axis=-1, keepdims=True)
    return center * lax.rsqrt(spread + EPS) * gain_vec + bias_vec


def sinus_rows(first, count, width):
    half = width // 2
    freq = jnp.power(10000.0, -jnp.arange(half, dtype=F32) / half)
    coarse = (first - 64 * jnp.arange(count // 64)).astype(F32)[:, None] * freq
    fine = jnp.arange(64).astype(F32)[:, None] * freq
    sa, ca = jnp.sin(coarse)[:, None], jnp.cos(coarse)[:, None]
    sb, cb = jnp.sin(fine)[None], jnp.cos(fine)[None]
    both = jnp.concatenate([sa * cb - ca * sb, ca * cb + sa * sb], axis=2)
    return both.astype(BF).reshape(count, width)


class Shards:
    def __init__(self):
        self.parts = lax.axis_size("fsdp")
        self.pair = self.parts == 2
        self.f = lax.axis_index("fsdp")
        self.ctx = lax.axis_index("ctx")
        self.count = lax.axis_size("ctx")
        self.bits = self.count.bit_length() - 1
        self.swap = [(0, 1), (1, 0)]

    def bit(self, k):
        return (self.ctx >> k) & 1

    def flip(self, a, k):
        return lax.ppermute(a, "ctx", [(i, i ^ (1 << k)) for i in range(self.count)])

    def trade(self, a):
        return lax.ppermute(a, "fsdp", self.swap)

    def order(self, mine, other, at):
        return jnp.where(at == 0, mine, other), jnp.where(at == 0, other, mine)

    def fetch_half(self, w):
        half = w.shape[0] // 2
        return self.trade(lax.dynamic_slice_in_dim(w, self.bit(0) * half, half, 0))

    def fetch_quarter(self, w):
        n = w.shape[0] // 4
        return self.trade(lax.dynamic_slice_in_dim(w, (self.ctx % 4) * n, n, 0))

    def pieces(self, got, y):
        return got, y, self.flip(got, 0), self.flip(y, 0)

    def full_small(self, w):
        if not self.pair:
            return lax.all_gather(w, "fsdp", axis=0, tiled=False)
        return jnp.stack(self.order(w, self.trade(w), self.f))

    def own(self, a, axis, other=False):
        n = a.shape[axis] // self.parts
        at = (1 - self.f) if other else self.f
        return lax.dynamic_slice_in_dim(a, at * n, n, axis)

    def window(self, block, planes):
        y = self.flip(block, 1)
        self.first_hop = y
        pair = jnp.stack(self.order(block, y, self.bit(1)))
        up = down = pair
        groups = [(pair[None], self.flip(pair[None], 0))]
        for _ in range(planes):
            up = lax.ppermute(up, "ctx", [(i, i + 4) for i in range(self.count - 4)])
            down = lax.ppermute(down, "ctx", [(i + 4, i) for i in range(self.count - 4)])
            both = jnp.stack([up, down])
            groups.append((both, self.flip(both, 0)))
        self.last_hop = both
        groups = [jnp.stack(self.order(a, b, self.bit(0)), axis=2) for a, b in groups]
        planes = [g[0] for g in groups[:0:-1]] + [groups[0][0]] + [g[1] for g in groups[1:]]
        return jnp.concatenate(planes, axis=0).reshape((-1,) + block.shape)

    def halve(self, a, k, axis):
        keep = lax.dynamic_index_in_dim(a, self.bit(k), axis, keepdims=False)
        send = lax.dynamic_index_in_dim(a, 1 - self.bit(k), axis, keepdims=False)
        return (keep.astype(F32) + self.flip(send, k).astype(F32)).astype(BF)

    def halve_cols(self, low, high):
        keep, send = self.order(low, high, self.bit(0))
        return (keep.astype(F32) + self.flip(send.astype(BF), 0).astype(F32)).astype(BF)

    def double(self, a, k, axis):
        return jnp.stack(self.order(a, self.flip(a, k), self.bit(k)), axis=axis)

    def spread(self, a):
        return a.reshape((2,) * self.bits + a.shape[1:])


def per_device(
    hidden_in,
    segment_ids,
    token_types,
    out_grad,
    query_proj,
    key_proj,
    value_proj,
    value_bias,
    content_bias,
    position_bias,
    type_bias,
    type_embed,
    position_proj,
    output_proj,
    output_bias,
    attn_gain,
    attn_shift,
    inner_proj,
    inner_bias,
    outer_proj,
    outer_bias,
    ffn_gain,
    ffn_shift,
):
    sh = Shards()
    hidden = hidden_in[0]
    cotangent = out_grad[0].astype(F32)
    T, D = hidden.shape
    C = sh.count
    ctx = sh.ctx
    L = T * C
    R = C // 2
    NB = 2 * R + 1
    W = NB * T
    dn = D // sh.parts
    r = dn // C

    lane = jnp.arange(128)[None, :]
    in_seg = (lane >= 8) & (lane < 16)
    seg_own = segment_ids[0][:, None]
    kind_own = token_types[0][:, None]
    kaug_own = jnp.where(
        lane < 4, kind_own == 1, jnp.where(lane < 8, kind_own == 0, in_seg & (lane - 8 == seg_own))
    ).astype(BF)
    pen = jnp.where(in_seg & (lane - 8 != seg_own), -BIG, 0.0).astype(F32)
    kind_q = jnp.broadcast_to(kind_own, (T, 128)).astype(F32)

    around = sh.window(jnp.concatenate([hidden, kaug_own], axis=1), R // 4)
    around = lax.dynamic_slice_in_dim(around, ctx % 4, NB, 0)
    x_win = around[:, :, :D].reshape(W, D)
    at = jnp.arange(NB) + ctx - R
    valid = ((at >= 0) & (at < C))[:, None, None]
    kaug = jnp.where(valid, around[:, :, D:], (lane[None] == 15).astype(BF)).reshape(W, 128)

    vectors = (
        value_bias, content_bias, position_bias, type_bias, type_embed, output_bias,
        attn_gain, attn_shift, outer_bias, ffn_gain, ffn_shift, inner_bias,
    )
    small = pack_rows(vectors, dn)
    small_full = sh.full_small(small)
    if sh.pair:
        odd = sh.bit(0) == 1
        got_a = sh.trade(jnp.where(odd, value_proj, position_proj))
        got_b = sh.trade(jnp.where(odd, key_proj, query_proj))
        got_o = sh.fetch_half(output_proj)
        got_a, got_b, got_o, i_sh, u_sh, small_full, _ = lax.optimization_barrier(
            (got_a, got_b, got_o, inner_proj, outer_proj, small_full, sh.last_hop)
        )
        other_p, other_v = sh.order(got_a, sh.flip(got_a, 0), sh.bit(0))
        other_q, other_k = sh.order(got_b, sh.flip(got_b, 0), sh.bit(0))
        p_full, q_full = (
            jnp.concatenate(sh.order(w, g, sh.f), axis=0)
            for w, g in ((position_proj, other_p), (query_proj, other_q))
        )
        own, other = (
            jnp.concatenate(a, axis=1) for a in ((key_proj, value_proj), (other_k, other_v))
        )
        kv_full = jnp.concatenate(sh.order(own, other, sh.f), axis=0)
        flip_o = sh.flip(got_o, 0)
        i_got, u_got = sh.fetch_quarter(i_sh), sh.fetch_quarter(u_sh)
    else:
        p_full, k_full, v_full, q_full, o_full, inner_full, outer_full = (
            lax.all_gather(w, "fsdp", axis=0, tiled=True)
            for w in (
                position_proj, key_proj, value_proj, query_proj, output_proj, inner_proj, outer_proj
            )
        )
        kv_full = jnp.concatenate([k_full, v_full], axis=1)

    vecs = jnp.concatenate([small_full[i] for i in range(sh.parts)], axis=1)

    q_lin = nn(hidden, q_full)
    if sh.pair:
        i_got, x_win = lax.optimization_barrier((i_got, x_win))
    kv_bias = jnp.concatenate([jnp.zeros((D,), F32), vecs[0]])
    key_values = (nn(x_win, kv_full) + kv_bias).astype(BF)
    sinus = lax.optimization_barrier(sinus_rows(T + R * T - 1, W + T, D))
    table = nn(sinus, p_full).astype(BF)

    if sh.pair:
        i_y = sh.flip(i_got, 1)
        u_got, key_values = lax.optimization_barrier((u_got, key_values))
        u_y = sh.flip(u_got, 1)
    mixed_f, probs = att_fwd(q_lin, vecs, pen, kind_q, key_values, table, kaug)
    mixed_low = mixed_f.astype(BF)
    if sh.pair:
        place = jnp.stack([sh.f, sh.bit(0), sh.bit(1), ctx])
        mixed_f, hid, fetched = lax.optimization_barrier((mixed_f, hidden, (i_got, i_y, u_got, u_y)))
        hidden_got = sh.trade(hid)
        mixed_low = mixed_f.astype(BF)
        parts = (
            (output_proj, got_o, flip_o),
            (inner_proj,) + sh.pieces(*fetched[:2]),
            (outer_proj,) + sh.pieces(*fetched[2:]),
        )
        FF = inner_proj.shape[1]
        mixed_got = sh.trade(mixed_low)
        normed_low, activ_low, pre, outcome, d_res2, d_outer, n1, rstd1, vec_a = ffn_fwd(
            place, hidden, mixed_f, out_grad[0], vecs, *parts, FF
        )
        ffn, d_res1, d_attn, d_mixed, vec_b = ffn_bwd(
            place, C, pre, activ_low, normed_low, d_outer, sh.trade(d_outer), d_res2, n1, rstd1,
            mixed_got, hidden_got, vecs, *parts,
        )
    else:
        attn_out = nn(mixed_low, o_full) + vecs[6]
        normed, first_pull = jax.vjp(layer_norm, hidden.astype(F32) + attn_out, vecs[7], vecs[8])
        normed_low = normed.astype(BF)
        inner_pre = nn(normed_low, inner_full) + vecs[12:].reshape(-1, sh.parts, dn).transpose(1, 0, 2).reshape(-1)
        activated, gelu_pull = jax.vjp(partial(jax.nn.gelu, approximate=True), inner_pre)
        activ_low = activated.astype(BF)
        outer_out = nn(activ_low, outer_full) + vecs[9]
        outcome, second_pull = jax.vjp(layer_norm, normed + outer_out, vecs[10], vecs[11])
        d_res2, grad_ffn_gain, grad_ffn_shift = second_pull(cotangent)
        d_outer = d_res2.astype(BF)
        grad_outer_bias = jnp.sum(d_outer.astype(F32), axis=0)
        d_inner = gelu_pull(nt(d_outer, outer_full))[0].astype(BF)
        grad_inner_bias = jnp.sum(d_inner.astype(F32), axis=0)
        d_normed = d_res2 + nt(d_inner, inner_full)
        d_res1, grad_attn_gain, grad_attn_shift = first_pull(d_normed)
        d_attn = d_res1.astype(BF)
        grad_output_bias = jnp.sum(d_attn.astype(F32), axis=0)
        d_mixed = nt(d_attn, o_full).astype(BF)
        vec_a = jnp.stack(
            [grad_ffn_gain, grad_ffn_shift, grad_outer_bias] + [jnp.zeros((D,), F32)] * 5
        )
        ib = grad_inner_bias.reshape(sh.parts, -1, dn).transpose(1, 0, 2).reshape(-1, D)
        vec_b = jnp.concatenate(
            [
                jnp.stack(
                    [
                        grad_attn_gain, grad_attn_shift, grad_output_bias,
                        jnp.sum(d_mixed.astype(F32), axis=0),
                    ]
                ),
                ib,
            ],
            axis=0,
        )
    if sh.pair:
        d_attn_got = sh.trade(d_attn)
    dq, att_vec, dkv, d_table = att_bwd(
        q_lin, vecs, kind_q, d_mixed, mixed_f, probs, key_values, table, kaug
    )
    if sh.pair:
        dq_got = sh.trade(dq)
        ffn = lax.psum_scatter(ffn, "ctx", scatter_dimension=0, tiled=False)

        whole = key_grads(dkv, d_table, x_win, sinus, (att_vec, vec_a, vec_b))
        whole = sh.halve(whole, 0, 0)
        keep, send = sh.order(whole[:, :dn], whole[:, dn:], sh.f)
        got_x = sh.trade(send)
        dkv, _ = lax.optimization_barrier((dkv, send))
        go, gq = (
            tn(
                jnp.concatenate([b, b_got], axis=0),
                jnp.concatenate([sh.own(a, 1), sh.own(a_got, 1)], axis=0),
            )
            for a, a_got, b, b_got in (
                (mixed_low, mixed_got, d_attn, d_attn_got), (hidden, hidden_got, dq, dq_got)
            )
        )
        mine = sh.halve_cols(go, gq)

        d_hid = hidden_grads(
            place, dkv.reshape(2 * D, W), key_proj, other_k, value_proj, other_v, C, R
        )
        got_x, d_hid, mine, ffn = lax.optimization_barrier((got_x, d_hid, mine, ffn))
        ffn = lax.all_gather(ffn, "ctx", axis=0, tiled=False)
        whole = (keep.astype(F32) + got_x.astype(F32)).astype(BF)
        grads = jnp.concatenate([whole, mine], axis=0)
        grads = grads.reshape((2,) * (sh.bits - 1) + (-1, dn))
        d_hid = sh.spread(d_hid)
        for k in range(1, sh.bits):
            grads = sh.halve(grads, k, grads.ndim - 3)
            d_hid = sh.halve(d_hid, k - 1, d_hid.ndim - 3)
            grads, d_hid = lax.optimization_barrier((grads, d_hid))
        n = grads.shape[0]
        cut = (n // 2 + 15) // 16 * 16
        one, two = grads[:cut], grads[cut:]
        highs = list(reversed(range(2, sh.bits)))
        for i, (k, other) in enumerate(zip(highs + [1], [1] + highs)):
            one = sh.double(one, k, one.ndim - 2)
            two = sh.double(two, other, 0 if i == 0 else i - 1)
            if i == 0:
                d_hid = sh.halve(d_hid, sh.bits - 1, d_hid.ndim - 3)
            if i == 0:
                one, two, d_hid, ffn = lax.optimization_barrier((one, two, d_hid, ffn))
            if i == 1:
                gi, gu = ffn_final(ffn, inner_bias.shape[0] * 2, D)
                one, two, gi, gu, d_hid = lax.optimization_barrier((one, two, gi, gu, d_hid))
                input_grad = input_grads(place, d_res1, dq, query_proj, other_q, d_hid)
        one, two, input_grad = lax.optimization_barrier((one, two, input_grad))
        one, two = one.reshape(-1, dn), two.reshape(-1, dn)
        gk, gv, gp, go, gq, s = grad_final(
            place, one, two, sh.flip(one, 0), sh.flip(two, 0), D, C // 2
        )
        s = unpack_rows(s)
    else:
        dkv = dkv.reshape(2 * D, W)
        gkv, gp = (
            lax.dot_general(a, b, (((0,), (1,)), ((), ())), preferred_element_type=F32)
            for a, b in ((x_win, dkv), (sinus, d_table))
        )
        d_hid = tn(dkv[:D], jnp.transpose(k_full)) + tn(dkv[D:], jnp.transpose(v_full))
        d_hid = d_hid.astype(BF)
        below = (C - 1 - R) * T
        d_hid = jnp.pad(d_hid, ((below, (C - 1) * T + L - below - W), (0, 0)))
        d_hid = lax.dynamic_slice_in_dim(d_hid, (C - 1 - ctx) * T, L, 0)
        d_hid = lax.psum_scatter(d_hid, "ctx", scatter_dimension=0, tiled=True)
        input_grad = d_res1 + nt(dq, q_full) + d_hid.astype(F32)
        s = jnp.concatenate([att_vec, vec_a, vec_b], axis=0)
        sums = [
            gkv, gp, tn(mixed_low, d_attn), tn(hidden, dq), tn(normed_low, d_inner),
            tn(activ_low, d_outer), jnp.transpose(s),
        ]
        sums = [
            lax.psum_scatter(a.astype(BF), "fsdp", scatter_dimension=0, tiled=True) for a in sums
        ]
        gkv, gp, go, gq, gi, gu, s = (a.astype(F32) for a in lax.psum(sums, "ctx"))
        gk, gv, s = gkv[:, :D], gkv[:, D:], jnp.transpose(s)
        s = [s[i] for i in (19, 0, 1, 2, 18, 16, 17, 10, 8, 9)] + [s[3:5], s[20:24].reshape(-1)]
    return (
        outcome.astype(BF)[None],
        input_grad[None],
        gq,
        gk,
        gv,
        s[0],
        s[1],
        s[2],
        s[3],
        s[10],
        gp,
        go,
        s[4],
        s[5],
        s[6],
        gi,
        s[11],
        gu,
        s[7],
        s[8],
        s[9],
    )


def solution(mesh):
    in_specs = (
        P("fsdp", "ctx", None),
        P("fsdp", "ctx"),
        P("fsdp", "ctx"),
        P("fsdp", "ctx", None),
        P("fsdp", None),
        P("fsdp", None),
        P("fsdp", None),
        P("fsdp"),
        P("fsdp"),
        P("fsdp"),
        P("fsdp"),
        P(None, "fsdp"),
        P("fsdp", None),
        P("fsdp", None),
        P("fsdp"),
        P("fsdp"),
        P("fsdp"),
        P("fsdp", None),
        P("fsdp"),
        P("fsdp", None),
        P("fsdp"),
        P("fsdp"),
        P("fsdp"),
    )
    out_specs = (
        P("fsdp", "ctx", None),
        P("fsdp", "ctx", None),
        P("fsdp", None),
        P("fsdp", None),
        P("fsdp", None),
        P("fsdp"),
        P("fsdp"),
        P("fsdp"),
        P("fsdp"),
        P(None, "fsdp"),
        P("fsdp", None),
        P("fsdp", None),
        P("fsdp"),
        P("fsdp"),
        P("fsdp"),
        P("fsdp", None),
        P("fsdp"),
        P("fsdp", None),
        P("fsdp"),
        P("fsdp"),
        P("fsdp"),
    )
    return jax.shard_map(
        per_device, mesh=mesh, in_specs=in_specs, out_specs=out_specs, check_vma=False
    )
```

```python
from functools import partial
import jax
import jax.numpy as jnp
from jax import lax
from jax.experimental import pallas as pl
from jax.experimental.pallas import tpu as pltpu
from jax.sharding import PartitionSpec as P

H = 12
DH = 64
EPS = 1e-06
BIG = 1e30
BF = jnp.bfloat16
F32 = jnp.float32


def nt(a, b):
    return lax.dot_general(a, b, (((1,), (1,)), ((), ())), preferred_element_type=F32)


def nn(a, b):
    return lax.dot_general(a, b, (((1,), (0,)), ((), ())), preferred_element_type=F32)


def tn(a, b):
    return lax.dot_general(a, b, (((0,), (0,)), ((), ())), preferred_element_type=F32)


def att_fwd_kernel(q_ref, v_rows, pen_ref, kind_ref, k_ref, v_ref, t_ref, ka_ref, o_ref, p_ref):
    T = q_ref.shape[0]
    W = k_ref.shape[0]
    blocks = W // T
    c = DH**-0.5
    q = q_ref[...]
    qc = ((q + v_rows[1:2, :]) * c).astype(BF)
    qp = ((q + v_rows[2:3, :]) * c).astype(BF)
    qt = (q + v_rows[3:4, :]) * c
    t0, t1 = qt * v_rows[4:5, :], qt * v_rows[5:6, :]
    lane = lax.broadcasted_iota(jnp.int32, (T, 128), 1)
    row = lax.broadcasted_iota(jnp.int32, (T, 128), 0)
    same = kind_ref[...] > 0.5
    pen = pen_ref[...]
    zero = jnp.zeros_like(qc)
    heads, where_q = [], []
    for h in range(2):
        mine = (lane < DH) if h == 0 else (lane >= DH)
        a0 = jnp.broadcast_to(jnp.sum(jnp.where(mine, t0, 0.0), axis=1, keepdims=True), (T, 128))
        a1 = jnp.broadcast_to(jnp.sum(jnp.where(mine, t1, 0.0), axis=1, keepdims=True), (T, 128))
        one, two = jnp.where(same, a1, a0), jnp.where(same, a0, a1)
        one_high, two_high = one.astype(BF).astype(F32), two.astype(BF).astype(F32)
        extra = jnp.where(lane == 4, two_high, jnp.where(lane == 5, two - two_high, pen))
        extra = jnp.where(lane == 0, one_high, jnp.where(lane == 1, one - one_high, extra))
        heads.append(jnp.concatenate([jnp.where(mine, qc, zero), extra.astype(BF)], axis=1))
        where_q.append(jnp.where(mine, qp, zero))
    s = nt(jnp.concatenate(heads, axis=0), jnp.concatenate([k_ref[...], ka_ref[...]], axis=1))
    w = nt(jnp.concatenate(where_q, axis=0), t_ref[...])
    probs = []
    for h in range(2):
        turned = [
            pltpu.roll(w[T * h : T * (h + 1), 128 * b : 128 * b + 128], 1, 1, stride=1, stride_axis=0)
            for b in range(blocks + 1)
        ]
        tiles = [
            s[T * h : T * (h + 1), 128 * b : 128 * b + 128]
            + jnp.where(lane <= row, turned[b], turned[b + 1])
            for b in range(blocks)
        ]
        top = tiles[0]
        for b in range(1, blocks):
            top = jnp.maximum(top, tiles[b])
        top = jnp.max(top, axis=1, keepdims=True)
        tiles = [jnp.exp(a - top) for a in tiles]
        total = tiles[0]
        for b in range(1, blocks):
            total = total + tiles[b]
        inverse = 1.0 / jnp.sum(total, axis=1, keepdims=True)
        p = jnp.concatenate([(a * inverse).astype(BF) for a in tiles], axis=1)
        p_ref[h] = p
        probs.append(p)
    out = nn(jnp.concatenate(probs, axis=0), v_ref[...])
    o_ref[...] = jnp.where(lane < DH, out[:T], out[T:])


def att_bwd_kernel(
    q_ref, v_rows, kind_ref, dm_ref, o_ref, p_ref, k_ref, v_ref, t_ref, ka_ref,
    dq_ref, vec_ref, dkv_ref, dt_ref,
):
    T = q_ref.shape[0]
    W = k_ref.shape[0]
    blocks = W // T
    c = DH**-0.5
    q = q_ref[...]
    qc = ((q + v_rows[1:2, :]) * c).astype(BF)
    qp = ((q + v_rows[2:3, :]) * c).astype(BF)
    qt = (q + v_rows[3:4, :]) * c
    e0, e1 = v_rows[4:5, :], v_rows[5:6, :]
    lane = lax.broadcasted_iota(jnp.int32, (T, 128), 1)
    row = lax.broadcasted_iota(jnp.int32, (T, 128), 0)
    same = kind_ref[...] > 0.5
    flip = jnp.where(lane + row == T - 1, 1.0, 0.0).astype(BF)
    qpr = nn(flip, qp).astype(BF)
    dm = dm_ref[...]
    dmo = dm.astype(F32) * o_ref[...]
    zero = jnp.zeros_like(dm)
    stack = lambda parts: jnp.concatenate(parts, axis=0)
    mine = [lane < DH, lane >= DH]
    pick = lambda a: stack([jnp.where(m, a, zero) for m in mine])
    dms = pick(dm)
    delta = jnp.sum(
        stack([jnp.where(m, dmo, 0.0) for m in mine]), axis=1, keepdims=True
    )
    dp = nt(dms, v_ref[...])
    p = stack([p_ref[0], p_ref[1]])
    ds = (p.astype(F32) * (dp - delta)).astype(BF)
    dc = nn(ds, jnp.concatenate([k_ref[...], ka_ref[...]], axis=1))
    wide = []
    for h in range(2):
        back = nn(flip, ds[T * h : T * (h + 1)])
        turned = [
            pltpu.roll(back[:, 128 * b : 128 * b + 128], 0, 1, stride=1, stride_axis=0)
            for b in range(blocks)
        ]
        edge = jnp.zeros((T, 128), F32)
        tiles = [
            jnp.where(lane >= row, a, b).astype(BF)
            for a, b in zip(turned + [edge], [edge] + turned)
        ]
        wide.append(jnp.concatenate(tiles, axis=1))
    wide = stack(wide)
    dqp = nn(wide, t_ref[...])
    dkv_ref[0] = tn(pick(qc), ds).astype(BF)
    dkv_ref[1] = tn(dms, p).astype(BF)
    dt_ref[...] = tn(pick(qpr), wide).astype(BF)
    both = lambda a: jnp.where(mine[0], a[:T], a[T:])
    dc_low = both(dc[:, :128]).astype(BF).astype(F32)
    dp_low = nn(flip, both(dqp).astype(BF))
    one = both(jnp.broadcast_to(dc[:, 128:129], (2 * T, 128)))
    two = both(jnp.broadcast_to(dc[:, 132:133], (2 * T, 128)))
    same_sum, other_sum = jnp.where(same, one, two), jnp.where(same, two, one)
    dt = other_sum * e0 + same_sum * e1
    dq_ref[...] = (c * (dc_low + dp_low + dt)).astype(BF)
    total = lambda a: jnp.sum(a, axis=0, keepdims=True)
    rows = [c * total(dc_low), c * total(dp_low), c * total(dt), total(other_sum * qt), total(same_sum * qt)]
    vec_ref[...] = jnp.concatenate(rows + [jnp.zeros((3, 128), F32)], axis=0)


def att_fwd(q, rows, pen, kind, kv, t, ka):
    T, D = q.shape
    W = kv.shape[0]
    keys, values = (pl.BlockSpec((W, 128), lambda i, n=n: (0, i + n * D // 128)) for n in range(2))
    heads = D // DH
    col = lambda n: pl.BlockSpec((n, 128), lambda i: (0, i))
    fixed = lambda n: pl.BlockSpec((n, 128), lambda i: (0, 0))
    return pl.pallas_call(
        att_fwd_kernel,
        grid=(D // 128,),
        in_specs=[col(T), col(16), fixed(T), fixed(T), keys, values, col(W + T), fixed(W)],
        out_specs=[col(T), pl.BlockSpec((2, T, W), lambda i: (i, 0, 0))],
        out_shape=[
            jax.ShapeDtypeStruct((T, D), F32),
            jax.ShapeDtypeStruct((heads, T, W), BF),
        ],
        compiler_params=pltpu.CompilerParams(vmem_limit_bytes=60 * 2**20),
        cost_estimate=pl.CostEstimate(
            flops=2 * heads * T * W * 2048,
            bytes_accessed=2 * (3 * W * D + heads * T * W),
            transcendentals=heads * T * W,
        ),
        name="att_fwd",
    )(q, rows, pen, kind, kv, kv, t, ka)


def att_bwd(q, rows, kind, dm, o, p, kv, t, ka):
    T, D = q.shape
    W = kv.shape[0]
    keys, values = (pl.BlockSpec((W, 128), lambda i, n=n: (0, i + n * D // 128)) for n in range(2))
    heads = D // DH
    col = lambda n: pl.BlockSpec((n, 128), lambda i: (0, i))
    fixed = lambda n: pl.BlockSpec((n, 128), lambda i: (0, 0))
    return pl.pallas_call(
        att_bwd_kernel,
        grid=(D // 128,),
        in_specs=[
            col(T), col(16), fixed(T), col(T), col(T), pl.BlockSpec((2, T, W), lambda i: (i, 0, 0)),
            keys, values, col(W + T), fixed(W),
        ],
        out_specs=[
            col(T), col(8), pl.BlockSpec((2, 128, W), lambda i: (0, i, 0)),
            pl.BlockSpec((128, W + T), lambda i: (i, 0)),
        ],
        out_shape=[
            jax.ShapeDtypeStruct((T, D), BF),
            jax.ShapeDtypeStruct((8, D), F32),
            jax.ShapeDtypeStruct((2, D, W), BF),
            jax.ShapeDtypeStruct((D, W + T), BF),
        ],
        compiler_params=pltpu.CompilerParams(vmem_limit_bytes=60 * 2**20),
        cost_estimate=pl.CostEstimate(
            flops=2**20, bytes_accessed=2**20, transcendentals=0
        ),
        name="att_bwd",
    )(q, rows, kind, dm, o, p, kv, kv, t, ka)


def pack_rows(vectors, dn):
    counts = [v.size // dn for v in vectors]

    def kernel(*refs):
        out = refs[-1]
        at = 0
        for ref, n in zip(refs, counts):
            for j in range(n):
                if len(ref.shape) == 1:
                    out[at, :] = ref[pl.ds(j * dn, dn)].astype(F32)
                else:
                    out[at, :] = ref[j, :].astype(F32)
                at += 1

    return pl.pallas_call(
        kernel,
        out_shape=jax.ShapeDtypeStruct((sum(counts), dn), F32),
        name="pack_rows",
    )(*vectors)


def ffn_final(blocks, FF, D):
    count, _, dn = blocks.shape
    steps = FF // D
    per = count // steps
    ri, ru = FF // count, FF // 2 // count

    def kernel(b_ref, i_ref, u_ref):
        gi = jnp.concatenate([b_ref[k, :ri] for k in range(per)], axis=0)
        i_ref[...] = jnp.transpose(gi.astype(F32))
        for k in range(per):
            u_ref[ru * k : ru * (k + 1), :dn] = b_ref[k, ri : ri + ru].astype(F32)
            u_ref[ru * k : ru * (k + 1), dn:] = b_ref[k, ri + ru :].astype(F32)

    return pl.pallas_call(
        kernel,
        grid=(steps,),
        in_specs=[pl.BlockSpec((per, ri + 2 * ru, dn), lambda i: (i, 0, 0))],
        out_specs=[
            pl.BlockSpec((dn, D), lambda i: (0, i)), pl.BlockSpec((FF // 2 // steps, D), lambda i: (i, 0))
        ],
        out_shape=[
            jax.ShapeDtypeStruct((dn, FF), F32), jax.ShapeDtypeStruct((FF // 2, D), F32)
        ],
        cost_estimate=pl.CostEstimate(flops=2**33, bytes_accessed=8 * D * FF, transcendentals=0),
        name="ffn_final",
    )(blocks)


def split_cols(a, f, odd):
    h = a.shape[1] // 2
    q = h // 2
    own = jnp.where(f == 0, a[:, :h], a[:, h:])
    other = jnp.where(f == 0, a[:, h:], a[:, :h])
    swapped = jnp.concatenate([other[:, q:], other[:, :q]], axis=1)
    return jnp.concatenate([own, jnp.where(odd, swapped, other)], axis=1)


def merge_cols(a, f, odd):
    h = a.shape[1] // 2
    q = h // 2
    own, other = a[:, :h], a[:, h:]
    swapped = jnp.concatenate([other[:, q:], other[:, :q]], axis=1)
    other = jnp.where(odd, swapped, other)
    return jnp.where(
        f == 0, jnp.concatenate([own, other], axis=1), jnp.concatenate([other, own], axis=1)
    )


def swap_quarters(a, y, odd):
    h = a.shape[1] // 2
    q = h // 2
    a = jnp.where(y, jnp.concatenate([a[:, h:], a[:, :h]], axis=1), a)
    pairs = jnp.concatenate([a[:, q:h], a[:, :q], a[:, h + q :], a[:, h : h + q]], axis=1)
    return jnp.where(odd, pairs, a)


def middle_swap(a):
    q = a.shape[1] // 4
    return jnp.concatenate([a[:, :q], a[:, 2 * q : 3 * q], a[:, q : 2 * q], a[:, 3 * q :]], axis=1)


def split_quarters(a, f, y, odd):
    h = a.shape[1] // 2
    own = jnp.where(f == 0, a[:, :h], a[:, h:])
    other = jnp.where(f == 0, a[:, h:], a[:, :h])
    return own, middle_swap(swap_quarters(other, y, odd))


def merge_quarters(a, f, y, odd):
    h = a.shape[1] // 2
    own, other = a[:, :h], swap_quarters(middle_swap(a[:, h:]), y, odd)
    return jnp.where(
        f == 0, jnp.concatenate([own, other], axis=1), jnp.concatenate([other, own], axis=1)
    )


def norm_stats(res):
    center = res - jnp.mean(res, axis=1, keepdims=True)
    rstd = lax.rsqrt(jnp.mean(center * center, axis=1, keepdims=True) + EPS)
    return center * rstd, rstd


def norm_back(g, gain, n, rstd):
    gg = g * gain
    return (gg - jnp.mean(gg, axis=1, keepdims=True) - n * jnp.mean(gg * n, axis=1, keepdims=True)) * rstd


def row_sum(a):
    return jnp.sum(a, axis=0, keepdims=True)


GELU_A = 0.7978845608028654
GELU_B = 0.044715


def ffn_specs(T, D, FF):
    steps = FF // D
    half = steps // 2
    c = FF // steps
    q = D // 8

    def chunk_at(j, s):
        other = half * (1 - s[0]) + (s[2] ^ jnp.maximum(j - half, 0))
        return jnp.where(j < half, half * s[0] + j, other)

    col = lambda j, s: (0, chunk_at(j, s))
    whole = lambda *shape: pl.BlockSpec(shape, lambda j, s: (0,) * len(shape))
    inner = [pl.BlockSpec((4 * q, c), col)] + [pl.BlockSpec((q, c), col)] * 4
    outer = [pl.BlockSpec((c, D), lambda j, s: (jnp.minimum(j, half - 1), 0))]
    outer += [whole(c // 2, D)] * 4
    proj = [whole(4 * q, D), whole(2 * q, D), whole(2 * q, D)]
    return steps, half, c, chunk_at, col, whole, inner, outer, proj


def outer_chunk(j, half, odd, refs):
    last = j > half
    a = jnp.where(last, refs[2][...], refs[1][...])
    b = jnp.where(last, refs[4][...], refs[3][...])
    pair = jnp.concatenate([jnp.where(odd, b, a), jnp.where(odd, a, b)], axis=0)
    return jnp.where(j < half, refs[0][...], pair)


def rows_of(refs):
    return jnp.concatenate([r[...] for r in refs], axis=0)


def inner_bias_chunk(b, half, vec_ref, D):
    rows = [vec_ref[pl.ds(12 + 2 * (b % half) + n, 1), :] for n in range(2)]
    parts = [jnp.where(b < half, r[:, : D // 2], r[:, D // 2 :]) for r in rows]
    return jnp.concatenate(parts, axis=1)


def gelu_tanh(u):
    return jnp.tanh(GELU_A * (u + GELU_B * u * u * u))


def first_norm(x, mixed, vec_ref, w, f, odd):
    attn = nn(split_cols(mixed, f, odd).astype(BF), w) + vec_ref[6:7, :]
    n1, rstd = norm_stats(x.astype(F32) + attn)
    return n1, rstd, n1 * vec_ref[7:8, :] + vec_ref[8:9, :]


def ffn_fwd(place, x, mixed, cot, vecs, o_parts, i_parts, u_parts, FF):
    T, D = x.shape
    steps, half, c, chunk_at, col, whole, inner, outer, proj = ffn_specs(T, D, FF)

    def kernel(s_ref, x_ref, m_ref, g_ref, v_ref, *refs):
        o_refs, i_refs, u_refs = refs[:3], refs[3:8], refs[8:13]
        nl_ref, act_ref, pre_ref, res_ref, dr_ref, do_ref, n1_ref, rs_ref, gv_ref = refs[13:22]
        np_ref, acc_ref, nf_ref = refs[22:]
        j = pl.program_id(0)
        f, odd, y = s_ref[0], s_ref[1] == 1, s_ref[2] == 1

        @pl.when(j == 0)
        def _():
            n1, rstd, normed = first_norm(x_ref[...], m_ref[...], v_ref, rows_of(o_refs), f, odd)
            n1_ref[...] = n1
            rs_ref[...] = jnp.broadcast_to(rstd, (T, 128))
            nf_ref[...] = normed
            nl_ref[...] = normed.astype(BF)
            np_ref[...] = jnp.concatenate(split_quarters(normed, f, y, odd), axis=1).astype(BF)
            acc_ref[...] = jnp.zeros_like(acc_ref)

        bias = inner_bias_chunk(chunk_at(j, s_ref), half, v_ref, D)
        pre = nn(np_ref[...], rows_of(i_refs)) + bias
        pre_ref[...] = pre
        act = (0.5 * pre * (1.0 + gelu_tanh(pre))).astype(BF)
        act_ref[...] = act
        acc_ref[...] += nn(act, outer_chunk(j, half, odd, u_refs))

        @pl.when(j == steps - 1)
        def _():
            n2, rstd = norm_stats(nf_ref[...] + (acc_ref[...] + v_ref[9:10, :]))
            g = g_ref[...].astype(F32)
            res_ref[...] = (n2 * v_ref[10:11, :] + v_ref[11:12, :]).astype(BF)
            d = norm_back(g, v_ref[10:11, :], n2, rstd)
            dr_ref[...] = d
            do = d.astype(BF)
            do_ref[...] = do
            gv_ref[0:1, :] = row_sum(g * n2)
            gv_ref[1:2, :] = row_sum(g)
            gv_ref[2:3, :] = row_sum(do.astype(F32))
            gv_ref[3:8, :] = jnp.zeros((5, D), F32)

    f32 = lambda *shape: jax.ShapeDtypeStruct(shape, F32)
    low = lambda *shape: jax.ShapeDtypeStruct(shape, BF)
    tok = whole(T, D)
    chunk = pl.BlockSpec((T, c), col)
    return pl.pallas_call(
        kernel,
        grid_spec=pltpu.PrefetchScalarGridSpec(
            num_scalar_prefetch=1,
            grid=(steps,),
            in_specs=[tok, tok, tok, whole(16, D)] + proj + inner + outer,
            out_specs=[tok, chunk, chunk, tok, tok, tok, tok, whole(T, 128), whole(8, D)],
            scratch_shapes=[
                pltpu.VMEM((T, D), BF), pltpu.VMEM((T, D), F32), pltpu.VMEM((T, D), F32)
            ],
        ),
        out_shape=[
            low(T, D), low(T, FF), f32(T, FF), low(T, D), f32(T, D), low(T, D), f32(T, D),
            f32(T, 128), f32(8, D),
        ],
        compiler_params=pltpu.CompilerParams(vmem_limit_bytes=60 * 2**20),
        cost_estimate=pl.CostEstimate(
            flops=4 * T * D * FF, bytes_accessed=4 * D * FF, transcendentals=T * FF
        ),
        name="ffn_fwd",
    )(place, x, mixed, cot, vecs, *o_parts, *i_parts, *u_parts)


def ffn_bwd(
    place, count, pre, act, normed, d_outer, d_outer_got, d_res2, n1, rstd1, mixed_got, x_got,
    vecs, o_parts, i_parts, u_parts,
):
    T, FF = pre.shape
    D = d_outer.shape[1]
    dn = D // 2
    steps, half, c, chunk_at, col, whole, inner, outer, proj = ffn_specs(T, D, FF)
    ri, ru = FF // count, FF // 2 // count

    def kernel(s_ref, pre_ref, act_ref, nl_ref, do_ref, dog_ref, dr_ref, n1_ref, rs_ref, mg_ref, xg_ref, v_ref, *refs):
        o_refs, i_refs, u_refs = refs[:3], refs[3:8], refs[8:13]
        pay_ref, d1_ref, da_ref, dm_ref, gv_ref = refs[13:18]
        acc_ref, ib_ref, np_ref, nf_ref, do_both = refs[18:]
        j = pl.program_id(0)
        f, odd, y = s_ref[0], s_ref[1] == 1, s_ref[2] == 1

        @pl.when(j == 0)
        def _():
            acc_ref[...] = jnp.zeros_like(acc_ref)
            theirs = first_norm(xg_ref[...], mg_ref[...], v_ref, rows_of(o_refs), f, odd)[2]
            own, other = split_quarters(theirs, f, y, odd)
            np_ref[...] = jnp.concatenate([own, other], axis=1).astype(BF)
            nl = nl_ref[...]
            nf_ref[:T] = jnp.where(f == 0, nl[:, :dn], nl[:, dn:])
            nf_ref[T:] = own.astype(BF)
            do_both[:T] = do_ref[...]
            do_both[T:] = dog_ref[...]

        b = chunk_at(j, s_ref)
        w = rows_of(i_refs)
        pre_got = nn(np_ref[...], w) + inner_bias_chunk(b, half, v_ref, D)
        u = jnp.concatenate([pre_ref[...], pre_got], axis=0)
        t = gelu_tanh(u)
        slope = 0.5 * (1.0 + t) + 0.5 * u * (1.0 - t * t) * (GELU_A * (1.0 + 3.0 * GELU_B * u * u))
        di = (nt(do_both[...], outer_chunk(j, half, odd, u_refs)) * slope).astype(BF)
        ib_ref[pl.ds(b, 1), :] = row_sum(di[:T].astype(F32))
        acc_ref[...] += nt(di[:T], w)
        gi = tn(di, nf_ref[...]).astype(BF)
        for k in range(c // ri):
            pay_ref[b * (c // ri) + k, :ri] = gi[ri * k : ri * (k + 1)]

        @pl.when(j < half)
        def _():
            act_got = (0.5 * u[T:] * (1.0 + t[T:])).astype(BF)
            gu = tn(jnp.concatenate([act_ref[...], act_got], axis=0), do_both[...]).astype(BF)
            for k in range(c // ru):
                pay_ref[j * (c // ru) + k, ri : ri + ru] = gu[ru * k : ru * (k + 1), :dn]
                pay_ref[j * (c // ru) + k, ri + ru :] = gu[ru * k : ru * (k + 1), dn:]

        @pl.when(j == steps - 1)
        def _():
            d_normed = dr_ref[...] + merge_quarters(acc_ref[...], f, y, odd)
            n1 = n1_ref[...]
            d1 = norm_back(d_normed, v_ref[7:8, :], n1, rs_ref[:, 0:1])
            d1_ref[...] = d1
            da = d1.astype(BF)
            da_ref[...] = da
            dm = merge_cols(nt(da, rows_of(o_refs)), f, odd)
            dm_ref[...] = dm.astype(BF)
            gv_ref[0:1, :] = row_sum(d_normed * n1)
            gv_ref[1:2, :] = row_sum(d_normed)
            gv_ref[2:3, :] = row_sum(da.astype(F32))
            gv_ref[3:4, :] = row_sum(dm.astype(BF).astype(F32))
            for n in range(2 * half):
                at = slice(0, dn) if n % 2 == 0 else slice(dn, D)
                gv_ref[4 + n : 5 + n, :dn] = ib_ref[n // 2 : n // 2 + 1, at]
                gv_ref[4 + n : 5 + n, dn:] = ib_ref[half + n // 2 : half + n // 2 + 1, at]

    f32 = lambda *shape: jax.ShapeDtypeStruct(shape, F32)
    low = lambda *shape: jax.ShapeDtypeStruct(shape, BF)
    tok = whole(T, D)
    chunk = pl.BlockSpec((T, c), col)
    return pl.pallas_call(
        kernel,
        grid_spec=pltpu.PrefetchScalarGridSpec(
            num_scalar_prefetch=1,
            grid=(steps,),
            in_specs=[chunk, chunk] + [tok] * 5 + [whole(T, 128), tok, tok, whole(16, D)]
            + proj + inner + outer,
            out_specs=[whole(count, ri + 2 * ru, dn), tok, tok, tok, whole(8, D)],
            scratch_shapes=[
                pltpu.VMEM((T, D), F32), pltpu.VMEM((steps, c), F32), pltpu.VMEM((T, D), BF),
                pltpu.VMEM((2 * T, dn), BF), pltpu.VMEM((2 * T, D), BF),
            ],
        ),
        out_shape=[low(count, ri + 2 * ru, dn), f32(T, D), low(T, D), low(T, D), f32(8, D)],
        compiler_params=pltpu.CompilerParams(vmem_limit_bytes=60 * 2**20),
        cost_estimate=pl.CostEstimate(
            flops=14 * T * D * FF, bytes_accessed=6 * D * FF, transcendentals=2 * T * FF
        ),
        name="ffn_bwd",
    )(
        place, pre, act, normed, d_outer, d_outer_got, d_res2, n1, rstd1, mixed_got, x_got, vecs,
        *o_parts, *i_parts, *u_parts,
    )


def key_grads(dkv, x_win):
    _, D, W = dkv.shape
    h = D // 2

    def kernel(kv_ref, x_ref, out_ref):
        out_ref[0] = nn(kv_ref[0], x_ref[...]).astype(BF)

    return pl.pallas_call(
        kernel,
        grid=(4,),
        in_specs=[
            pl.BlockSpec((1, h, W), lambda i: (i // 2, i % 2, 0)),
            pl.BlockSpec((W, D), lambda i: (0, 0)),
        ],
        out_specs=pl.BlockSpec((1, h, D), lambda i: (i // 2, i % 2, 0)),
        out_shape=jax.ShapeDtypeStruct((2, D, D), BF),
        compiler_params=pltpu.CompilerParams(vmem_limit_bytes=60 * 2**20),
        cost_estimate=pl.CostEstimate(
            flops=4 * D * D * W, bytes_accessed=6 * D * W, transcendentals=0
        ),
        name="key_grads",
    )(dkv, x_win)


def position_grads(d_table, sinus, vectors):
    D, WT = d_table.shape
    h = D // 2

    def kernel(t_ref, s_ref, *refs):
        v_refs, out_ref = refs[:-1], refs[-1]
        out_ref[0, :h, :] = nn(t_ref[...], s_ref[...]).astype(BF)
        small = jnp.concatenate([r[...] for r in v_refs], axis=0)
        small = jnp.concatenate([small, jnp.zeros((64 - small.shape[0], D), F32)], axis=0)
        out_ref[0, h:, :] = jnp.where(pl.program_id(0) == 0, small, 0.0).astype(BF)

    whole = lambda *shape: pl.BlockSpec(shape, lambda i: (0,) * len(shape))
    return pl.pallas_call(
        kernel,
        grid=(2,),
        in_specs=[pl.BlockSpec((h, WT), lambda i: (i, 0)), whole(WT, D)]
        + [whole(8, D)] * len(vectors),
        out_specs=pl.BlockSpec((1, h + 64, D), lambda i: (i, 0, 0)),
        out_shape=jax.ShapeDtypeStruct((2, h + 64, D), BF),
        compiler_params=pltpu.CompilerParams(vmem_limit_bytes=60 * 2**20),
        cost_estimate=pl.CostEstimate(
            flops=2 * D * D * WT, bytes_accessed=4 * D * WT, transcendentals=0
        ),
        name="position_grads",
    )(d_table, sinus, *vectors)


def hidden_grads(place, dkv, k_own, k_other, v_own, v_other, count, reach):
    D2, W = dkv.shape
    D = D2 // 2
    h = D // 2
    T = 128
    blocks = W // T

    def kernel(s_ref, a_ref, b_ref, k0, k1, v0, v1, out_ref):
        s = pl.program_id(0)
        x = jnp.concatenate([a_ref[...], b_ref[...]], axis=1)
        for at, k, v in ((s_ref[0], k0, v0), (1 - s_ref[0], k1, v1)):
            g = nn(jnp.concatenate([k[...], v[...]], axis=1), x).astype(BF)
            for n in range(2):
                rel = 2 * s + n - s_ref[3] + reach
                ok = (rel >= 0) & (rel < blocks)
                part = g[:, T * n : T * (n + 1)]
                out_ref[n, pl.ds(pl.multiple_of(at * h, h), h), :] = jnp.where(
                    ok, part, jnp.zeros_like(part)
                )

    whole = pl.BlockSpec((h, D), lambda s, p: (0, 0))
    block = lambda n: pl.BlockSpec(
        (D2, T), lambda s, p: (0, jnp.clip(2 * s + n - p[3] + reach, 0, blocks - 1))
    )
    return pl.pallas_call(
        kernel,
        grid_spec=pltpu.PrefetchScalarGridSpec(
            num_scalar_prefetch=1,
            grid=(count // 2,),
            in_specs=[block(0), block(1), whole, whole, whole, whole],
            out_specs=pl.BlockSpec((2, D, T), lambda s, p: (s, 0, 0)),
        ),
        out_shape=jax.ShapeDtypeStruct((count, D, T), BF),
        compiler_params=pltpu.CompilerParams(vmem_limit_bytes=60 * 2**20),
        cost_estimate=pl.CostEstimate(flops=2**20, bytes_accessed=2**20, transcendentals=0),
        name="hidden_grads",
    )(place, dkv, dkv, k_own, k_other, v_own, v_other)


def input_grads(place, d_res1, dq, q_own, q_other, d_hid):
    T, D = d_res1.shape

    def kernel(s_ref, r_ref, dq_ref, q0, q1, h_ref, out_ref):
        own, other = nt(dq_ref[...], q0[...]), nt(dq_ref[...], q1[...])
        first = s_ref[0] == 0
        g = jnp.concatenate([jnp.where(first, own, other), jnp.where(first, other, own)], axis=1)
        out_ref[...] = r_ref[...] + g + jnp.transpose(h_ref[...].astype(F32))

    whole = lambda a: pl.BlockSpec(a.shape, lambda i, s: (0, 0))
    args = (d_res1, dq, q_own, q_other, d_hid)
    return pl.pallas_call(
        kernel,
        grid_spec=pltpu.PrefetchScalarGridSpec(
            num_scalar_prefetch=1,
            grid=(1,),
            in_specs=[whole(a) for a in args],
            out_specs=whole(d_res1),
        ),
        out_shape=jax.ShapeDtypeStruct((T, D), F32),
        cost_estimate=pl.CostEstimate(
            flops=2**32, bytes_accessed=2**24, transcendentals=0
        ),
        name="input_grads",
    )(place, *args)


def grad_final(place, one, two, one_got, two_got, D, blocks):
    dn = one.shape[1]
    h = D // 2
    p, q = one.shape[0] // blocks, two.shape[0] // blocks

    def kernel(s_ref, a_ref, b_ref, c_ref, d_ref, k_ref, v_ref, p_ref, o_ref, q_ref, small_ref):
        odd = s_ref[1] == 1

        def rows(x_ref, y_ref):
            x, y = x_ref[...].astype(F32), y_ref[...].astype(F32)
            parts = []
            for n in range(blocks):
                parts += [x[p * n : p * (n + 1)], y[q * n : q * (n + 1)]]
            return jnp.concatenate(parts, axis=0)

        mine, other = rows(a_ref, b_ref), rows(c_ref, d_ref)
        low, high = jnp.where(odd, other, mine), jnp.where(odd, mine, other)
        k_ref[...] = jnp.transpose(low[:D])
        v_ref[...] = jnp.transpose(high[:D])
        p_ref[...] = jnp.transpose(jnp.concatenate([low[D : D + h], high[D : D + h]], axis=0))
        small_ref[...] = low[D + h : D + h + 64]
        o_ref[...] = jnp.transpose(low[D + h + 64 :])
        q_ref[...] = jnp.transpose(high[D + h + 64 :])

    lanes = lambda n: pl.BlockSpec((n, 128), lambda i, s: (0, i))
    out = pl.BlockSpec((128, D), lambda i, s: (i, 0))
    return pl.pallas_call(
        kernel,
        grid_spec=pltpu.PrefetchScalarGridSpec(
            num_scalar_prefetch=1,
            grid=(dn // 128,),
            in_specs=[lanes(a.shape[0]) for a in (one, two, one_got, two_got)],
            out_specs=[out] * 5 + [lanes(64)],
        ),
        out_shape=[jax.ShapeDtypeStruct((dn, D), F32)] * 5 + [jax.ShapeDtypeStruct((64, dn), F32)],
        name="grad_final",
    )(place, one, two, one_got, two_got)


def unpack_rows(s):
    dn = s.shape[1]
    singles = (19, 0, 1, 2, 18, 16, 17, 10, 8, 9)

    def kernel(s_ref, *outs):
        for i, out in zip(singles, outs):
            out[...] = s_ref[i, :]
        outs[-2][...] = s_ref[3:5, :]
        for j in range(4):
            outs[-1][pl.ds(j * dn, dn)] = s_ref[20 + j, :]

    shapes = [(dn,)] * len(singles) + [(2, dn), (4 * dn,)]
    return pl.pallas_call(
        kernel,
        out_shape=[jax.ShapeDtypeStruct(a, F32) for a in shapes],
        name="unpack_rows",
    )(s)


def layer_norm(residual, gain_vec, bias_vec):
    center = residual - jnp.mean(residual, axis=-1, keepdims=True)
    spread = jnp.mean(center * center, axis=-1, keepdims=True)
    return center * lax.rsqrt(spread + EPS) * gain_vec + bias_vec


def sinus_rows(first, count, width):
    half = width // 2
    freq = jnp.power(10000.0, -jnp.arange(half, dtype=F32) / half)
    coarse = (first - 64 * jnp.arange(count // 64)).astype(F32)[:, None] * freq
    fine = jnp.arange(64).astype(F32)[:, None] * freq
    sa, ca = jnp.sin(coarse)[:, None], jnp.cos(coarse)[:, None]
    sb, cb = jnp.sin(fine)[None], jnp.cos(fine)[None]
    both = jnp.concatenate([sa * cb - ca * sb, ca * cb + sa * sb], axis=2)
    return both.astype(BF).reshape(count, width)


class Shards:
    def __init__(self):
        self.parts = lax.axis_size("fsdp")
        self.pair = self.parts == 2
        self.f = lax.axis_index("fsdp")
        self.ctx = lax.axis_index("ctx")
        self.count = lax.axis_size("ctx")
        self.bits = self.count.bit_length() - 1
        self.swap = [(0, 1), (1, 0)]

    def bit(self, k):
        return (self.ctx >> k) & 1

    def flip(self, a, k):
        return lax.ppermute(a, "ctx", [(i, i ^ (1 << k)) for i in range(self.count)])

    def trade(self, a):
        return lax.ppermute(a, "fsdp", self.swap)

    def order(self, mine, other, at):
        return jnp.where(at == 0, mine, other), jnp.where(at == 0, other, mine)

    def fetch_half(self, w):
        half = w.shape[0] // 2
        return self.trade(lax.dynamic_slice_in_dim(w, self.bit(0) * half, half, 0))

    def fetch_quarter(self, w):
        n = w.shape[0] // 4
        return self.trade(lax.dynamic_slice_in_dim(w, (self.ctx % 4) * n, n, 0))

    def pieces(self, got, y):
        return got, y, self.flip(got, 0), self.flip(y, 0)

    def full_small(self, w):
        if not self.pair:
            return lax.all_gather(w, "fsdp", axis=0, tiled=False)
        return jnp.stack(self.order(w, self.trade(w), self.f))

    def own(self, a, axis, other=False):
        n = a.shape[axis] // self.parts
        at = (1 - self.f) if other else self.f
        return lax.dynamic_slice_in_dim(a, at * n, n, axis)

    def window(self, block, planes):
        y = self.flip(block, 1)
        self.first_hop = y
        pair = jnp.stack(self.order(block, y, self.bit(1)))
        up = down = pair
        groups = [(pair[None], self.flip(pair[None], 0))]
        for _ in range(planes):
            up = lax.ppermute(up, "ctx", [(i, i + 4) for i in range(self.count - 4)])
            down = lax.ppermute(down, "ctx", [(i + 4, i) for i in range(self.count - 4)])
            both = jnp.stack([up, down])
            groups.append((both, self.flip(both, 0)))
        self.last_hop = both
        groups = [jnp.stack(self.order(a, b, self.bit(0)), axis=2) for a, b in groups]
        planes = [g[0] for g in groups[:0:-1]] + [groups[0][0]] + [g[1] for g in groups[1:]]
        return jnp.concatenate(planes, axis=0).reshape((-1,) + block.shape)

    def sides(self, a, k, axis):
        keep = lax.dynamic_index_in_dim(a, self.bit(k), axis, keepdims=False)
        return keep, lax.dynamic_index_in_dim(a, 1 - self.bit(k), axis, keepdims=False)

    def add(self, a, b):
        return (a.astype(F32) + b.astype(F32)).astype(BF)

    def halve(self, a, k, axis):
        keep, send = self.sides(a, k, axis)
        return self.add(keep, self.flip(send, k))

    def halve_cols(self, low, high):
        keep, send = self.order(low, high, self.bit(0))
        return (keep.astype(F32) + self.flip(send.astype(BF), 0).astype(F32)).astype(BF)

    def double(self, a, k, axis):
        return jnp.stack(self.order(a, self.flip(a, k), self.bit(k)), axis=axis)

    def spread(self, a):
        return a.reshape((2,) * self.bits + a.shape[1:])


def per_device(
    hidden_in,
    segment_ids,
    token_types,
    out_grad,
    query_proj,
    key_proj,
    value_proj,
    value_bias,
    content_bias,
    position_bias,
    type_bias,
    type_embed,
    position_proj,
    output_proj,
    output_bias,
    attn_gain,
    attn_shift,
    inner_proj,
    inner_bias,
    outer_proj,
    outer_bias,
    ffn_gain,
    ffn_shift,
):
    sh = Shards()
    hidden = hidden_in[0]
    cotangent = out_grad[0].astype(F32)
    T, D = hidden.shape
    C = sh.count
    ctx = sh.ctx
    L = T * C
    R = C // 2
    NB = 2 * R + 1
    W = NB * T
    dn = D // sh.parts
    r = dn // C

    lane = jnp.arange(128)[None, :]
    in_seg = (lane >= 8) & (lane < 16)
    seg_own = segment_ids[0][:, None]
    kind_own = token_types[0][:, None]
    kaug_own = jnp.where(
        lane < 4, kind_own == 1, jnp.where(lane < 8, kind_own == 0, in_seg & (lane - 8 == seg_own))
    ).astype(BF)
    pen = jnp.where(in_seg & (lane - 8 != seg_own), -BIG, 0.0).astype(F32)
    kind_q = jnp.broadcast_to(kind_own, (T, 128)).astype(F32)

    around = sh.window(jnp.concatenate([hidden, kaug_own], axis=1), R // 4)
    around = lax.dynamic_slice_in_dim(around, ctx % 4, NB, 0)
    x_win = around[:, :, :D].reshape(W, D)
    at = jnp.arange(NB) + ctx - R
    valid = ((at >= 0) & (at < C))[:, None, None]
    kaug = jnp.where(valid, around[:, :, D:], (lane[None] == 15).astype(BF)).reshape(W, 128)

    vectors = (
        value_bias, content_bias, position_bias, type_bias, type_embed, output_bias,
        attn_gain, attn_shift, outer_bias, ffn_gain, ffn_shift, inner_bias,
    )
    small = pack_rows(vectors, dn)
    small_full = sh.full_small(small)
    if sh.pair:
        odd = sh.bit(0) == 1
        got_a = sh.trade(jnp.where(odd, value_proj, position_proj))
        got_b = sh.trade(jnp.where(odd, key_proj, query_proj))
        got_o = sh.fetch_half(output_proj)
        got_a, got_b, got_o, i_sh, u_sh, small_full, _ = lax.optimization_barrier(
            (got_a, got_b, got_o, inner_proj, outer_proj, small_full, sh.last_hop)
        )
        other_p, other_v = sh.order(got_a, sh.flip(got_a, 0), sh.bit(0))
        other_q, other_k = sh.order(got_b, sh.flip(got_b, 0), sh.bit(0))
        p_full, q_full = (
            jnp.concatenate(sh.order(w, g, sh.f), axis=0)
            for w, g in ((position_proj, other_p), (query_proj, other_q))
        )
        own, other = (
            jnp.concatenate(a, axis=1) for a in ((key_proj, value_proj), (other_k, other_v))
        )
        kv_full = jnp.concatenate(sh.order(own, other, sh.f), axis=0)
        flip_o = sh.flip(got_o, 0)
        i_got, u_got = sh.fetch_quarter(i_sh), sh.fetch_quarter(u_sh)
    else:
        p_full, k_full, v_full, q_full, o_full, inner_full, outer_full = (
            lax.all_gather(w, "fsdp", axis=0, tiled=True)
            for w in (
                position_proj, key_proj, value_proj, query_proj, output_proj, inner_proj, outer_proj
            )
        )
        kv_full = jnp.concatenate([k_full, v_full], axis=1)

    vecs = jnp.concatenate([small_full[i] for i in range(sh.parts)], axis=1)

    q_lin = nn(hidden, q_full)
    if sh.pair:
        i_got, x_win = lax.optimization_barrier((i_got, x_win))
    kv_bias = jnp.concatenate([jnp.zeros((D,), F32), vecs[0]])
    key_values = (nn(x_win, kv_full) + kv_bias).astype(BF)
    sinus = lax.optimization_barrier(sinus_rows(T + R * T - 1, W + T, D))
    table = nn(sinus, p_full).astype(BF)

    if sh.pair:
        i_y = sh.flip(i_got, 1)
        u_got, key_values = lax.optimization_barrier((u_got, key_values))
        u_y = sh.flip(u_got, 1)
    mixed_f, probs = att_fwd(q_lin, vecs, pen, kind_q, key_values, table, kaug)
    mixed_low = mixed_f.astype(BF)
    if sh.pair:
        place = jnp.stack([sh.f, sh.bit(0), sh.bit(1), ctx])
        mixed_f, hid, fetched = lax.optimization_barrier((mixed_f, hidden, (i_got, i_y, u_got, u_y)))
        hidden_got = sh.trade(hid)
        mixed_low = mixed_f.astype(BF)
        parts = (
            (output_proj, got_o, flip_o),
            (inner_proj,) + sh.pieces(*fetched[:2]),
            (outer_proj,) + sh.pieces(*fetched[2:]),
        )
        FF = inner_proj.shape[1]
        mixed_got = sh.trade(mixed_low)
        normed_low, activ_low, pre, outcome, d_res2, d_outer, n1, rstd1, vec_a = ffn_fwd(
            place, hidden, mixed_f, out_grad[0], vecs, *parts, FF
        )
        ffn, d_res1, d_attn, d_mixed, vec_b = ffn_bwd(
            place, C, pre, activ_low, normed_low, d_outer, sh.trade(d_outer), d_res2, n1, rstd1,
            mixed_got, hidden_got, vecs, *parts,
        )
    else:
        attn_out = nn(mixed_low, o_full) + vecs[6]
        normed, first_pull = jax.vjp(layer_norm, hidden.astype(F32) + attn_out, vecs[7], vecs[8])
        normed_low = normed.astype(BF)
        inner_pre = nn(normed_low, inner_full) + vecs[12:].reshape(-1, sh.parts, dn).transpose(1, 0, 2).reshape(-1)
        activated, gelu_pull = jax.vjp(partial(jax.nn.gelu, approximate=True), inner_pre)
        activ_low = activated.astype(BF)
        outer_out = nn(activ_low, outer_full) + vecs[9]
        outcome, second_pull = jax.vjp(layer_norm, normed + outer_out, vecs[10], vecs[11])
        d_res2, grad_ffn_gain, grad_ffn_shift = second_pull(cotangent)
        d_outer = d_res2.astype(BF)
        grad_outer_bias = jnp.sum(d_outer.astype(F32), axis=0)
        d_inner = gelu_pull(nt(d_outer, outer_full))[0].astype(BF)
        grad_inner_bias = jnp.sum(d_inner.astype(F32), axis=0)
        d_normed = d_res2 + nt(d_inner, inner_full)
        d_res1, grad_attn_gain, grad_attn_shift = first_pull(d_normed)
        d_attn = d_res1.astype(BF)
        grad_output_bias = jnp.sum(d_attn.astype(F32), axis=0)
        d_mixed = nt(d_attn, o_full).astype(BF)
        vec_a = jnp.stack(
            [grad_ffn_gain, grad_ffn_shift, grad_outer_bias] + [jnp.zeros((D,), F32)] * 5
        )
        ib = grad_inner_bias.reshape(sh.parts, -1, dn).transpose(1, 0, 2).reshape(-1, D)
        vec_b = jnp.concatenate(
            [
                jnp.stack(
                    [
                        grad_attn_gain, grad_attn_shift, grad_output_bias,
                        jnp.sum(d_mixed.astype(F32), axis=0),
                    ]
                ),
                ib,
            ],
            axis=0,
        )
    if sh.pair:
        d_attn_got = sh.trade(d_attn)
    dq, att_vec, dkv, d_table = att_bwd(
        q_lin, vecs, kind_q, d_mixed, mixed_f, probs, key_values, table, kaug
    )
    if sh.pair:
        dq_got = sh.trade(dq)
        ffn = lax.psum_scatter(ffn, "ctx", scatter_dimension=0, tiled=False)

        d_hid = hidden_grads(
            place, dkv.reshape(2 * D, W), key_proj, other_k, value_proj, other_v, C, R
        )
        keep, send = sh.sides(sh.spread(d_hid), 0, sh.bits - 1)
        got = sh.flip(send, 0)
        dkv, _ = lax.optimization_barrier((dkv, send))

        whole = key_grads(dkv, x_win)
        whole, got = lax.optimization_barrier((whole, got))
        d_hid = sh.add(keep, got)
        keep, send = sh.sides(d_hid, 1, sh.bits - 2)
        got = sh.flip(send, 1)
        keep_w, send_w = sh.sides(whole, 0, 0)
        got_w = sh.flip(send_w, 0)
        d_table, _, _ = lax.optimization_barrier((d_table, send, send_w))
        rest = position_grads(d_table, sinus, (att_vec, vec_a, vec_b))
        rest, got_w = lax.optimization_barrier((rest, got_w))
        whole = jnp.concatenate([sh.add(keep_w, got_w), sh.halve(rest, 0, 0)], axis=0)
        keep_w, send_w = sh.order(whole[:, :dn], whole[:, dn:], sh.f)
        got_x = sh.trade(send_w)
        go, gq = (
            tn(
                jnp.concatenate([b, b_got], axis=0),
                jnp.concatenate([sh.own(a, 1), sh.own(a_got, 1)], axis=0),
            )
            for a, a_got, b, b_got in (
                (mixed_low, mixed_got, d_attn, d_attn_got), (hidden, hidden_got, dq, dq_got)
            )
        )
        mine = sh.halve_cols(go, gq)
        d_hid = sh.halve(sh.add(keep, got), 2, sh.bits - 3)
        got_x, d_hid, mine, ffn = lax.optimization_barrier((got_x, d_hid, mine, ffn))
        ffn = lax.all_gather(ffn, "ctx", axis=0, tiled=False)
        grads = jnp.concatenate([sh.add(keep_w, got_x), mine], axis=0)
        grads = grads.reshape((2,) * (sh.bits - 1) + (-1, dn))
        for k in range(1, sh.bits):
            grads = sh.halve(grads, k, grads.ndim - 3)
            if k + 2 < sh.bits:
                d_hid = sh.halve(d_hid, k + 2, d_hid.ndim - 3)
                grads, d_hid = lax.optimization_barrier((grads, d_hid))
        n = grads.shape[0]
        cut = (n // 2 + 15) // 16 * 16
        one, two = grads[:cut], grads[cut:]
        highs = list(reversed(range(2, sh.bits)))
        for i, (k, other) in enumerate(zip(highs + [1], [1] + highs)):
            one = sh.double(one, k, one.ndim - 2)
            two = sh.double(two, other, 0 if i == 0 else i - 1)
            if i == 0:
                one, two, d_hid, ffn = lax.optimization_barrier((one, two, d_hid, ffn))
            if i == 1:
                gi, gu = ffn_final(ffn, inner_bias.shape[0] * 2, D)
                one, two, gi, gu, d_hid = lax.optimization_barrier((one, two, gi, gu, d_hid))
                input_grad = input_grads(place, d_res1, dq, query_proj, other_q, d_hid)
        one, two, input_grad = lax.optimization_barrier((one, two, input_grad))
        one, two = one.reshape(-1, dn), two.reshape(-1, dn)
        gk, gv, gp, go, gq, s = grad_final(
            place, one, two, sh.flip(one, 0), sh.flip(two, 0), D, C // 2
        )
        s = unpack_rows(s)
    else:
        dkv = dkv.reshape(2 * D, W)
        gkv, gp = (
            lax.dot_general(a, b, (((0,), (1,)), ((), ())), preferred_element_type=F32)
            for a, b in ((x_win, dkv), (sinus, d_table))
        )
        d_hid = tn(dkv[:D], jnp.transpose(k_full)) + tn(dkv[D:], jnp.transpose(v_full))
        d_hid = d_hid.astype(BF)
        below = (C - 1 - R) * T
        d_hid = jnp.pad(d_hid, ((below, (C - 1) * T + L - below - W), (0, 0)))
        d_hid = lax.dynamic_slice_in_dim(d_hid, (C - 1 - ctx) * T, L, 0)
        d_hid = lax.psum_scatter(d_hid, "ctx", scatter_dimension=0, tiled=True)
        input_grad = d_res1 + nt(dq, q_full) + d_hid.astype(F32)
        s = jnp.concatenate([att_vec, vec_a, vec_b], axis=0)
        sums = [
            gkv, gp, tn(mixed_low, d_attn), tn(hidden, dq), tn(normed_low, d_inner),
            tn(activ_low, d_outer), jnp.transpose(s),
        ]
        sums = [
            lax.psum_scatter(a.astype(BF), "fsdp", scatter_dimension=0, tiled=True) for a in sums
        ]
        gkv, gp, go, gq, gi, gu, s = (a.astype(F32) for a in lax.psum(sums, "ctx"))
        gk, gv, s = gkv[:, :D], gkv[:, D:], jnp.transpose(s)
        s = [s[i] for i in (19, 0, 1, 2, 18, 16, 17, 10, 8, 9)] + [s[3:5], s[20:24].reshape(-1)]
    return (
        outcome.astype(BF)[None],
        input_grad[None],
        gq,
        gk,
        gv,
        s[0],
        s[1],
        s[2],
        s[3],
        s[10],
        gp,
        go,
        s[4],
        s[5],
        s[6],
        gi,
        s[11],
        gu,
        s[7],
        s[8],
        s[9],
    )


def solution(mesh):
    in_specs = (
        P("fsdp", "ctx", None),
        P("fsdp", "ctx"),
        P("fsdp", "ctx"),
        P("fsdp", "ctx", None),
        P("fsdp", None),
        P("fsdp", None),
        P("fsdp", None),
        P("fsdp"),
        P("fsdp"),
        P("fsdp"),
        P("fsdp"),
        P(None, "fsdp"),
        P("fsdp", None),
        P("fsdp", None),
        P("fsdp"),
        P("fsdp"),
        P("fsdp"),
        P("fsdp", None),
        P("fsdp"),
        P("fsdp", None),
        P("fsdp"),
        P("fsdp"),
        P("fsdp"),
    )
    out_specs = (
        P("fsdp", "ctx", None),
        P("fsdp", "ctx", None),
        P("fsdp", None),
        P("fsdp", None),
        P("fsdp", None),
        P("fsdp"),
        P("fsdp"),
        P("fsdp"),
        P("fsdp"),
        P(None, "fsdp"),
        P("fsdp", None),
        P("fsdp", None),
        P("fsdp"),
        P("fsdp"),
        P("fsdp"),
        P("fsdp", None),
        P("fsdp"),
        P("fsdp", None),
        P("fsdp"),
        P("fsdp"),
        P("fsdp"),
    )
    return jax.shard_map(
        per_device, mesh=mesh, in_specs=in_specs, out_specs=out_specs, check_vma=False
    )
```

```python
from functools import partial
import jax
import jax.numpy as jnp
from jax import lax
from jax.experimental import pallas as pl
from jax.experimental.pallas import tpu as pltpu
from jax.sharding import PartitionSpec as P

H = 12
DH = 64
EPS = 1e-06
BIG = 1e30
BF = jnp.bfloat16
F32 = jnp.float32


def nt(a, b):
    return lax.dot_general(a, b, (((1,), (1,)), ((), ())), preferred_element_type=F32)


def nn(a, b):
    return lax.dot_general(a, b, (((1,), (0,)), ((), ())), preferred_element_type=F32)


def tn(a, b):
    return lax.dot_general(a, b, (((0,), (0,)), ((), ())), preferred_element_type=F32)


def att_fwd_kernel(
    q_ref, v_rows, pen_ref, kind_ref, k_ref, v_ref, t_ref, ka_ref, o_ref, low_ref, p_ref
):
    T = q_ref.shape[0]
    W = k_ref.shape[0]
    blocks = W // T
    c = DH**-0.5
    q = q_ref[...]
    qc = ((q + v_rows[1:2, :]) * c).astype(BF)
    qp = ((q + v_rows[2:3, :]) * c).astype(BF)
    qt = (q + v_rows[3:4, :]) * c
    t0, t1 = qt * v_rows[4:5, :], qt * v_rows[5:6, :]
    lane = lax.broadcasted_iota(jnp.int32, (T, 128), 1)
    row = lax.broadcasted_iota(jnp.int32, (T, 128), 0)
    same = kind_ref[...] > 0.5
    pen = pen_ref[...]
    zero = jnp.zeros_like(qc)
    heads, where_q = [], []
    for h in range(2):
        mine = (lane < DH) if h == 0 else (lane >= DH)
        a0 = jnp.broadcast_to(jnp.sum(jnp.where(mine, t0, 0.0), axis=1, keepdims=True), (T, 128))
        a1 = jnp.broadcast_to(jnp.sum(jnp.where(mine, t1, 0.0), axis=1, keepdims=True), (T, 128))
        one, two = jnp.where(same, a1, a0), jnp.where(same, a0, a1)
        one_high, two_high = one.astype(BF).astype(F32), two.astype(BF).astype(F32)
        extra = jnp.where(lane == 4, two_high, jnp.where(lane == 5, two - two_high, pen))
        extra = jnp.where(lane == 0, one_high, jnp.where(lane == 1, one - one_high, extra))
        heads.append(jnp.concatenate([jnp.where(mine, qc, zero), extra.astype(BF)], axis=1))
        where_q.append(jnp.where(mine, qp, zero))
    s = nt(jnp.concatenate(heads, axis=0), jnp.concatenate([k_ref[...], ka_ref[...]], axis=1))
    w = nt(jnp.concatenate(where_q, axis=0), t_ref[...])
    probs = []
    for h in range(2):
        turned = [
            pltpu.roll(w[T * h : T * (h + 1), 128 * b : 128 * b + 128], 1, 1, stride=1, stride_axis=0)
            for b in range(blocks + 1)
        ]
        tiles = [
            s[T * h : T * (h + 1), 128 * b : 128 * b + 128]
            + jnp.where(lane <= row, turned[b], turned[b + 1])
            for b in range(blocks)
        ]
        top = tiles[0]
        for b in range(1, blocks):
            top = jnp.maximum(top, tiles[b])
        top = jnp.max(top, axis=1, keepdims=True)
        tiles = [jnp.exp(a - top) for a in tiles]
        total = tiles[0]
        for b in range(1, blocks):
            total = total + tiles[b]
        inverse = 1.0 / jnp.sum(total, axis=1, keepdims=True)
        p = jnp.concatenate([(a * inverse).astype(BF) for a in tiles], axis=1)
        p_ref[h] = p
        probs.append(p)
    out = nn(jnp.concatenate(probs, axis=0), v_ref[...])
    out = jnp.where(lane < DH, out[:T], out[T:])
    o_ref[...] = out
    low_ref[...] = out.astype(BF)


def att_bwd_kernel(
    q_ref, v_rows, kind_ref, dm_ref, o_ref, p_ref, k_ref, v_ref, t_ref, ka_ref,
    dq_ref, vec_ref, dkv_ref, dt_ref,
):
    T = q_ref.shape[0]
    W = k_ref.shape[0]
    blocks = W // T
    c = DH**-0.5
    q = q_ref[...]
    qc = ((q + v_rows[1:2, :]) * c).astype(BF)
    qp = ((q + v_rows[2:3, :]) * c).astype(BF)
    qt = (q + v_rows[3:4, :]) * c
    e0, e1 = v_rows[4:5, :], v_rows[5:6, :]
    lane = lax.broadcasted_iota(jnp.int32, (T, 128), 1)
    row = lax.broadcasted_iota(jnp.int32, (T, 128), 0)
    same = kind_ref[...] > 0.5
    flip = jnp.where(lane + row == T - 1, 1.0, 0.0).astype(BF)
    qpr = nn(flip, qp).astype(BF)
    dm = dm_ref[...]
    dmo = dm.astype(F32) * o_ref[...]
    zero = jnp.zeros_like(dm)
    stack = lambda parts: jnp.concatenate(parts, axis=0)
    mine = [lane < DH, lane >= DH]
    pick = lambda a: stack([jnp.where(m, a, zero) for m in mine])
    dms = pick(dm)
    delta = jnp.sum(
        stack([jnp.where(m, dmo, 0.0) for m in mine]), axis=1, keepdims=True
    )
    dp = nt(dms, v_ref[...])
    p = stack([p_ref[0], p_ref[1]])
    ds = (p.astype(F32) * (dp - delta)).astype(BF)
    dc = nn(ds, jnp.concatenate([k_ref[...], ka_ref[...]], axis=1))
    wide = []
    for h in range(2):
        back = nn(flip, ds[T * h : T * (h + 1)])
        turned = [
            pltpu.roll(back[:, 128 * b : 128 * b + 128], 0, 1, stride=1, stride_axis=0)
            for b in range(blocks)
        ]
        edge = jnp.zeros((T, 128), F32)
        tiles = [
            jnp.where(lane >= row, a, b).astype(BF)
            for a, b in zip(turned + [edge], [edge] + turned)
        ]
        wide.append(jnp.concatenate(tiles, axis=1))
    wide = stack(wide)
    dqp = nn(wide, t_ref[...])
    dkv_ref[0] = tn(pick(qc), ds).astype(BF)
    dkv_ref[1] = tn(dms, p).astype(BF)
    dt_ref[...] = tn(pick(qpr), wide).astype(BF)
    both = lambda a: jnp.where(mine[0], a[:T], a[T:])
    dc_low = both(dc[:, :128]).astype(BF).astype(F32)
    dp_low = nn(flip, both(dqp).astype(BF))
    one = both(jnp.broadcast_to(dc[:, 128:129], (2 * T, 128)))
    two = both(jnp.broadcast_to(dc[:, 132:133], (2 * T, 128)))
    same_sum, other_sum = jnp.where(same, one, two), jnp.where(same, two, one)
    dt = other_sum * e0 + same_sum * e1
    dq_ref[...] = (c * (dc_low + dp_low + dt)).astype(BF)
    total = lambda a: jnp.sum(a, axis=0, keepdims=True)
    rows = [c * total(dc_low), c * total(dp_low), c * total(dt), total(other_sum * qt), total(same_sum * qt)]
    vec_ref[...] = jnp.concatenate(rows + [jnp.zeros((3, 128), F32)], axis=0)


def att_fwd(q, rows, pen, kind, kv, t, ka):
    T, D = q.shape
    W = kv.shape[0]
    keys, values = (pl.BlockSpec((W, 128), lambda i, n=n: (0, i + n * D // 128)) for n in range(2))
    heads = D // DH
    col = lambda n: pl.BlockSpec((n, 128), lambda i: (0, i))
    fixed = lambda n: pl.BlockSpec((n, 128), lambda i: (0, 0))
    return pl.pallas_call(
        att_fwd_kernel,
        grid=(D // 128,),
        in_specs=[col(T), col(16), fixed(T), fixed(T), keys, values, col(W + T), fixed(W)],
        out_specs=[col(T), col(T), pl.BlockSpec((2, T, W), lambda i: (i, 0, 0))],
        out_shape=[
            jax.ShapeDtypeStruct((T, D), F32),
            jax.ShapeDtypeStruct((T, D), BF),
            jax.ShapeDtypeStruct((heads, T, W), BF),
        ],
        compiler_params=pltpu.CompilerParams(vmem_limit_bytes=60 * 2**20),
        cost_estimate=pl.CostEstimate(
            flops=2 * heads * T * W * 2048,
            bytes_accessed=2 * (3 * W * D + heads * T * W),
            transcendentals=heads * T * W,
        ),
        name="att_fwd",
    )(q, rows, pen, kind, kv, kv, t, ka)


def att_bwd(q, rows, kind, dm, o, p, kv, t, ka):
    T, D = q.shape
    W = kv.shape[0]
    keys, values = (pl.BlockSpec((W, 128), lambda i, n=n: (0, i + n * D // 128)) for n in range(2))
    heads = D // DH
    col = lambda n: pl.BlockSpec((n, 128), lambda i: (0, i))
    fixed = lambda n: pl.BlockSpec((n, 128), lambda i: (0, 0))
    return pl.pallas_call(
        att_bwd_kernel,
        grid=(D // 128,),
        in_specs=[
            col(T), col(16), fixed(T), col(T), col(T), pl.BlockSpec((2, T, W), lambda i: (i, 0, 0)),
            keys, values, col(W + T), fixed(W),
        ],
        out_specs=[
            col(T), col(8), pl.BlockSpec((2, 128, W), lambda i: (0, i, 0)),
            pl.BlockSpec((128, W + T), lambda i: (i, 0)),
        ],
        out_shape=[
            jax.ShapeDtypeStruct((T, D), BF),
            jax.ShapeDtypeStruct((8, D), F32),
            jax.ShapeDtypeStruct((2, D, W), BF),
            jax.ShapeDtypeStruct((D, W + T), BF),
        ],
        compiler_params=pltpu.CompilerParams(vmem_limit_bytes=60 * 2**20),
        cost_estimate=pl.CostEstimate(
            flops=2**20, bytes_accessed=2**20, transcendentals=0
        ),
        name="att_bwd",
    )(q, rows, kind, dm, o, p, kv, kv, t, ka)


def pack_rows(vectors, dn):
    counts = [v.size // dn for v in vectors]

    def kernel(*refs):
        out = refs[-1]
        at = 0
        for ref, n in zip(refs, counts):
            for j in range(n):
                if len(ref.shape) == 1:
                    out[at, :] = ref[pl.ds(j * dn, dn)].astype(F32)
                else:
                    out[at, :] = ref[j, :].astype(F32)
                at += 1

    return pl.pallas_call(
        kernel,
        out_shape=jax.ShapeDtypeStruct((sum(counts), dn), F32),
        name="pack_rows",
    )(*vectors)


def ffn_final(blocks, FF, D):
    count, _, dn = blocks.shape
    steps = FF // D
    per = count // steps
    ri, ru = FF // count, FF // 2 // count

    def kernel(b_ref, i_ref, u_ref):
        gi = jnp.concatenate([b_ref[k, :ri] for k in range(per)], axis=0)
        i_ref[...] = jnp.transpose(gi.astype(F32))
        for k in range(per):
            u_ref[ru * k : ru * (k + 1), :dn] = b_ref[k, ri : ri + ru].astype(F32)
            u_ref[ru * k : ru * (k + 1), dn:] = b_ref[k, ri + ru :].astype(F32)

    return pl.pallas_call(
        kernel,
        grid=(steps,),
        in_specs=[pl.BlockSpec((per, ri + 2 * ru, dn), lambda i: (i, 0, 0))],
        out_specs=[
            pl.BlockSpec((dn, D), lambda i: (0, i)), pl.BlockSpec((FF // 2 // steps, D), lambda i: (i, 0))
        ],
        out_shape=[
            jax.ShapeDtypeStruct((dn, FF), F32), jax.ShapeDtypeStruct((FF // 2, D), F32)
        ],
        cost_estimate=pl.CostEstimate(flops=2**33, bytes_accessed=8 * D * FF, transcendentals=0),
        name="ffn_final",
    )(blocks)


def split_cols(a, f, odd):
    h = a.shape[1] // 2
    q = h // 2
    own = jnp.where(f == 0, a[:, :h], a[:, h:])
    other = jnp.where(f == 0, a[:, h:], a[:, :h])
    swapped = jnp.concatenate([other[:, q:], other[:, :q]], axis=1)
    return jnp.concatenate([own, jnp.where(odd, swapped, other)], axis=1)


def merge_cols(a, f, odd):
    h = a.shape[1] // 2
    q = h // 2
    own, other = a[:, :h], a[:, h:]
    swapped = jnp.concatenate([other[:, q:], other[:, :q]], axis=1)
    other = jnp.where(odd, swapped, other)
    return jnp.where(
        f == 0, jnp.concatenate([own, other], axis=1), jnp.concatenate([other, own], axis=1)
    )


def swap_quarters(a, y, odd):
    h = a.shape[1] // 2
    q = h // 2
    a = jnp.where(y, jnp.concatenate([a[:, h:], a[:, :h]], axis=1), a)
    pairs = jnp.concatenate([a[:, q:h], a[:, :q], a[:, h + q :], a[:, h : h + q]], axis=1)
    return jnp.where(odd, pairs, a)


def middle_swap(a):
    q = a.shape[1] // 4
    return jnp.concatenate([a[:, :q], a[:, 2 * q : 3 * q], a[:, q : 2 * q], a[:, 3 * q :]], axis=1)


def split_quarters(a, f, y, odd):
    h = a.shape[1] // 2
    own = jnp.where(f == 0, a[:, :h], a[:, h:])
    other = jnp.where(f == 0, a[:, h:], a[:, :h])
    return own, middle_swap(swap_quarters(other, y, odd))


def merge_quarters(a, f, y, odd):
    h = a.shape[1] // 2
    own, other = a[:, :h], swap_quarters(middle_swap(a[:, h:]), y, odd)
    return jnp.where(
        f == 0, jnp.concatenate([own, other], axis=1), jnp.concatenate([other, own], axis=1)
    )


def norm_stats(res):
    center = res - jnp.mean(res, axis=1, keepdims=True)
    rstd = lax.rsqrt(jnp.mean(center * center, axis=1, keepdims=True) + EPS)
    return center * rstd, rstd


def norm_back(g, gain, n, rstd):
    gg = g * gain
    return (gg - jnp.mean(gg, axis=1, keepdims=True) - n * jnp.mean(gg * n, axis=1, keepdims=True)) * rstd


def row_sum(a):
    return jnp.sum(a, axis=0, keepdims=True)


GELU_A = 0.7978845608028654
GELU_B = 0.044715


def ffn_specs(T, D, FF):
    steps = FF // D
    half = steps // 2
    c = FF // steps
    q = D // 8

    def chunk_at(j, s):
        other = half * (1 - s[0]) + (s[2] ^ jnp.maximum(j - half, 0))
        return jnp.where(j < half, half * s[0] + j, other)

    col = lambda j, s: (0, chunk_at(j, s))
    whole = lambda *shape: pl.BlockSpec(shape, lambda j, s: (0,) * len(shape))
    inner = [pl.BlockSpec((4 * q, c), col)] + [pl.BlockSpec((q, c), col)] * 4
    outer = [pl.BlockSpec((c, D), lambda j, s: (jnp.minimum(j, half - 1), 0))]
    outer += [whole(c // 2, D)] * 4
    proj = [whole(4 * q, D), whole(2 * q, D), whole(2 * q, D)]
    return steps, half, c, chunk_at, col, whole, inner, outer, proj


def outer_chunk(j, half, odd, refs):
    last = j > half
    a = jnp.where(last, refs[2][...], refs[1][...])
    b = jnp.where(last, refs[4][...], refs[3][...])
    pair = jnp.concatenate([jnp.where(odd, b, a), jnp.where(odd, a, b)], axis=0)
    return jnp.where(j < half, refs[0][...], pair)


def rows_of(refs):
    return jnp.concatenate([r[...] for r in refs], axis=0)


def inner_bias_chunk(b, half, vec_ref, D):
    rows = [vec_ref[pl.ds(12 + 2 * (b % half) + n, 1), :] for n in range(2)]
    parts = [jnp.where(b < half, r[:, : D // 2], r[:, D // 2 :]) for r in rows]
    return jnp.concatenate(parts, axis=1)


def gelu_tanh(u):
    return jnp.tanh(GELU_A * (u + GELU_B * u * u * u))


def first_norm(x, mixed, vec_ref, w, f, odd):
    attn = nn(split_cols(mixed, f, odd).astype(BF), w) + vec_ref[6:7, :]
    n1, rstd = norm_stats(x.astype(F32) + attn)
    return n1, rstd, n1 * vec_ref[7:8, :] + vec_ref[8:9, :]


def ffn_fwd(place, x, mixed, cot, vecs, o_parts, i_parts, u_parts, FF):
    T, D = x.shape
    steps, half, c, chunk_at, col, whole, inner, outer, proj = ffn_specs(T, D, FF)

    def kernel(s_ref, x_ref, m_ref, g_ref, v_ref, *refs):
        o_refs, i_refs, u_refs = refs[:3], refs[3:8], refs[8:13]
        nl_ref, act_ref, pre_ref, res_ref, dr_ref, do_ref, n1_ref, rs_ref, gv_ref = refs[13:22]
        np_ref, acc_ref, nf_ref = refs[22:]
        j = pl.program_id(0)
        f, odd, y = s_ref[0], s_ref[1] == 1, s_ref[2] == 1

        @pl.when(j == 0)
        def _():
            n1, rstd, normed = first_norm(x_ref[...], m_ref[...], v_ref, rows_of(o_refs), f, odd)
            n1_ref[...] = n1
            rs_ref[...] = jnp.broadcast_to(rstd, (T, 128))
            nf_ref[...] = normed
            nl_ref[...] = normed.astype(BF)
            np_ref[...] = jnp.concatenate(split_quarters(normed, f, y, odd), axis=1).astype(BF)
            acc_ref[...] = jnp.zeros_like(acc_ref)

        bias = inner_bias_chunk(chunk_at(j, s_ref), half, v_ref, D)
        pre = nn(np_ref[...], rows_of(i_refs)) + bias
        pre_ref[...] = pre
        act = (0.5 * pre * (1.0 + gelu_tanh(pre))).astype(BF)
        act_ref[...] = act
        acc_ref[...] += nn(act, outer_chunk(j, half, odd, u_refs))

        @pl.when(j == steps - 1)
        def _():
            n2, rstd = norm_stats(nf_ref[...] + (acc_ref[...] + v_ref[9:10, :]))
            g = g_ref[...].astype(F32)
            res_ref[...] = (n2 * v_ref[10:11, :] + v_ref[11:12, :]).astype(BF)
            d = norm_back(g, v_ref[10:11, :], n2, rstd)
            dr_ref[...] = d
            do = d.astype(BF)
            do_ref[...] = do
            gv_ref[0:1, :] = row_sum(g * n2)
            gv_ref[1:2, :] = row_sum(g)
            gv_ref[2:3, :] = row_sum(do.astype(F32))
            gv_ref[3:8, :] = jnp.zeros((5, D), F32)

    f32 = lambda *shape: jax.ShapeDtypeStruct(shape, F32)
    low = lambda *shape: jax.ShapeDtypeStruct(shape, BF)
    tok = whole(T, D)
    chunk = pl.BlockSpec((T, c), col)
    return pl.pallas_call(
        kernel,
        grid_spec=pltpu.PrefetchScalarGridSpec(
            num_scalar_prefetch=1,
            grid=(steps,),
            in_specs=[tok, tok, tok, whole(16, D)] + proj + inner + outer,
            out_specs=[tok, chunk, chunk, tok, tok, tok, tok, whole(T, 128), whole(8, D)],
            scratch_shapes=[
                pltpu.VMEM((T, D), BF), pltpu.VMEM((T, D), F32), pltpu.VMEM((T, D), F32)
            ],
        ),
        out_shape=[
            low(T, D), low(T, FF), f32(T, FF), low(T, D), f32(T, D), low(T, D), f32(T, D),
            f32(T, 128), f32(8, D),
        ],
        compiler_params=pltpu.CompilerParams(vmem_limit_bytes=60 * 2**20),
        cost_estimate=pl.CostEstimate(
            flops=4 * T * D * FF, bytes_accessed=4 * D * FF, transcendentals=T * FF
        ),
        name="ffn_fwd",
    )(place, x, mixed, cot, vecs, *o_parts, *i_parts, *u_parts)


def ffn_bwd(
    place, count, pre, act, normed, d_outer, d_outer_got, d_res2, n1, rstd1, mixed_got, x_got,
    vecs, o_parts, i_parts, u_parts,
):
    T, FF = pre.shape
    D = d_outer.shape[1]
    dn = D // 2
    steps, half, c, chunk_at, col, whole, inner, outer, proj = ffn_specs(T, D, FF)
    ri, ru = FF // count, FF // 2 // count

    def kernel(s_ref, pre_ref, act_ref, nl_ref, do_ref, dog_ref, dr_ref, n1_ref, rs_ref, mg_ref, xg_ref, v_ref, *refs):
        o_refs, i_refs, u_refs = refs[:3], refs[3:8], refs[8:13]
        pay_ref, d1_ref, da_ref, dm_ref, gv_ref = refs[13:18]
        acc_ref, ib_ref, np_ref, nf_ref, do_both = refs[18:]
        j = pl.program_id(0)
        f, odd, y = s_ref[0], s_ref[1] == 1, s_ref[2] == 1

        @pl.when(j == 0)
        def _():
            acc_ref[...] = jnp.zeros_like(acc_ref)
            theirs = first_norm(xg_ref[...], mg_ref[...], v_ref, rows_of(o_refs), f, odd)[2]
            own, other = split_quarters(theirs, f, y, odd)
            np_ref[...] = jnp.concatenate([own, other], axis=1).astype(BF)
            nl = nl_ref[...]
            nf_ref[:T] = jnp.where(f == 0, nl[:, :dn], nl[:, dn:])
            nf_ref[T:] = own.astype(BF)
            do_both[:T] = do_ref[...]
            do_both[T:] = dog_ref[...]

        b = chunk_at(j, s_ref)
        w = rows_of(i_refs)
        pre_got = nn(np_ref[...], w) + inner_bias_chunk(b, half, v_ref, D)
        u = jnp.concatenate([pre_ref[...], pre_got], axis=0)
        t = gelu_tanh(u)
        slope = 0.5 * (1.0 + t) + 0.5 * u * (1.0 - t * t) * (GELU_A * (1.0 + 3.0 * GELU_B * u * u))
        di = (nt(do_both[...], outer_chunk(j, half, odd, u_refs)) * slope).astype(BF)
        ib_ref[pl.ds(b, 1), :] = row_sum(di[:T].astype(F32))
        acc_ref[...] += nt(di[:T], w)
        gi = tn(di, nf_ref[...]).astype(BF)
        for k in range(c // ri):
            pay_ref[b * (c // ri) + k, :ri] = gi[ri * k : ri * (k + 1)]

        @pl.when(j < half)
        def _():
            act_got = (0.5 * u[T:] * (1.0 + t[T:])).astype(BF)
            gu = tn(jnp.concatenate([act_ref[...], act_got], axis=0), do_both[...]).astype(BF)
            for k in range(c // ru):
                pay_ref[j * (c // ru) + k, ri : ri + ru] = gu[ru * k : ru * (k + 1), :dn]
                pay_ref[j * (c // ru) + k, ri + ru :] = gu[ru * k : ru * (k + 1), dn:]

        @pl.when(j == steps - 1)
        def _():
            d_normed = dr_ref[...] + merge_quarters(acc_ref[...], f, y, odd)
            n1 = n1_ref[...]
            d1 = norm_back(d_normed, v_ref[7:8, :], n1, rs_ref[:, 0:1])
            d1_ref[...] = d1
            da = d1.astype(BF)
            da_ref[...] = da
            dm = merge_cols(nt(da, rows_of(o_refs)), f, odd)
            dm_ref[...] = dm.astype(BF)
            gv_ref[0:1, :] = row_sum(d_normed * n1)
            gv_ref[1:2, :] = row_sum(d_normed)
            gv_ref[2:3, :] = row_sum(da.astype(F32))
            gv_ref[3:4, :] = row_sum(dm.astype(BF).astype(F32))
            for n in range(2 * half):
                at = slice(0, dn) if n % 2 == 0 else slice(dn, D)
                gv_ref[4 + n : 5 + n, :dn] = ib_ref[n // 2 : n // 2 + 1, at]
                gv_ref[4 + n : 5 + n, dn:] = ib_ref[half + n // 2 : half + n // 2 + 1, at]

    f32 = lambda *shape: jax.ShapeDtypeStruct(shape, F32)
    low = lambda *shape: jax.ShapeDtypeStruct(shape, BF)
    tok = whole(T, D)
    chunk = pl.BlockSpec((T, c), col)
    return pl.pallas_call(
        kernel,
        grid_spec=pltpu.PrefetchScalarGridSpec(
            num_scalar_prefetch=1,
            grid=(steps,),
            in_specs=[chunk, chunk] + [tok] * 5 + [whole(T, 128), tok, tok, whole(16, D)]
            + proj + inner + outer,
            out_specs=[whole(count, ri + 2 * ru, dn), tok, tok, tok, whole(8, D)],
            scratch_shapes=[
                pltpu.VMEM((T, D), F32), pltpu.VMEM((steps, c), F32), pltpu.VMEM((T, D), BF),
                pltpu.VMEM((2 * T, dn), BF), pltpu.VMEM((2 * T, D), BF),
            ],
        ),
        out_shape=[low(count, ri + 2 * ru, dn), f32(T, D), low(T, D), low(T, D), f32(8, D)],
        compiler_params=pltpu.CompilerParams(vmem_limit_bytes=60 * 2**20),
        cost_estimate=pl.CostEstimate(
            flops=14 * T * D * FF, bytes_accessed=6 * D * FF, transcendentals=2 * T * FF
        ),
        name="ffn_bwd",
    )(
        place, pre, act, normed, d_outer, d_outer_got, d_res2, n1, rstd1, mixed_got, x_got, vecs,
        *o_parts, *i_parts, *u_parts,
    )


def key_grads(place, dkv, x_win):
    _, D, W = dkv.shape
    h = D // 2

    def kernel(s_ref, kv_ref, x_ref, send_ref, keep_ref):
        g = nn(kv_ref[0], x_ref[...]).astype(BF)

        @pl.when(pl.program_id(0) < 2)
        def _():
            send_ref[...] = g

        @pl.when(pl.program_id(0) >= 2)
        def _():
            keep_ref[...] = g

    return pl.pallas_call(
        kernel,
        grid_spec=pltpu.PrefetchScalarGridSpec(
            num_scalar_prefetch=1,
            grid=(4,),
            in_specs=[
                pl.BlockSpec((1, h, W), lambda i, s: (jnp.where(i < 2, 1 - s[1], s[1]), i % 2, 0)),
                pl.BlockSpec((W, D), lambda i, s: (0, 0)),
            ],
            out_specs=[
                pl.BlockSpec((h, D), lambda i, s: (jnp.minimum(i, 1), 0)),
                pl.BlockSpec((h, D), lambda i, s: (jnp.maximum(i - 2, 0), 0)),
            ],
        ),
        out_shape=[jax.ShapeDtypeStruct((D, D), BF)] * 2,
        compiler_params=pltpu.CompilerParams(vmem_limit_bytes=60 * 2**20),
        cost_estimate=pl.CostEstimate(
            flops=4 * D * D * W, bytes_accessed=6 * D * W, transcendentals=0
        ),
        name="key_grads",
    )(place, dkv, x_win)


def position_grads(place, d_table, sinus, vectors):
    D, WT = d_table.shape
    h = D // 2

    def kernel(s_ref, t_ref, x_ref, *refs):
        v_refs, (send_ref, keep_ref) = refs[:-2], refs[-2:]
        i = pl.program_id(0)
        g = nn(t_ref[...], x_ref[...]).astype(BF)
        small = jnp.concatenate([r[...] for r in v_refs], axis=0)
        small = jnp.concatenate([small, jnp.zeros((64 - small.shape[0], D), F32)], axis=0)
        even = jnp.where(i == 0, 1 - s_ref[1], s_ref[1]) == 0
        small = jnp.where(even, small, 0.0).astype(BF)

        @pl.when(i == 0)
        def _():
            send_ref[:h] = g
            send_ref[h:] = small

        @pl.when(i == 1)
        def _():
            keep_ref[:h] = g
            keep_ref[h:] = small

    whole = lambda *shape: pl.BlockSpec(shape, lambda i, s: (0,) * len(shape))
    return pl.pallas_call(
        kernel,
        grid_spec=pltpu.PrefetchScalarGridSpec(
            num_scalar_prefetch=1,
            grid=(2,),
            in_specs=[
                pl.BlockSpec((h, WT), lambda i, s: (jnp.where(i == 0, 1 - s[1], s[1]), 0)),
                whole(WT, D),
            ]
            + [whole(8, D)] * len(vectors),
            out_specs=[whole(h + 64, D)] * 2,
        ),
        out_shape=[jax.ShapeDtypeStruct((h + 64, D), BF)] * 2,
        compiler_params=pltpu.CompilerParams(vmem_limit_bytes=60 * 2**20),
        cost_estimate=pl.CostEstimate(
            flops=2 * D * D * WT, bytes_accessed=4 * D * WT, transcendentals=0
        ),
        name="position_grads",
    )(place, d_table, sinus, *vectors)


def hidden_grads(place, dkv, k_own, k_other, v_own, v_other, count, reach):
    D2, W = dkv.shape
    D = D2 // 2
    h = D // 2
    T = 128
    blocks = W // T

    def kernel(s_ref, a_ref, b_ref, k0, k1, v0, v1, send_ref, keep_ref):
        s = pl.program_id(0)
        odd = s_ref[1] == 1
        x = jnp.concatenate([a_ref[...], b_ref[...]], axis=1)
        for at, k, v in ((s_ref[0], k0, v0), (1 - s_ref[0], k1, v1)):
            g = nn(jnp.concatenate([k[...], v[...]], axis=1), x).astype(BF)
            parts = []
            for n in range(2):
                rel = 2 * s + n - s_ref[3] + reach
                part = g[:, T * n : T * (n + 1)]
                parts.append(jnp.where((rel >= 0) & (rel < blocks), part, jnp.zeros_like(part)))
            rows = pl.ds(pl.multiple_of(at * h, h), h)
            send_ref[0, rows, :] = jnp.where(odd, parts[0], parts[1])
            keep_ref[0, rows, :] = jnp.where(odd, parts[1], parts[0])

    whole = pl.BlockSpec((h, D), lambda s, p: (0, 0))
    block = lambda n: pl.BlockSpec(
        (D2, T), lambda s, p: (0, jnp.clip(2 * s + n - p[3] + reach, 0, blocks - 1))
    )
    return pl.pallas_call(
        kernel,
        grid_spec=pltpu.PrefetchScalarGridSpec(
            num_scalar_prefetch=1,
            grid=(count // 2,),
            in_specs=[block(0), block(1), whole, whole, whole, whole],
            out_specs=[pl.BlockSpec((1, D, T), lambda s, p: (s, 0, 0))] * 2,
        ),
        out_shape=[jax.ShapeDtypeStruct((count // 2, D, T), BF)] * 2,
        compiler_params=pltpu.CompilerParams(vmem_limit_bytes=60 * 2**20),
        cost_estimate=pl.CostEstimate(flops=2**20, bytes_accessed=2**20, transcendentals=0),
        name="hidden_grads",
    )(place, dkv, dkv, k_own, k_other, v_own, v_other)


def input_grads(place, d_res1, dq, q_own, q_other, d_hid):
    T, D = d_res1.shape

    def kernel(s_ref, r_ref, dq_ref, q0, q1, h_ref, out_ref):
        own, other = nt(dq_ref[...], q0[...]), nt(dq_ref[...], q1[...])
        first = s_ref[0] == 0
        g = jnp.concatenate([jnp.where(first, own, other), jnp.where(first, other, own)], axis=1)
        out_ref[...] = r_ref[...] + g + jnp.transpose(h_ref[...].astype(F32))

    whole = lambda a: pl.BlockSpec(a.shape, lambda i, s: (0, 0))
    args = (d_res1, dq, q_own, q_other, d_hid)
    return pl.pallas_call(
        kernel,
        grid_spec=pltpu.PrefetchScalarGridSpec(
            num_scalar_prefetch=1,
            grid=(1,),
            in_specs=[whole(a) for a in args],
            out_specs=whole(d_res1),
        ),
        out_shape=jax.ShapeDtypeStruct((T, D), F32),
        cost_estimate=pl.CostEstimate(
            flops=2**32, bytes_accessed=2**24, transcendentals=0
        ),
        name="input_grads",
    )(place, *args)


def grad_final(place, one, two, one_got, two_got, D, blocks):
    dn = one.shape[1]
    h = D // 2
    p, q = one.shape[0] // blocks, two.shape[0] // blocks

    def kernel(s_ref, a_ref, b_ref, c_ref, d_ref, k_ref, v_ref, p_ref, o_ref, q_ref, small_ref):
        odd = s_ref[1] == 1

        def rows(x_ref, y_ref):
            x, y = x_ref[...].astype(F32), y_ref[...].astype(F32)
            parts = []
            for n in range(blocks):
                parts += [x[p * n : p * (n + 1)], y[q * n : q * (n + 1)]]
            return jnp.concatenate(parts, axis=0)

        mine, other = rows(a_ref, b_ref), rows(c_ref, d_ref)
        low, high = jnp.where(odd, other, mine), jnp.where(odd, mine, other)
        k_ref[...] = jnp.transpose(low[:D])
        v_ref[...] = jnp.transpose(high[:D])
        p_ref[...] = jnp.transpose(jnp.concatenate([low[D : D + h], high[D : D + h]], axis=0))
        small_ref[...] = low[D + h : D + h + 64]
        o_ref[...] = jnp.transpose(low[D + h + 64 :])
        q_ref[...] = jnp.transpose(high[D + h + 64 :])

    lanes = lambda n: pl.BlockSpec((n, 128), lambda i, s: (0, i))
    out = pl.BlockSpec((128, D), lambda i, s: (i, 0))
    return pl.pallas_call(
        kernel,
        grid_spec=pltpu.PrefetchScalarGridSpec(
            num_scalar_prefetch=1,
            grid=(dn // 128,),
            in_specs=[lanes(a.shape[0]) for a in (one, two, one_got, two_got)],
            out_specs=[out] * 5 + [lanes(64)],
        ),
        out_shape=[jax.ShapeDtypeStruct((dn, D), F32)] * 5 + [jax.ShapeDtypeStruct((64, dn), F32)],
        name="grad_final",
    )(place, one, two, one_got, two_got)


def unpack_rows(s):
    dn = s.shape[1]
    singles = (19, 0, 1, 2, 18, 16, 17, 10, 8, 9)

    def kernel(s_ref, *outs):
        for i, out in zip(singles, outs):
            out[...] = s_ref[i, :]
        outs[-2][...] = s_ref[3:5, :]
        for j in range(4):
            outs[-1][pl.ds(j * dn, dn)] = s_ref[20 + j, :]

    shapes = [(dn,)] * len(singles) + [(2, dn), (4 * dn,)]
    return pl.pallas_call(
        kernel,
        out_shape=[jax.ShapeDtypeStruct(a, F32) for a in shapes],
        name="unpack_rows",
    )(s)


def layer_norm(residual, gain_vec, bias_vec):
    center = residual - jnp.mean(residual, axis=-1, keepdims=True)
    spread = jnp.mean(center * center, axis=-1, keepdims=True)
    return center * lax.rsqrt(spread + EPS) * gain_vec + bias_vec


def sinus_rows(first, count, width):
    half = width // 2
    freq = jnp.power(10000.0, -jnp.arange(half, dtype=F32) / half)
    coarse = (first - 64 * jnp.arange(count // 64)).astype(F32)[:, None] * freq
    fine = jnp.arange(64).astype(F32)[:, None] * freq
    sa, ca = jnp.sin(coarse)[:, None], jnp.cos(coarse)[:, None]
    sb, cb = jnp.sin(fine)[None], jnp.cos(fine)[None]
    both = jnp.concatenate([sa * cb - ca * sb, ca * cb + sa * sb], axis=2)
    return both.astype(BF).reshape(count, width)


class Shards:
    def __init__(self):
        self.parts = lax.axis_size("fsdp")
        self.pair = self.parts == 2
        self.f = lax.axis_index("fsdp")
        self.ctx = lax.axis_index("ctx")
        self.count = lax.axis_size("ctx")
        self.bits = self.count.bit_length() - 1
        self.swap = [(0, 1), (1, 0)]

    def bit(self, k):
        return (self.ctx >> k) & 1

    def flip(self, a, k):
        return lax.ppermute(a, "ctx", [(i, i ^ (1 << k)) for i in range(self.count)])

    def trade(self, a):
        return lax.ppermute(a, "fsdp", self.swap)

    def order(self, mine, other, at):
        return jnp.where(at == 0, mine, other), jnp.where(at == 0, other, mine)

    def fetch_half(self, w):
        half = w.shape[0] // 2
        return self.trade(lax.dynamic_slice_in_dim(w, self.bit(0) * half, half, 0))

    def fetch_quarter(self, w):
        n = w.shape[0] // 4
        return self.trade(lax.dynamic_slice_in_dim(w, (self.ctx % 4) * n, n, 0))

    def pieces(self, got, y):
        return got, y, self.flip(got, 0), self.flip(y, 0)

    def full_small(self, w):
        if not self.pair:
            return lax.all_gather(w, "fsdp", axis=0, tiled=False)
        return jnp.stack(self.order(w, self.trade(w), self.f))

    def own(self, a, axis, other=False):
        n = a.shape[axis] // self.parts
        at = (1 - self.f) if other else self.f
        return lax.dynamic_slice_in_dim(a, at * n, n, axis)

    def window(self, block, planes):
        y = self.flip(block, 1)
        self.first_hop = y
        pair = jnp.stack(self.order(block, y, self.bit(1)))
        up = down = pair
        groups = [(pair[None], self.flip(pair[None], 0))]
        for _ in range(planes):
            up = lax.ppermute(up, "ctx", [(i, i + 4) for i in range(self.count - 4)])
            down = lax.ppermute(down, "ctx", [(i + 4, i) for i in range(self.count - 4)])
            both = jnp.stack([up, down])
            groups.append((both, self.flip(both, 0)))
        self.last_hop = both
        groups = [jnp.stack(self.order(a, b, self.bit(0)), axis=2) for a, b in groups]
        planes = [g[0] for g in groups[:0:-1]] + [groups[0][0]] + [g[1] for g in groups[1:]]
        return jnp.concatenate(planes, axis=0).reshape((-1,) + block.shape)

    def sides(self, a, k, axis):
        keep = lax.dynamic_index_in_dim(a, self.bit(k), axis, keepdims=False)
        return keep, lax.dynamic_index_in_dim(a, 1 - self.bit(k), axis, keepdims=False)

    def add(self, a, b):
        return (a.astype(F32) + b.astype(F32)).astype(BF)

    def halve(self, a, k, axis):
        keep, send = self.sides(a, k, axis)
        return self.add(keep, self.flip(send, k))

    def halve_cols(self, low, high):
        keep, send = self.order(low, high, self.bit(0))
        return (keep.astype(F32) + self.flip(send.astype(BF), 0).astype(F32)).astype(BF)

    def double(self, a, k, axis):
        return jnp.stack(self.order(a, self.flip(a, k), self.bit(k)), axis=axis)

    def spread(self, a):
        return a.reshape((2,) * self.bits + a.shape[1:])


def per_device(
    hidden_in,
    segment_ids,
    token_types,
    out_grad,
    query_proj,
    key_proj,
    value_proj,
    value_bias,
    content_bias,
    position_bias,
    type_bias,
    type_embed,
    position_proj,
    output_proj,
    output_bias,
    attn_gain,
    attn_shift,
    inner_proj,
    inner_bias,
    outer_proj,
    outer_bias,
    ffn_gain,
    ffn_shift,
):
    sh = Shards()
    hidden = hidden_in[0]
    cotangent = out_grad[0].astype(F32)
    T, D = hidden.shape
    C = sh.count
    ctx = sh.ctx
    L = T * C
    R = C // 2
    NB = 2 * R + 1
    W = NB * T
    dn = D // sh.parts
    r = dn // C

    lane = jnp.arange(128)[None, :]
    in_seg = (lane >= 8) & (lane < 16)
    seg_own = segment_ids[0][:, None]
    kind_own = token_types[0][:, None]
    kaug_own = jnp.where(
        lane < 4, kind_own == 1, jnp.where(lane < 8, kind_own == 0, in_seg & (lane - 8 == seg_own))
    ).astype(BF)
    pen = jnp.where(in_seg & (lane - 8 != seg_own), -BIG, 0.0).astype(F32)
    kind_q = jnp.broadcast_to(kind_own, (T, 128)).astype(F32)

    around = sh.window(jnp.concatenate([hidden, kaug_own], axis=1), R // 4)
    around = lax.dynamic_slice_in_dim(around, ctx % 4, NB, 0)
    x_win = around[:, :, :D].reshape(W, D)
    at = jnp.arange(NB) + ctx - R
    valid = ((at >= 0) & (at < C))[:, None, None]
    kaug = jnp.where(valid, around[:, :, D:], (lane[None] == 15).astype(BF)).reshape(W, 128)

    vectors = (
        value_bias, content_bias, position_bias, type_bias, type_embed, output_bias,
        attn_gain, attn_shift, outer_bias, ffn_gain, ffn_shift, inner_bias,
    )
    small = pack_rows(vectors, dn)
    small_full = sh.full_small(small)
    if sh.pair:
        odd = sh.bit(0) == 1
        got_a = sh.trade(jnp.where(odd, value_proj, position_proj))
        got_b = sh.trade(jnp.where(odd, key_proj, query_proj))
        got_o = sh.fetch_half(output_proj)
        got_a, got_b, got_o, i_sh, u_sh, small_full, _ = lax.optimization_barrier(
            (got_a, got_b, got_o, inner_proj, outer_proj, small_full, sh.last_hop)
        )
        other_p, other_v = sh.order(got_a, sh.flip(got_a, 0), sh.bit(0))
        other_q, other_k = sh.order(got_b, sh.flip(got_b, 0), sh.bit(0))
        p_full, q_full = (
            jnp.concatenate(sh.order(w, g, sh.f), axis=0)
            for w, g in ((position_proj, other_p), (query_proj, other_q))
        )
        own, other = (
            jnp.concatenate(a, axis=1) for a in ((key_proj, value_proj), (other_k, other_v))
        )
        kv_full = jnp.concatenate(sh.order(own, other, sh.f), axis=0)
        flip_o = sh.flip(got_o, 0)
        i_got, u_got = sh.fetch_quarter(i_sh), sh.fetch_quarter(u_sh)
    else:
        p_full, k_full, v_full, q_full, o_full, inner_full, outer_full = (
            lax.all_gather(w, "fsdp", axis=0, tiled=True)
            for w in (
                position_proj, key_proj, value_proj, query_proj, output_proj, inner_proj, outer_proj
            )
        )
        kv_full = jnp.concatenate([k_full, v_full], axis=1)

    vecs = jnp.concatenate([small_full[i] for i in range(sh.parts)], axis=1)

    q_lin = nn(hidden, q_full)
    if sh.pair:
        i_got, x_win = lax.optimization_barrier((i_got, x_win))
    kv_bias = jnp.concatenate([jnp.zeros((D,), F32), vecs[0]])
    key_values = (nn(x_win, kv_full) + kv_bias).astype(BF)
    sinus = lax.optimization_barrier(sinus_rows(T + R * T - 1, W + T, D))
    table = nn(sinus, p_full).astype(BF)

    if sh.pair:
        i_y = sh.flip(i_got, 1)
        u_got, key_values = lax.optimization_barrier((u_got, key_values))
        u_y = sh.flip(u_got, 1)
    mixed_f, mixed_low, probs = att_fwd(q_lin, vecs, pen, kind_q, key_values, table, kaug)
    if sh.pair:
        place = jnp.stack([sh.f, sh.bit(0), sh.bit(1), ctx])
        mixed_f, mixed_low, hid, fetched = lax.optimization_barrier(
            (mixed_f, mixed_low, hidden, (i_got, i_y, u_got, u_y))
        )
        hidden_got = sh.trade(hid)
        parts = (
            (output_proj, got_o, flip_o),
            (inner_proj,) + sh.pieces(*fetched[:2]),
            (outer_proj,) + sh.pieces(*fetched[2:]),
        )
        FF = inner_proj.shape[1]
        mixed_got = sh.trade(mixed_low)
        normed_low, activ_low, pre, outcome, d_res2, d_outer, n1, rstd1, vec_a = ffn_fwd(
            place, hidden, mixed_f, out_grad[0], vecs, *parts, FF
        )
        ffn, d_res1, d_attn, d_mixed, vec_b = ffn_bwd(
            place, C, pre, activ_low, normed_low, d_outer, sh.trade(d_outer), d_res2, n1, rstd1,
            mixed_got, hidden_got, vecs, *parts,
        )
    else:
        attn_out = nn(mixed_low, o_full) + vecs[6]
        normed, first_pull = jax.vjp(layer_norm, hidden.astype(F32) + attn_out, vecs[7], vecs[8])
        normed_low = normed.astype(BF)
        inner_pre = nn(normed_low, inner_full) + vecs[12:].reshape(-1, sh.parts, dn).transpose(1, 0, 2).reshape(-1)
        activated, gelu_pull = jax.vjp(partial(jax.nn.gelu, approximate=True), inner_pre)
        activ_low = activated.astype(BF)
        outer_out = nn(activ_low, outer_full) + vecs[9]
        outcome, second_pull = jax.vjp(layer_norm, normed + outer_out, vecs[10], vecs[11])
        d_res2, grad_ffn_gain, grad_ffn_shift = second_pull(cotangent)
        d_outer = d_res2.astype(BF)
        grad_outer_bias = jnp.sum(d_outer.astype(F32), axis=0)
        d_inner = gelu_pull(nt(d_outer, outer_full))[0].astype(BF)
        grad_inner_bias = jnp.sum(d_inner.astype(F32), axis=0)
        d_normed = d_res2 + nt(d_inner, inner_full)
        d_res1, grad_attn_gain, grad_attn_shift = first_pull(d_normed)
        d_attn = d_res1.astype(BF)
        grad_output_bias = jnp.sum(d_attn.astype(F32), axis=0)
        d_mixed = nt(d_attn, o_full).astype(BF)
        vec_a = jnp.stack(
            [grad_ffn_gain, grad_ffn_shift, grad_outer_bias] + [jnp.zeros((D,), F32)] * 5
        )
        ib = grad_inner_bias.reshape(sh.parts, -1, dn).transpose(1, 0, 2).reshape(-1, D)
        vec_b = jnp.concatenate(
            [
                jnp.stack(
                    [
                        grad_attn_gain, grad_attn_shift, grad_output_bias,
                        jnp.sum(d_mixed.astype(F32), axis=0),
                    ]
                ),
                ib,
            ],
            axis=0,
        )
    if sh.pair:
        d_attn_got = sh.trade(d_attn)
    dq, att_vec, dkv, d_table = att_bwd(
        q_lin, vecs, kind_q, d_mixed, mixed_f, probs, key_values, table, kaug
    )
    if sh.pair:
        dq_got = sh.trade(dq)
        ffn = lax.psum_scatter(ffn, "ctx", scatter_dimension=0, tiled=False)

        send, keep = hidden_grads(
            place, dkv.reshape(2 * D, W), key_proj, other_k, value_proj, other_v, C, R
        )
        got = sh.flip(send, 0)
        dkv, _ = lax.optimization_barrier((dkv, send))

        send_w, keep_w = key_grads(place, dkv, x_win)
        send_w, keep_w, got = lax.optimization_barrier((send_w, keep_w, got))
        d_hid = sh.add(keep, got).reshape((2,) * (sh.bits - 1) + (D, T))
        keep, send = sh.sides(d_hid, 1, sh.bits - 2)
        got = sh.flip(send, 1)
        got_w = sh.flip(send_w, 0)
        d_table, _ = lax.optimization_barrier((d_table, send))
        send_p, keep_p = position_grads(place, d_table, sinus, (att_vec, vec_a, vec_b))
        send_p, keep_p, got_w = lax.optimization_barrier((send_p, keep_p, got_w))
        whole = jnp.concatenate(
            [sh.add(keep_w, got_w), sh.add(keep_p, sh.flip(send_p, 0))], axis=0
        )
        keep_w, send_w = sh.order(whole[:, :dn], whole[:, dn:], sh.f)
        got_x = sh.trade(send_w)
        go, gq = (
            tn(
                jnp.concatenate([b, b_got], axis=0),
                jnp.concatenate([sh.own(a, 1), sh.own(a_got, 1)], axis=0),
            )
            for a, a_got, b, b_got in (
                (mixed_low, mixed_got, d_attn, d_attn_got), (hidden, hidden_got, dq, dq_got)
            )
        )
        mine = sh.halve_cols(go, gq)
        d_hid = sh.add(keep, got)
        got_x, d_hid, mine, ffn = lax.optimization_barrier((got_x, d_hid, mine, ffn))
        ffn = lax.all_gather(ffn, "ctx", axis=0, tiled=False)
        grads = jnp.concatenate([sh.add(keep_w, got_x), mine], axis=0)
        grads = grads.reshape((2,) * (sh.bits - 1) + (-1, dn))
        for k in range(1, sh.bits):
            grads = sh.halve(grads, k, grads.ndim - 3)
            if k + 2 < sh.bits:
                d_hid = sh.halve(d_hid, k + 1, d_hid.ndim - 3)
                grads, d_hid = lax.optimization_barrier((grads, d_hid))
        n = grads.shape[0]
        cut = (n // 2 + 15) // 16 * 16
        one, two = grads[:cut], grads[cut:]
        highs = list(reversed(range(2, sh.bits)))
        for i, (k, other) in enumerate(zip(highs + [1], [1] + highs)):
            one = sh.double(one, k, one.ndim - 2)
            two = sh.double(two, other, 0 if i == 0 else i - 1)
            if i == 0:
                one, two, d_hid, ffn = lax.optimization_barrier((one, two, d_hid, ffn))
            if i == 1:
                d_hid = sh.halve(d_hid, sh.bits - 1, d_hid.ndim - 3)
                gi, gu = ffn_final(ffn, inner_bias.shape[0] * 2, D)
                one, two, gi, gu, d_hid = lax.optimization_barrier((one, two, gi, gu, d_hid))
                input_grad = input_grads(place, d_res1, dq, query_proj, other_q, d_hid)
        one, two, input_grad = lax.optimization_barrier((one, two, input_grad))
        one, two = one.reshape(-1, dn), two.reshape(-1, dn)
        gk, gv, gp, go, gq, s = grad_final(
            place, one, two, sh.flip(one, 0), sh.flip(two, 0), D, C // 2
        )
        s = unpack_rows(s)
    else:
        dkv = dkv.reshape(2 * D, W)
        gkv, gp = (
            lax.dot_general(a, b, (((0,), (1,)), ((), ())), preferred_element_type=F32)
            for a, b in ((x_win, dkv), (sinus, d_table))
        )
        d_hid = tn(dkv[:D], jnp.transpose(k_full)) + tn(dkv[D:], jnp.transpose(v_full))
        d_hid = d_hid.astype(BF)
        below = (C - 1 - R) * T
        d_hid = jnp.pad(d_hid, ((below, (C - 1) * T + L - below - W), (0, 0)))
        d_hid = lax.dynamic_slice_in_dim(d_hid, (C - 1 - ctx) * T, L, 0)
        d_hid = lax.psum_scatter(d_hid, "ctx", scatter_dimension=0, tiled=True)
        input_grad = d_res1 + nt(dq, q_full) + d_hid.astype(F32)
        s = jnp.concatenate([att_vec, vec_a, vec_b], axis=0)
        sums = [
            gkv, gp, tn(mixed_low, d_attn), tn(hidden, dq), tn(normed_low, d_inner),
            tn(activ_low, d_outer), jnp.transpose(s),
        ]
        sums = [
            lax.psum_scatter(a.astype(BF), "fsdp", scatter_dimension=0, tiled=True) for a in sums
        ]
        gkv, gp, go, gq, gi, gu, s = (a.astype(F32) for a in lax.psum(sums, "ctx"))
        gk, gv, s = gkv[:, :D], gkv[:, D:], jnp.transpose(s)
        s = [s[i] for i in (19, 0, 1, 2, 18, 16, 17, 10, 8, 9)] + [s[3:5], s[20:24].reshape(-1)]
    return (
        outcome.astype(BF)[None],
        input_grad[None],
        gq,
        gk,
        gv,
        s[0],
        s[1],
        s[2],
        s[3],
        s[10],
        gp,
        go,
        s[4],
        s[5],
        s[6],
        gi,
        s[11],
        gu,
        s[7],
        s[8],
        s[9],
    )


def solution(mesh):
    in_specs = (
        P("fsdp", "ctx", None),
        P("fsdp", "ctx"),
        P("fsdp", "ctx"),
        P("fsdp", "ctx", None),
        P("fsdp", None),
        P("fsdp", None),
        P("fsdp", None),
        P("fsdp"),
        P("fsdp"),
        P("fsdp"),
        P("fsdp"),
        P(None, "fsdp"),
        P("fsdp", None),
        P("fsdp", None),
        P("fsdp"),
        P("fsdp"),
        P("fsdp"),
        P("fsdp", None),
        P("fsdp"),
        P("fsdp", None),
        P("fsdp"),
        P("fsdp"),
        P("fsdp"),
    )
    out_specs = (
        P("fsdp", "ctx", None),
        P("fsdp", "ctx", None),
        P("fsdp", None),
        P("fsdp", None),
        P("fsdp", None),
        P("fsdp"),
        P("fsdp"),
        P("fsdp"),
        P("fsdp"),
        P(None, "fsdp"),
        P("fsdp", None),
        P("fsdp", None),
        P("fsdp"),
        P("fsdp"),
        P("fsdp"),
        P("fsdp", None),
        P("fsdp"),
        P("fsdp", None),
        P("fsdp"),
        P("fsdp"),
        P("fsdp"),
    )
    return jax.shard_map(
        per_device, mesh=mesh, in_specs=in_specs, out_specs=out_specs, check_vma=False
    )
```

```python
from functools import partial
import jax
import jax.numpy as jnp
from jax import lax
from jax.experimental import pallas as pl
from jax.experimental.pallas import tpu as pltpu
from jax.sharding import PartitionSpec as P

H = 12
DH = 64
EPS = 1e-06
BIG = 1e30
BF = jnp.bfloat16
F32 = jnp.float32


def nt(a, b):
    return lax.dot_general(a, b, (((1,), (1,)), ((), ())), preferred_element_type=F32)


def nn(a, b):
    return lax.dot_general(a, b, (((1,), (0,)), ((), ())), preferred_element_type=F32)


def tn(a, b):
    return lax.dot_general(a, b, (((0,), (0,)), ((), ())), preferred_element_type=F32)


def att_fwd_kernel(
    q_ref, v_rows, pen_ref, kind_ref, k_ref, v_ref, t_ref, ka_ref, o_ref, low_ref, p_ref
):
    T = q_ref.shape[0]
    W = k_ref.shape[0]
    blocks = W // T
    c = DH**-0.5
    q = q_ref[...]
    qc = ((q + v_rows[1:2, :]) * c).astype(BF)
    qp = ((q + v_rows[2:3, :]) * c).astype(BF)
    qt = (q + v_rows[3:4, :]) * c
    t0, t1 = qt * v_rows[4:5, :], qt * v_rows[5:6, :]
    lane = lax.broadcasted_iota(jnp.int32, (T, 128), 1)
    row = lax.broadcasted_iota(jnp.int32, (T, 128), 0)
    same = kind_ref[...] > 0.5
    pen = pen_ref[...]
    zero = jnp.zeros_like(qc)
    heads, where_q = [], []
    for h in range(2):
        mine = (lane < DH) if h == 0 else (lane >= DH)
        a0 = jnp.broadcast_to(jnp.sum(jnp.where(mine, t0, 0.0), axis=1, keepdims=True), (T, 128))
        a1 = jnp.broadcast_to(jnp.sum(jnp.where(mine, t1, 0.0), axis=1, keepdims=True), (T, 128))
        one, two = jnp.where(same, a1, a0), jnp.where(same, a0, a1)
        one_high, two_high = one.astype(BF).astype(F32), two.astype(BF).astype(F32)
        extra = jnp.where(lane == 4, two_high, jnp.where(lane == 5, two - two_high, pen))
        extra = jnp.where(lane == 0, one_high, jnp.where(lane == 1, one - one_high, extra))
        heads.append(jnp.concatenate([jnp.where(mine, qc, zero), extra.astype(BF)], axis=1))
        where_q.append(jnp.where(mine, qp, zero))
    s = nt(jnp.concatenate(heads, axis=0), jnp.concatenate([k_ref[...], ka_ref[...]], axis=1))
    w = nt(jnp.concatenate(where_q, axis=0), t_ref[...])
    probs = []
    for h in range(2):
        turned = [
            pltpu.roll(w[T * h : T * (h + 1), 128 * b : 128 * b + 128], 1, 1, stride=1, stride_axis=0)
            for b in range(blocks + 1)
        ]
        tiles = [
            s[T * h : T * (h + 1), 128 * b : 128 * b + 128]
            + jnp.where(lane <= row, turned[b], turned[b + 1])
            for b in range(blocks)
        ]
        top = tiles[0]
        for b in range(1, blocks):
            top = jnp.maximum(top, tiles[b])
        top = jnp.max(top, axis=1, keepdims=True)
        tiles = [jnp.exp(a - top) for a in tiles]
        total = tiles[0]
        for b in range(1, blocks):
            total = total + tiles[b]
        inverse = 1.0 / jnp.sum(total, axis=1, keepdims=True)
        p = jnp.concatenate([(a * inverse).astype(BF) for a in tiles], axis=1)
        p_ref[h] = p
        probs.append(p)
    out = nn(jnp.concatenate(probs, axis=0), v_ref[...])
    out = jnp.where(lane < DH, out[:T], out[T:])
    o_ref[...] = out
    low_ref[...] = out.astype(BF)


def att_bwd_kernel(
    q_ref, v_rows, kind_ref, dm_ref, o_ref, p_ref, k_ref, v_ref, t_ref, ka_ref,
    dq_ref, vec_ref, dkv_ref, dt_ref,
):
    T = q_ref.shape[0]
    W = k_ref.shape[0]
    blocks = W // T
    c = DH**-0.5
    q = q_ref[...]
    qc = ((q + v_rows[1:2, :]) * c).astype(BF)
    qp = ((q + v_rows[2:3, :]) * c).astype(BF)
    qt = (q + v_rows[3:4, :]) * c
    e0, e1 = v_rows[4:5, :], v_rows[5:6, :]
    lane = lax.broadcasted_iota(jnp.int32, (T, 128), 1)
    row = lax.broadcasted_iota(jnp.int32, (T, 128), 0)
    same = kind_ref[...] > 0.5
    flip = jnp.where(lane + row == T - 1, 1.0, 0.0).astype(BF)
    qpr = nn(flip, qp).astype(BF)
    dm = dm_ref[...]
    dmo = dm.astype(F32) * o_ref[...]
    zero = jnp.zeros_like(dm)
    stack = lambda parts: jnp.concatenate(parts, axis=0)
    mine = [lane < DH, lane >= DH]
    pick = lambda a: stack([jnp.where(m, a, zero) for m in mine])
    dms = pick(dm)
    delta = jnp.sum(
        stack([jnp.where(m, dmo, 0.0) for m in mine]), axis=1, keepdims=True
    )
    dp = nt(dms, v_ref[...])
    p = stack([p_ref[0], p_ref[1]])
    ds = (p.astype(F32) * (dp - delta)).astype(BF)
    dc = nn(ds, jnp.concatenate([k_ref[...], ka_ref[...]], axis=1))
    wide = []
    for h in range(2):
        back = nn(flip, ds[T * h : T * (h + 1)])
        turned = [
            pltpu.roll(back[:, 128 * b : 128 * b + 128], 0, 1, stride=1, stride_axis=0)
            for b in range(blocks)
        ]
        edge = jnp.zeros((T, 128), F32)
        tiles = [
            jnp.where(lane >= row, a, b).astype(BF)
            for a, b in zip(turned + [edge], [edge] + turned)
        ]
        wide.append(jnp.concatenate(tiles, axis=1))
    wide = stack(wide)
    dqp = nn(wide, t_ref[...])
    dkv_ref[0] = tn(pick(qc), ds).astype(BF)
    dkv_ref[1] = tn(dms, p).astype(BF)
    dt_ref[...] = tn(pick(qpr), wide).astype(BF)
    both = lambda a: jnp.where(mine[0], a[:T], a[T:])
    dc_low = both(dc[:, :128]).astype(BF).astype(F32)
    dp_low = nn(flip, both(dqp).astype(BF))
    one = both(jnp.broadcast_to(dc[:, 128:129], (2 * T, 128)))
    two = both(jnp.broadcast_to(dc[:, 132:133], (2 * T, 128)))
    same_sum, other_sum = jnp.where(same, one, two), jnp.where(same, two, one)
    dt = other_sum * e0 + same_sum * e1
    dq_ref[...] = (c * (dc_low + dp_low + dt)).astype(BF)
    total = lambda a: jnp.sum(a, axis=0, keepdims=True)
    rows = [c * total(dc_low), c * total(dp_low), c * total(dt), total(other_sum * qt), total(same_sum * qt)]
    vec_ref[...] = jnp.concatenate(rows + [jnp.zeros((3, 128), F32)], axis=0)


def att_fwd(q, rows, pen, kind, kv, t, ka):
    T, D = q.shape
    W = kv.shape[0]
    keys, values = (pl.BlockSpec((W, 128), lambda i, n=n: (0, i + n * D // 128)) for n in range(2))
    heads = D // DH
    col = lambda n: pl.BlockSpec((n, 128), lambda i: (0, i))
    fixed = lambda n: pl.BlockSpec((n, 128), lambda i: (0, 0))
    return pl.pallas_call(
        att_fwd_kernel,
        grid=(D // 128,),
        in_specs=[col(T), col(16), fixed(T), fixed(T), keys, values, col(W + T), fixed(W)],
        out_specs=[col(T), col(T), pl.BlockSpec((2, T, W), lambda i: (i, 0, 0))],
        out_shape=[
            jax.ShapeDtypeStruct((T, D), F32),
            jax.ShapeDtypeStruct((T, D), BF),
            jax.ShapeDtypeStruct((heads, T, W), BF),
        ],
        compiler_params=pltpu.CompilerParams(vmem_limit_bytes=60 * 2**20),
        cost_estimate=pl.CostEstimate(
            flops=2 * heads * T * W * 2048,
            bytes_accessed=2 * (3 * W * D + heads * T * W),
            transcendentals=heads * T * W,
        ),
        name="att_fwd",
    )(q, rows, pen, kind, kv, kv, t, ka)


def att_bwd(q, rows, kind, dm, o, p, kv, t, ka):
    T, D = q.shape
    W = kv.shape[0]
    keys, values = (pl.BlockSpec((W, 128), lambda i, n=n: (0, i + n * D // 128)) for n in range(2))
    heads = D // DH
    col = lambda n: pl.BlockSpec((n, 128), lambda i: (0, i))
    fixed = lambda n: pl.BlockSpec((n, 128), lambda i: (0, 0))
    return pl.pallas_call(
        att_bwd_kernel,
        grid=(D // 128,),
        in_specs=[
            col(T), col(16), fixed(T), col(T), col(T), pl.BlockSpec((2, T, W), lambda i: (i, 0, 0)),
            keys, values, col(W + T), fixed(W),
        ],
        out_specs=[
            col(T), col(8), pl.BlockSpec((2, 128, W), lambda i: (0, i, 0)),
            pl.BlockSpec((128, W + T), lambda i: (i, 0)),
        ],
        out_shape=[
            jax.ShapeDtypeStruct((T, D), BF),
            jax.ShapeDtypeStruct((8, D), F32),
            jax.ShapeDtypeStruct((2, D, W), BF),
            jax.ShapeDtypeStruct((D, W + T), BF),
        ],
        compiler_params=pltpu.CompilerParams(vmem_limit_bytes=60 * 2**20),
        cost_estimate=pl.CostEstimate(
            flops=2**20, bytes_accessed=2**20, transcendentals=0
        ),
        name="att_bwd",
    )(q, rows, kind, dm, o, p, kv, kv, t, ka)


def pack_rows(vectors, dn):
    counts = [v.size // dn for v in vectors]

    def kernel(*refs):
        out = refs[-1]
        at = 0
        for ref, n in zip(refs, counts):
            for j in range(n):
                if len(ref.shape) == 1:
                    out[at, :] = ref[pl.ds(j * dn, dn)].astype(F32)
                else:
                    out[at, :] = ref[j, :].astype(F32)
                at += 1

    return pl.pallas_call(
        kernel,
        out_shape=jax.ShapeDtypeStruct((sum(counts), dn), F32),
        name="pack_rows",
    )(*vectors)


def ffn_final(blocks, FF, D):
    count, _, dn = blocks.shape
    steps = FF // D
    per = count // steps
    ri, ru = FF // count, FF // 2 // count

    def kernel(b_ref, i_ref, u_ref):
        gi = jnp.concatenate([b_ref[k, :ri] for k in range(per)], axis=0)
        i_ref[...] = jnp.transpose(gi.astype(F32))
        for k in range(per):
            u_ref[ru * k : ru * (k + 1), :dn] = b_ref[k, ri : ri + ru].astype(F32)
            u_ref[ru * k : ru * (k + 1), dn:] = b_ref[k, ri + ru :].astype(F32)

    return pl.pallas_call(
        kernel,
        grid=(steps,),
        in_specs=[pl.BlockSpec((per, ri + 2 * ru, dn), lambda i: (i, 0, 0))],
        out_specs=[
            pl.BlockSpec((dn, D), lambda i: (0, i)), pl.BlockSpec((FF // 2 // steps, D), lambda i: (i, 0))
        ],
        out_shape=[
            jax.ShapeDtypeStruct((dn, FF), F32), jax.ShapeDtypeStruct((FF // 2, D), F32)
        ],
        cost_estimate=pl.CostEstimate(flops=2**33, bytes_accessed=8 * D * FF, transcendentals=0),
        name="ffn_final",
    )(blocks)


def split_cols(a, f, odd):
    h = a.shape[1] // 2
    q = h // 2
    own = jnp.where(f == 0, a[:, :h], a[:, h:])
    other = jnp.where(f == 0, a[:, h:], a[:, :h])
    swapped = jnp.concatenate([other[:, q:], other[:, :q]], axis=1)
    return jnp.concatenate([own, jnp.where(odd, swapped, other)], axis=1)


def merge_cols(a, f, odd):
    h = a.shape[1] // 2
    q = h // 2
    own, other = a[:, :h], a[:, h:]
    swapped = jnp.concatenate([other[:, q:], other[:, :q]], axis=1)
    other = jnp.where(odd, swapped, other)
    return jnp.where(
        f == 0, jnp.concatenate([own, other], axis=1), jnp.concatenate([other, own], axis=1)
    )


def swap_quarters(a, y, odd):
    h = a.shape[1] // 2
    q = h // 2
    a = jnp.where(y, jnp.concatenate([a[:, h:], a[:, :h]], axis=1), a)
    pairs = jnp.concatenate([a[:, q:h], a[:, :q], a[:, h + q :], a[:, h : h + q]], axis=1)
    return jnp.where(odd, pairs, a)


def middle_swap(a):
    q = a.shape[1] // 4
    return jnp.concatenate([a[:, :q], a[:, 2 * q : 3 * q], a[:, q : 2 * q], a[:, 3 * q :]], axis=1)


def split_quarters(a, f, y, odd):
    h = a.shape[1] // 2
    own = jnp.where(f == 0, a[:, :h], a[:, h:])
    other = jnp.where(f == 0, a[:, h:], a[:, :h])
    return own, middle_swap(swap_quarters(other, y, odd))


def merge_quarters(a, f, y, odd):
    h = a.shape[1] // 2
    own, other = a[:, :h], swap_quarters(middle_swap(a[:, h:]), y, odd)
    return jnp.where(
        f == 0, jnp.concatenate([own, other], axis=1), jnp.concatenate([other, own], axis=1)
    )


def norm_stats(res):
    center = res - jnp.mean(res, axis=1, keepdims=True)
    rstd = lax.rsqrt(jnp.mean(center * center, axis=1, keepdims=True) + EPS)
    return center * rstd, rstd


def norm_back(g, gain, n, rstd):
    gg = g * gain
    return (gg - jnp.mean(gg, axis=1, keepdims=True) - n * jnp.mean(gg * n, axis=1, keepdims=True)) * rstd


def row_sum(a):
    return jnp.sum(a, axis=0, keepdims=True)


GELU_A = 0.7978845608028654
GELU_B = 0.044715


def ffn_specs(T, D, FF):
    steps = FF // D
    half = steps // 2
    c = FF // steps
    q = D // 8

    def chunk_at(j, s):
        other = half * (1 - s[0]) + (s[2] ^ jnp.maximum(j - half, 0))
        return jnp.where(j < half, half * s[0] + j, other)

    col = lambda j, s: (0, chunk_at(j, s))
    whole = lambda *shape: pl.BlockSpec(shape, lambda j, s: (0,) * len(shape))
    inner = [pl.BlockSpec((4 * q, c), col)] + [pl.BlockSpec((q, c), col)] * 4
    outer = [pl.BlockSpec((c, D), lambda j, s: (jnp.minimum(j, half - 1), 0))]
    outer += [whole(c // 2, D)] * 4
    proj = [whole(4 * q, D), whole(2 * q, D), whole(2 * q, D)]
    return steps, half, c, chunk_at, col, whole, inner, outer, proj


def outer_chunk(j, half, odd, refs):
    last = j > half
    a = jnp.where(last, refs[2][...], refs[1][...])
    b = jnp.where(last, refs[4][...], refs[3][...])
    pair = jnp.concatenate([jnp.where(odd, b, a), jnp.where(odd, a, b)], axis=0)
    return jnp.where(j < half, refs[0][...], pair)


def rows_of(refs):
    return jnp.concatenate([r[...] for r in refs], axis=0)


def inner_bias_chunk(b, half, vec_ref, D):
    rows = [vec_ref[pl.ds(12 + 2 * (b % half) + n, 1), :] for n in range(2)]
    parts = [jnp.where(b < half, r[:, : D // 2], r[:, D // 2 :]) for r in rows]
    return jnp.concatenate(parts, axis=1)


def gelu_tanh(u):
    return jnp.tanh(GELU_A * (u + GELU_B * u * u * u))


def first_norm(x, mixed, vec_ref, w, f, odd):
    attn = nn(split_cols(mixed, f, odd).astype(BF), w) + vec_ref[6:7, :]
    n1, rstd = norm_stats(x.astype(F32) + attn)
    return n1, rstd, n1 * vec_ref[7:8, :] + vec_ref[8:9, :]


def ffn_fwd(place, x, mixed, cot, vecs, o_parts, i_parts, u_parts, FF):
    T, D = x.shape
    steps, half, c, chunk_at, col, whole, inner, outer, proj = ffn_specs(T, D, FF)

    def kernel(s_ref, x_ref, m_ref, g_ref, v_ref, *refs):
        o_refs, i_refs, u_refs = refs[:3], refs[3:8], refs[8:13]
        nl_ref, act_ref, pre_ref, res_ref, dr_ref, do_ref, n1_ref, rs_ref, gv_ref = refs[13:22]
        np_ref, acc_ref, nf_ref = refs[22:]
        j = pl.program_id(0)
        f, odd, y = s_ref[0], s_ref[1] == 1, s_ref[2] == 1

        @pl.when(j == 0)
        def _():
            n1, rstd, normed = first_norm(x_ref[...], m_ref[...], v_ref, rows_of(o_refs), f, odd)
            n1_ref[...] = n1
            rs_ref[...] = jnp.broadcast_to(rstd, (T, 128))
            nf_ref[...] = normed
            nl_ref[...] = normed.astype(BF)
            np_ref[...] = jnp.concatenate(split_quarters(normed, f, y, odd), axis=1).astype(BF)
            acc_ref[...] = jnp.zeros_like(acc_ref)

        bias = inner_bias_chunk(chunk_at(j, s_ref), half, v_ref, D)
        pre = nn(np_ref[...], rows_of(i_refs)) + bias
        pre_ref[...] = pre
        act = (0.5 * pre * (1.0 + gelu_tanh(pre))).astype(BF)
        act_ref[...] = act
        acc_ref[...] += nn(act, outer_chunk(j, half, odd, u_refs))

        @pl.when(j == steps - 1)
        def _():
            n2, rstd = norm_stats(nf_ref[...] + (acc_ref[...] + v_ref[9:10, :]))
            g = g_ref[...].astype(F32)
            res_ref[...] = (n2 * v_ref[10:11, :] + v_ref[11:12, :]).astype(BF)
            d = norm_back(g, v_ref[10:11, :], n2, rstd)
            dr_ref[...] = d
            do = d.astype(BF)
            do_ref[...] = do
            gv_ref[0:1, :] = row_sum(g * n2)
            gv_ref[1:2, :] = row_sum(g)
            gv_ref[2:3, :] = row_sum(do.astype(F32))
            gv_ref[3:8, :] = jnp.zeros((5, D), F32)

    f32 = lambda *shape: jax.ShapeDtypeStruct(shape, F32)
    low = lambda *shape: jax.ShapeDtypeStruct(shape, BF)
    tok = whole(T, D)
    chunk = pl.BlockSpec((T, c), col)
    return pl.pallas_call(
        kernel,
        grid_spec=pltpu.PrefetchScalarGridSpec(
            num_scalar_prefetch=1,
            grid=(steps,),
            in_specs=[tok, tok, tok, whole(16, D)] + proj + inner + outer,
            out_specs=[tok, chunk, chunk, tok, tok, tok, tok, whole(T, 128), whole(8, D)],
            scratch_shapes=[
                pltpu.VMEM((T, D), BF), pltpu.VMEM((T, D), F32), pltpu.VMEM((T, D), F32)
            ],
        ),
        out_shape=[
            low(T, D), low(T, FF), f32(T, FF), low(T, D), f32(T, D), low(T, D), f32(T, D),
            f32(T, 128), f32(8, D),
        ],
        compiler_params=pltpu.CompilerParams(vmem_limit_bytes=60 * 2**20),
        cost_estimate=pl.CostEstimate(
            flops=4 * T * D * FF, bytes_accessed=4 * D * FF, transcendentals=T * FF
        ),
        name="ffn_fwd",
    )(place, x, mixed, cot, vecs, *o_parts, *i_parts, *u_parts)


def ffn_bwd(
    place, count, pre, act, normed, d_outer, d_outer_got, d_res2, n1, rstd1, mixed_got, x_got,
    vecs, o_parts, i_parts, u_parts,
):
    T, FF = pre.shape
    D = d_outer.shape[1]
    dn = D // 2
    steps, half, c, chunk_at, col, whole, inner, outer, proj = ffn_specs(T, D, FF)
    ri, ru = FF // count, FF // 2 // count

    def kernel(s_ref, pre_ref, act_ref, nl_ref, do_ref, dog_ref, dr_ref, n1_ref, rs_ref, mg_ref, xg_ref, v_ref, *refs):
        o_refs, i_refs, u_refs = refs[:3], refs[3:8], refs[8:13]
        pay_ref, d1_ref, da_ref, dm_ref, gv_ref = refs[13:18]
        acc_ref, ib_ref, np_ref, nf_ref, do_both = refs[18:]
        j = pl.program_id(0)
        f, odd, y = s_ref[0], s_ref[1] == 1, s_ref[2] == 1

        @pl.when(j == 0)
        def _():
            acc_ref[...] = jnp.zeros_like(acc_ref)
            theirs = first_norm(xg_ref[...], mg_ref[...], v_ref, rows_of(o_refs), f, odd)[2]
            own, other = split_quarters(theirs, f, y, odd)
            np_ref[...] = jnp.concatenate([own, other], axis=1).astype(BF)
            nl = nl_ref[...]
            nf_ref[:T] = jnp.where(f == 0, nl[:, :dn], nl[:, dn:])
            nf_ref[T:] = own.astype(BF)
            do_both[:T] = do_ref[...]
            do_both[T:] = dog_ref[...]

        b = chunk_at(j, s_ref)
        w = rows_of(i_refs)
        pre_got = nn(np_ref[...], w) + inner_bias_chunk(b, half, v_ref, D)
        u = jnp.concatenate([pre_ref[...], pre_got], axis=0)
        t = gelu_tanh(u)
        slope = 0.5 * (1.0 + t) + 0.5 * u * (1.0 - t * t) * (GELU_A * (1.0 + 3.0 * GELU_B * u * u))
        di = (nt(do_both[...], outer_chunk(j, half, odd, u_refs)) * slope).astype(BF)
        ib_ref[pl.ds(b, 1), :] = row_sum(di[:T].astype(F32))
        acc_ref[...] += nt(di[:T], w)
        gi = tn(di, nf_ref[...]).astype(BF)
        for k in range(c // ri):
            pay_ref[b * (c // ri) + k, :ri] = gi[ri * k : ri * (k + 1)]

        @pl.when(j < half)
        def _():
            act_got = (0.5 * u[T:] * (1.0 + t[T:])).astype(BF)
            gu = tn(jnp.concatenate([act_ref[...], act_got], axis=0), do_both[...]).astype(BF)
            for k in range(c // ru):
                pay_ref[j * (c // ru) + k, ri : ri + ru] = gu[ru * k : ru * (k + 1), :dn]
                pay_ref[j * (c // ru) + k, ri + ru :] = gu[ru * k : ru * (k + 1), dn:]

        @pl.when(j == steps - 1)
        def _():
            d_normed = dr_ref[...] + merge_quarters(acc_ref[...], f, y, odd)
            n1 = n1_ref[...]
            d1 = norm_back(d_normed, v_ref[7:8, :], n1, rs_ref[:, 0:1])
            d1_ref[...] = d1
            da = d1.astype(BF)
            da_ref[...] = da
            dm = merge_cols(nt(da, rows_of(o_refs)), f, odd)
            dm_ref[...] = dm.astype(BF)
            gv_ref[0:1, :] = row_sum(d_normed * n1)
            gv_ref[1:2, :] = row_sum(d_normed)
            gv_ref[2:3, :] = row_sum(da.astype(F32))
            gv_ref[3:4, :] = row_sum(dm.astype(BF).astype(F32))
            for n in range(2 * half):
                at = slice(0, dn) if n % 2 == 0 else slice(dn, D)
                gv_ref[4 + n : 5 + n, :dn] = ib_ref[n // 2 : n // 2 + 1, at]
                gv_ref[4 + n : 5 + n, dn:] = ib_ref[half + n // 2 : half + n // 2 + 1, at]

    f32 = lambda *shape: jax.ShapeDtypeStruct(shape, F32)
    low = lambda *shape: jax.ShapeDtypeStruct(shape, BF)
    tok = whole(T, D)
    chunk = pl.BlockSpec((T, c), col)
    return pl.pallas_call(
        kernel,
        grid_spec=pltpu.PrefetchScalarGridSpec(
            num_scalar_prefetch=1,
            grid=(steps,),
            in_specs=[chunk, chunk] + [tok] * 5 + [whole(T, 128), tok, tok, whole(16, D)]
            + proj + inner + outer,
            out_specs=[whole(count, ri + 2 * ru, dn), tok, tok, tok, whole(8, D)],
            scratch_shapes=[
                pltpu.VMEM((T, D), F32), pltpu.VMEM((steps, c), F32), pltpu.VMEM((T, D), BF),
                pltpu.VMEM((2 * T, dn), BF), pltpu.VMEM((2 * T, D), BF),
            ],
        ),
        out_shape=[low(count, ri + 2 * ru, dn), f32(T, D), low(T, D), low(T, D), f32(8, D)],
        compiler_params=pltpu.CompilerParams(vmem_limit_bytes=60 * 2**20),
        cost_estimate=pl.CostEstimate(
            flops=14 * T * D * FF, bytes_accessed=6 * D * FF, transcendentals=2 * T * FF
        ),
        name="ffn_bwd",
    )(
        place, pre, act, normed, d_outer, d_outer_got, d_res2, n1, rstd1, mixed_got, x_got, vecs,
        *o_parts, *i_parts, *u_parts,
    )


def key_grads(place, dkv, x_win):
    _, D, W = dkv.shape
    h = D // 2

    def kernel(s_ref, kv_ref, x_ref, send_ref, keep_ref):
        g = nn(kv_ref[0], x_ref[...]).astype(BF)

        @pl.when(pl.program_id(0) < 2)
        def _():
            send_ref[...] = g

        @pl.when(pl.program_id(0) >= 2)
        def _():
            keep_ref[...] = g

    return pl.pallas_call(
        kernel,
        grid_spec=pltpu.PrefetchScalarGridSpec(
            num_scalar_prefetch=1,
            grid=(4,),
            in_specs=[
                pl.BlockSpec((1, h, W), lambda i, s: (jnp.where(i < 2, 1 - s[1], s[1]), i % 2, 0)),
                pl.BlockSpec((W, D), lambda i, s: (0, 0)),
            ],
            out_specs=[
                pl.BlockSpec((h, D), lambda i, s: (jnp.minimum(i, 1), 0)),
                pl.BlockSpec((h, D), lambda i, s: (jnp.maximum(i - 2, 0), 0)),
            ],
        ),
        out_shape=[jax.ShapeDtypeStruct((D, D), BF)] * 2,
        compiler_params=pltpu.CompilerParams(vmem_limit_bytes=60 * 2**20),
        cost_estimate=pl.CostEstimate(
            flops=4 * D * D * W, bytes_accessed=6 * D * W, transcendentals=0
        ),
        name="key_grads",
    )(place, dkv, x_win)


def position_grads(place, d_table, sinus, vectors):
    D, WT = d_table.shape
    h = D // 2

    def kernel(s_ref, t_ref, x_ref, *refs):
        v_refs, (send_ref, keep_ref) = refs[:-2], refs[-2:]
        i = pl.program_id(0)
        g = nn(t_ref[...], x_ref[...]).astype(BF)
        small = jnp.concatenate([r[...] for r in v_refs], axis=0)
        small = jnp.concatenate([small, jnp.zeros((64 - small.shape[0], D), F32)], axis=0)
        even = jnp.where(i == 0, 1 - s_ref[1], s_ref[1]) == 0
        small = jnp.where(even, small, 0.0).astype(BF)

        @pl.when(i == 0)
        def _():
            send_ref[:h] = g
            send_ref[h:] = small

        @pl.when(i == 1)
        def _():
            keep_ref[:h] = g
            keep_ref[h:] = small

    whole = lambda *shape: pl.BlockSpec(shape, lambda i, s: (0,) * len(shape))
    return pl.pallas_call(
        kernel,
        grid_spec=pltpu.PrefetchScalarGridSpec(
            num_scalar_prefetch=1,
            grid=(2,),
            in_specs=[
                pl.BlockSpec((h, WT), lambda i, s: (jnp.where(i == 0, 1 - s[1], s[1]), 0)),
                whole(WT, D),
            ]
            + [whole(8, D)] * len(vectors),
            out_specs=[whole(h + 64, D)] * 2,
        ),
        out_shape=[jax.ShapeDtypeStruct((h + 64, D), BF)] * 2,
        compiler_params=pltpu.CompilerParams(vmem_limit_bytes=60 * 2**20),
        cost_estimate=pl.CostEstimate(
            flops=2 * D * D * WT, bytes_accessed=4 * D * WT, transcendentals=0
        ),
        name="position_grads",
    )(place, d_table, sinus, *vectors)


def hidden_grads(place, dkv, k_own, k_other, v_own, v_other, count, reach):
    D2, W = dkv.shape
    D = D2 // 2
    h = D // 2
    T = 128
    blocks = W // T

    def kernel(s_ref, a_ref, b_ref, k0, k1, v0, v1, send_ref, keep_ref):
        s = pl.program_id(0)
        odd = s_ref[1] == 1
        x = jnp.concatenate([a_ref[...], b_ref[...]], axis=1)
        for at, k, v in ((s_ref[0], k0, v0), (1 - s_ref[0], k1, v1)):
            g = nn(jnp.concatenate([k[...], v[...]], axis=1), x).astype(BF)
            parts = []
            for n in range(2):
                rel = 2 * s + n - s_ref[3] + reach
                part = g[:, T * n : T * (n + 1)]
                parts.append(jnp.where((rel >= 0) & (rel < blocks), part, jnp.zeros_like(part)))
            rows = pl.ds(pl.multiple_of(at * h, h), h)
            send_ref[0, rows, :] = jnp.where(odd, parts[0], parts[1])
            keep_ref[0, rows, :] = jnp.where(odd, parts[1], parts[0])

    whole = pl.BlockSpec((h, D), lambda s, p: (0, 0))
    block = lambda n: pl.BlockSpec(
        (D2, T), lambda s, p: (0, jnp.clip(2 * s + n - p[3] + reach, 0, blocks - 1))
    )
    return pl.pallas_call(
        kernel,
        grid_spec=pltpu.PrefetchScalarGridSpec(
            num_scalar_prefetch=1,
            grid=(count // 2,),
            in_specs=[block(0), block(1), whole, whole, whole, whole],
            out_specs=[pl.BlockSpec((1, D, T), lambda s, p: (s, 0, 0))] * 2,
        ),
        out_shape=[jax.ShapeDtypeStruct((count // 2, D, T), BF)] * 2,
        compiler_params=pltpu.CompilerParams(vmem_limit_bytes=60 * 2**20),
        cost_estimate=pl.CostEstimate(flops=2**20, bytes_accessed=2**20, transcendentals=0),
        name="hidden_grads",
    )(place, dkv, dkv, k_own, k_other, v_own, v_other)


def input_grads(place, d_res1, dq, q_own, q_other, d_hid):
    T, D = d_res1.shape

    def kernel(s_ref, r_ref, dq_ref, q0, q1, h_ref, out_ref):
        own, other = nt(dq_ref[...], q0[...]), nt(dq_ref[...], q1[...])
        first = s_ref[0] == 0
        g = jnp.concatenate([jnp.where(first, own, other), jnp.where(first, other, own)], axis=1)
        out_ref[...] = r_ref[...] + g + jnp.transpose(h_ref[...].astype(F32))

    whole = lambda a: pl.BlockSpec(a.shape, lambda i, s: (0, 0))
    args = (d_res1, dq, q_own, q_other, d_hid)
    return pl.pallas_call(
        kernel,
        grid_spec=pltpu.PrefetchScalarGridSpec(
            num_scalar_prefetch=1,
            grid=(1,),
            in_specs=[whole(a) for a in args],
            out_specs=whole(d_res1),
        ),
        out_shape=jax.ShapeDtypeStruct((T, D), F32),
        cost_estimate=pl.CostEstimate(
            flops=2**32, bytes_accessed=2**24, transcendentals=0
        ),
        name="input_grads",
    )(place, *args)


def grad_final(place, one, two, one_got, two_got, D, blocks):
    dn = one.shape[1]
    h = D // 2
    p, q = one.shape[0] // blocks, two.shape[0] // blocks

    def kernel(s_ref, a_ref, b_ref, c_ref, d_ref, k_ref, v_ref, p_ref, o_ref, q_ref, small_ref):
        odd = s_ref[1] == 1

        def rows(x_ref, y_ref):
            x, y = x_ref[...].astype(F32), y_ref[...].astype(F32)
            parts = []
            for n in range(blocks):
                parts += [x[p * n : p * (n + 1)], y[q * n : q * (n + 1)]]
            return jnp.concatenate(parts, axis=0)

        mine, other = rows(a_ref, b_ref), rows(c_ref, d_ref)
        low, high = jnp.where(odd, other, mine), jnp.where(odd, mine, other)
        k_ref[...] = jnp.transpose(low[:D])
        v_ref[...] = jnp.transpose(high[:D])
        p_ref[...] = jnp.transpose(jnp.concatenate([low[D : D + h], high[D : D + h]], axis=0))
        small_ref[...] = low[D + h : D + h + 64]
        o_ref[...] = jnp.transpose(low[D + h + 64 :])
        q_ref[...] = jnp.transpose(high[D + h + 64 :])

    lanes = lambda n: pl.BlockSpec((n, 128), lambda i, s: (0, i))
    out = pl.BlockSpec((128, D), lambda i, s: (i, 0))
    return pl.pallas_call(
        kernel,
        grid_spec=pltpu.PrefetchScalarGridSpec(
            num_scalar_prefetch=1,
            grid=(dn // 128,),
            in_specs=[lanes(a.shape[0]) for a in (one, two, one_got, two_got)],
            out_specs=[out] * 5 + [lanes(64)],
        ),
        out_shape=[jax.ShapeDtypeStruct((dn, D), F32)] * 5 + [jax.ShapeDtypeStruct((64, dn), F32)],
        compiler_params=pltpu.CompilerParams(vmem_limit_bytes=60 * 2**20),
        name="grad_final",
    )(place, one, two, one_got, two_got)


def unpack_rows(s):
    dn = s.shape[1]
    singles = (19, 0, 1, 2, 18, 16, 17, 10, 8, 9)

    def kernel(s_ref, *outs):
        for i, out in zip(singles, outs):
            out[...] = s_ref[i, :]
        outs[-2][...] = s_ref[3:5, :]
        for j in range(4):
            outs[-1][pl.ds(j * dn, dn)] = s_ref[20 + j, :]

    shapes = [(dn,)] * len(singles) + [(2, dn), (4 * dn,)]
    return pl.pallas_call(
        kernel,
        out_shape=[jax.ShapeDtypeStruct(a, F32) for a in shapes],
        name="unpack_rows",
    )(s)


def layer_norm(residual, gain_vec, bias_vec):
    center = residual - jnp.mean(residual, axis=-1, keepdims=True)
    spread = jnp.mean(center * center, axis=-1, keepdims=True)
    return center * lax.rsqrt(spread + EPS) * gain_vec + bias_vec


def sinus_rows(first, count, width):
    half = width // 2
    freq = jnp.power(10000.0, -jnp.arange(half, dtype=F32) / half)
    coarse = (first - 64 * jnp.arange(count // 64)).astype(F32)[:, None] * freq
    fine = jnp.arange(64).astype(F32)[:, None] * freq
    sa, ca = jnp.sin(coarse)[:, None], jnp.cos(coarse)[:, None]
    sb, cb = jnp.sin(fine)[None], jnp.cos(fine)[None]
    both = jnp.concatenate([sa * cb - ca * sb, ca * cb + sa * sb], axis=2)
    return both.astype(BF).reshape(count, width)


class Shards:
    def __init__(self):
        self.parts = lax.axis_size("fsdp")
        self.pair = self.parts == 2
        self.f = lax.axis_index("fsdp")
        self.ctx = lax.axis_index("ctx")
        self.count = lax.axis_size("ctx")
        self.bits = self.count.bit_length() - 1
        self.swap = [(0, 1), (1, 0)]

    def bit(self, k):
        return (self.ctx >> k) & 1

    def flip(self, a, k):
        return lax.ppermute(a, "ctx", [(i, i ^ (1 << k)) for i in range(self.count)])

    def trade(self, a):
        return lax.ppermute(a, "fsdp", self.swap)

    def order(self, mine, other, at):
        return jnp.where(at == 0, mine, other), jnp.where(at == 0, other, mine)

    def fetch_half(self, w):
        half = w.shape[0] // 2
        return self.trade(lax.dynamic_slice_in_dim(w, self.bit(0) * half, half, 0))

    def fetch_quarter(self, w):
        n = w.shape[0] // 4
        return self.trade(lax.dynamic_slice_in_dim(w, (self.ctx % 4) * n, n, 0))

    def pieces(self, got, y):
        return got, y, self.flip(got, 0), self.flip(y, 0)

    def full_small(self, w):
        if not self.pair:
            return lax.all_gather(w, "fsdp", axis=0, tiled=False)
        return jnp.stack(self.order(w, self.trade(w), self.f))

    def own(self, a, axis, other=False):
        n = a.shape[axis] // self.parts
        at = (1 - self.f) if other else self.f
        return lax.dynamic_slice_in_dim(a, at * n, n, axis)

    def window(self, block, planes):
        y = self.flip(block, 1)
        self.first_hop = y
        pair = jnp.stack(self.order(block, y, self.bit(1)))
        up = down = pair
        groups = [(pair[None], self.flip(pair[None], 0))]
        for _ in range(planes):
            up = lax.ppermute(up, "ctx", [(i, i + 4) for i in range(self.count - 4)])
            down = lax.ppermute(down, "ctx", [(i + 4, i) for i in range(self.count - 4)])
            both = jnp.stack([up, down])
            groups.append((both, self.flip(both, 0)))
        self.last_hop = both
        groups = [jnp.stack(self.order(a, b, self.bit(0)), axis=2) for a, b in groups]
        planes = [g[0] for g in groups[:0:-1]] + [groups[0][0]] + [g[1] for g in groups[1:]]
        return jnp.concatenate(planes, axis=0).reshape((-1,) + block.shape)

    def sides(self, a, k, axis):
        keep = lax.dynamic_index_in_dim(a, self.bit(k), axis, keepdims=False)
        return keep, lax.dynamic_index_in_dim(a, 1 - self.bit(k), axis, keepdims=False)

    def add(self, a, b):
        return (a.astype(F32) + b.astype(F32)).astype(BF)

    def halve(self, a, k, axis):
        keep, send = self.sides(a, k, axis)
        return self.add(keep, self.flip(send, k))

    def halve_cols(self, low, high):
        keep, send = self.order(low, high, self.bit(0))
        return (keep.astype(F32) + self.flip(send.astype(BF), 0).astype(F32)).astype(BF)

    def double(self, a, k, axis):
        return jnp.stack(self.order(a, self.flip(a, k), self.bit(k)), axis=axis)

    def spread(self, a):
        return a.reshape((2,) * self.bits + a.shape[1:])


def per_device(
    hidden_in,
    segment_ids,
    token_types,
    out_grad,
    query_proj,
    key_proj,
    value_proj,
    value_bias,
    content_bias,
    position_bias,
    type_bias,
    type_embed,
    position_proj,
    output_proj,
    output_bias,
    attn_gain,
    attn_shift,
    inner_proj,
    inner_bias,
    outer_proj,
    outer_bias,
    ffn_gain,
    ffn_shift,
):
    sh = Shards()
    hidden = hidden_in[0]
    cotangent = out_grad[0].astype(F32)
    T, D = hidden.shape
    C = sh.count
    ctx = sh.ctx
    L = T * C
    R = C // 2
    NB = 2 * R + 1
    W = NB * T
    dn = D // sh.parts
    r = dn // C

    lane = jnp.arange(128)[None, :]
    in_seg = (lane >= 8) & (lane < 16)
    seg_own = segment_ids[0][:, None]
    kind_own = token_types[0][:, None]
    kaug_own = jnp.where(
        lane < 4, kind_own == 1, jnp.where(lane < 8, kind_own == 0, in_seg & (lane - 8 == seg_own))
    ).astype(BF)
    pen = jnp.where(in_seg & (lane - 8 != seg_own), -BIG, 0.0).astype(F32)
    kind_q = jnp.broadcast_to(kind_own, (T, 128)).astype(F32)

    around = sh.window(jnp.concatenate([hidden, kaug_own], axis=1), R // 4)
    around = lax.dynamic_slice_in_dim(around, ctx % 4, NB, 0)
    x_win = around[:, :, :D].reshape(W, D)
    at = jnp.arange(NB) + ctx - R
    valid = ((at >= 0) & (at < C))[:, None, None]
    kaug = jnp.where(valid, around[:, :, D:], (lane[None] == 15).astype(BF)).reshape(W, 128)

    vectors = (
        value_bias, content_bias, position_bias, type_bias, type_embed, output_bias,
        attn_gain, attn_shift, outer_bias, ffn_gain, ffn_shift, inner_bias,
    )
    small = pack_rows(vectors, dn)
    small_full = sh.full_small(small)
    if sh.pair:
        odd = sh.bit(0) == 1
        got_a = sh.trade(jnp.where(odd, value_proj, position_proj))
        got_b = sh.trade(jnp.where(odd, key_proj, query_proj))
        got_o = sh.fetch_half(output_proj)
        got_a, got_b, got_o, i_sh, u_sh, small_full, _ = lax.optimization_barrier(
            (got_a, got_b, got_o, inner_proj, outer_proj, small_full, sh.last_hop)
        )
        other_p, other_v = sh.order(got_a, sh.flip(got_a, 0), sh.bit(0))
        other_q, other_k = sh.order(got_b, sh.flip(got_b, 0), sh.bit(0))
        p_full, q_full = (
            jnp.concatenate(sh.order(w, g, sh.f), axis=0)
            for w, g in ((position_proj, other_p), (query_proj, other_q))
        )
        own, other = (
            jnp.concatenate(a, axis=1) for a in ((key_proj, value_proj), (other_k, other_v))
        )
        kv_full = jnp.concatenate(sh.order(own, other, sh.f), axis=0)
        flip_o = sh.flip(got_o, 0)
        i_got, u_got = sh.fetch_quarter(i_sh), sh.fetch_quarter(u_sh)
    else:
        p_full, k_full, v_full, q_full, o_full, inner_full, outer_full = (
            lax.all_gather(w, "fsdp", axis=0, tiled=True)
            for w in (
                position_proj, key_proj, value_proj, query_proj, output_proj, inner_proj, outer_proj
            )
        )
        kv_full = jnp.concatenate([k_full, v_full], axis=1)

    vecs = jnp.concatenate([small_full[i] for i in range(sh.parts)], axis=1)

    q_lin = nn(hidden, q_full)
    if sh.pair:
        i_got, x_win = lax.optimization_barrier((i_got, x_win))
    kv_bias = jnp.concatenate([jnp.zeros((D,), F32), vecs[0]])
    key_values = (nn(x_win, kv_full) + kv_bias).astype(BF)
    sinus = lax.optimization_barrier(sinus_rows(T + R * T - 1, W + T, D))
    table = nn(sinus, p_full).astype(BF)

    if sh.pair:
        i_y = sh.flip(i_got, 1)
        u_got, key_values = lax.optimization_barrier((u_got, key_values))
        u_y = sh.flip(u_got, 1)
    mixed_f, mixed_low, probs = att_fwd(q_lin, vecs, pen, kind_q, key_values, table, kaug)
    if sh.pair:
        place = jnp.stack([sh.f, sh.bit(0), sh.bit(1), ctx])
        mixed_f, mixed_low, hid, fetched = lax.optimization_barrier(
            (mixed_f, mixed_low, hidden, (i_got, i_y, u_got, u_y))
        )
        hidden_got = sh.trade(hid)
        parts = (
            (output_proj, got_o, flip_o),
            (inner_proj,) + sh.pieces(*fetched[:2]),
            (outer_proj,) + sh.pieces(*fetched[2:]),
        )
        FF = inner_proj.shape[1]
        mixed_got = sh.trade(mixed_low)
        normed_low, activ_low, pre, outcome, d_res2, d_outer, n1, rstd1, vec_a = ffn_fwd(
            place, hidden, mixed_f, out_grad[0], vecs, *parts, FF
        )
        ffn, d_res1, d_attn, d_mixed, vec_b = ffn_bwd(
            place, C, pre, activ_low, normed_low, d_outer, sh.trade(d_outer), d_res2, n1, rstd1,
            mixed_got, hidden_got, vecs, *parts,
        )
    else:
        attn_out = nn(mixed_low, o_full) + vecs[6]
        normed, first_pull = jax.vjp(layer_norm, hidden.astype(F32) + attn_out, vecs[7], vecs[8])
        normed_low = normed.astype(BF)
        inner_pre = nn(normed_low, inner_full) + vecs[12:].reshape(-1, sh.parts, dn).transpose(1, 0, 2).reshape(-1)
        activated, gelu_pull = jax.vjp(partial(jax.nn.gelu, approximate=True), inner_pre)
        activ_low = activated.astype(BF)
        outer_out = nn(activ_low, outer_full) + vecs[9]
        outcome, second_pull = jax.vjp(layer_norm, normed + outer_out, vecs[10], vecs[11])
        d_res2, grad_ffn_gain, grad_ffn_shift = second_pull(cotangent)
        d_outer = d_res2.astype(BF)
        grad_outer_bias = jnp.sum(d_outer.astype(F32), axis=0)
        d_inner = gelu_pull(nt(d_outer, outer_full))[0].astype(BF)
        grad_inner_bias = jnp.sum(d_inner.astype(F32), axis=0)
        d_normed = d_res2 + nt(d_inner, inner_full)
        d_res1, grad_attn_gain, grad_attn_shift = first_pull(d_normed)
        d_attn = d_res1.astype(BF)
        grad_output_bias = jnp.sum(d_attn.astype(F32), axis=0)
        d_mixed = nt(d_attn, o_full).astype(BF)
        vec_a = jnp.stack(
            [grad_ffn_gain, grad_ffn_shift, grad_outer_bias] + [jnp.zeros((D,), F32)] * 5
        )
        ib = grad_inner_bias.reshape(sh.parts, -1, dn).transpose(1, 0, 2).reshape(-1, D)
        vec_b = jnp.concatenate(
            [
                jnp.stack(
                    [
                        grad_attn_gain, grad_attn_shift, grad_output_bias,
                        jnp.sum(d_mixed.astype(F32), axis=0),
                    ]
                ),
                ib,
            ],
            axis=0,
        )
    if sh.pair:
        d_attn_got = sh.trade(d_attn)
    dq, att_vec, dkv, d_table = att_bwd(
        q_lin, vecs, kind_q, d_mixed, mixed_f, probs, key_values, table, kaug
    )
    if sh.pair:
        dq_got = sh.trade(dq)
        ffn = lax.psum_scatter(ffn, "ctx", scatter_dimension=0, tiled=False)

        send, keep = hidden_grads(
            place, dkv.reshape(2 * D, W), key_proj, other_k, value_proj, other_v, C, R
        )
        got = sh.flip(send, 0)
        dkv, _ = lax.optimization_barrier((dkv, send))

        send_w, keep_w = key_grads(place, dkv, x_win)
        send_w, keep_w, got = lax.optimization_barrier((send_w, keep_w, got))
        d_hid = sh.add(keep, got).reshape((2,) * (sh.bits - 1) + (D, T))
        keep, send = sh.sides(d_hid, 1, sh.bits - 2)
        got = sh.flip(send, 1)
        got_w = sh.flip(send_w, 0)
        d_table, _ = lax.optimization_barrier((d_table, send))
        send_p, keep_p = position_grads(place, d_table, sinus, (att_vec, vec_a, vec_b))
        send_p, keep_p, got_w = lax.optimization_barrier((send_p, keep_p, got_w))
        whole = jnp.concatenate(
            [sh.add(keep_w, got_w), sh.add(keep_p, sh.flip(send_p, 0))], axis=0
        )
        keep_w, send_w = sh.order(whole[:, :dn], whole[:, dn:], sh.f)
        got_x = sh.trade(send_w)
        go, gq = (
            tn(
                jnp.concatenate([b, b_got], axis=0),
                jnp.concatenate([sh.own(a, 1), sh.own(a_got, 1)], axis=0),
            )
            for a, a_got, b, b_got in (
                (mixed_low, mixed_got, d_attn, d_attn_got), (hidden, hidden_got, dq, dq_got)
            )
        )
        mine = sh.halve_cols(go, gq)
        d_hid = sh.add(keep, got)
        got_x, d_hid, mine, ffn = lax.optimization_barrier((got_x, d_hid, mine, ffn))
        ffn = lax.all_gather(ffn, "ctx", axis=0, tiled=False)
        grads = jnp.concatenate([sh.add(keep_w, got_x), mine], axis=0)
        grads = grads.reshape((2,) * (sh.bits - 1) + (-1, dn))
        for k in range(1, sh.bits):
            grads = sh.halve(grads, k, grads.ndim - 3)
            if k + 2 < sh.bits:
                d_hid = sh.halve(d_hid, k + 1, d_hid.ndim - 3)
                grads, d_hid = lax.optimization_barrier((grads, d_hid))
        n = grads.shape[0]
        cut = (n // 2 + 15) // 16 * 16
        one, two = grads[:cut], grads[cut:]
        highs = list(reversed(range(2, sh.bits)))
        for i, (k, other) in enumerate(zip(highs + [1], [1] + highs)):
            one = sh.double(one, k, one.ndim - 2)
            two = sh.double(two, other, 0 if i == 0 else i - 1)
            if i == 0:
                one, two, d_hid, ffn = lax.optimization_barrier((one, two, d_hid, ffn))
            if i == 1:
                d_hid = sh.halve(d_hid, sh.bits - 1, d_hid.ndim - 3)
                gi, gu = ffn_final(ffn, inner_bias.shape[0] * 2, D)
                one, two, gi, gu, d_hid = lax.optimization_barrier((one, two, gi, gu, d_hid))
                input_grad = input_grads(place, d_res1, dq, query_proj, other_q, d_hid)
        one, two, input_grad = lax.optimization_barrier((one, two, input_grad))
        one, two = one.reshape(-1, dn), two.reshape(-1, dn)
        gk, gv, gp, go, gq, s = grad_final(
            place, one, two, sh.flip(one, 0), sh.flip(two, 0), D, C // 2
        )
        s = unpack_rows(s)
    else:
        dkv = dkv.reshape(2 * D, W)
        gkv, gp = (
            lax.dot_general(a, b, (((0,), (1,)), ((), ())), preferred_element_type=F32)
            for a, b in ((x_win, dkv), (sinus, d_table))
        )
        d_hid = tn(dkv[:D], jnp.transpose(k_full)) + tn(dkv[D:], jnp.transpose(v_full))
        d_hid = d_hid.astype(BF)
        below = (C - 1 - R) * T
        d_hid = jnp.pad(d_hid, ((below, (C - 1) * T + L - below - W), (0, 0)))
        d_hid = lax.dynamic_slice_in_dim(d_hid, (C - 1 - ctx) * T, L, 0)
        d_hid = lax.psum_scatter(d_hid, "ctx", scatter_dimension=0, tiled=True)
        input_grad = d_res1 + nt(dq, q_full) + d_hid.astype(F32)
        s = jnp.concatenate([att_vec, vec_a, vec_b], axis=0)
        sums = [
            gkv, gp, tn(mixed_low, d_attn), tn(hidden, dq), tn(normed_low, d_inner),
            tn(activ_low, d_outer), jnp.transpose(s),
        ]
        sums = [
            lax.psum_scatter(a.astype(BF), "fsdp", scatter_dimension=0, tiled=True) for a in sums
        ]
        gkv, gp, go, gq, gi, gu, s = (a.astype(F32) for a in lax.psum(sums, "ctx"))
        gk, gv, s = gkv[:, :D], gkv[:, D:], jnp.transpose(s)
        s = [s[i] for i in (19, 0, 1, 2, 18, 16, 17, 10, 8, 9)] + [s[3:5], s[20:24].reshape(-1)]
    return (
        outcome.astype(BF)[None],
        input_grad[None],
        gq,
        gk,
        gv,
        s[0],
        s[1],
        s[2],
        s[3],
        s[10],
        gp,
        go,
        s[4],
        s[5],
        s[6],
        gi,
        s[11],
        gu,
        s[7],
        s[8],
        s[9],
    )


def solution(mesh):
    in_specs = (
        P("fsdp", "ctx", None),
        P("fsdp", "ctx"),
        P("fsdp", "ctx"),
        P("fsdp", "ctx", None),
        P("fsdp", None),
        P("fsdp", None),
        P("fsdp", None),
        P("fsdp"),
        P("fsdp"),
        P("fsdp"),
        P("fsdp"),
        P(None, "fsdp"),
        P("fsdp", None),
        P("fsdp", None),
        P("fsdp"),
        P("fsdp"),
        P("fsdp"),
        P("fsdp", None),
        P("fsdp"),
        P("fsdp", None),
        P("fsdp"),
        P("fsdp"),
        P("fsdp"),
    )
    out_specs = (
        P("fsdp", "ctx", None),
        P("fsdp", "ctx", None),
        P("fsdp", None),
        P("fsdp", None),
        P("fsdp", None),
        P("fsdp"),
        P("fsdp"),
        P("fsdp"),
        P("fsdp"),
        P(None, "fsdp"),
        P("fsdp", None),
        P("fsdp", None),
        P("fsdp"),
        P("fsdp"),
        P("fsdp"),
        P("fsdp", None),
        P("fsdp"),
        P("fsdp", None),
        P("fsdp"),
        P("fsdp"),
        P("fsdp"),
    )
    return jax.shard_map(
        per_device, mesh=mesh, in_specs=in_specs, out_specs=out_specs, check_vma=False
    )
```
